32 devices in a mesh: dp: 8 (over y, x, core), mp: 4 (over z).
Axes of the slice: x: 2, y: 2, z: 4, core: 2. Of those that a mesh axis runs over, the one named last changes fastest.
Arguments:
- frames_in: bfloat16 [8, 512, 1024], P('dp', 'mp'), may hold values from -6 to 6
- lengths: int32 [8], replicated, may hold values from 128 to 512, as said below
- out_grad: bfloat16 [8, 512, 1024], P('dp', 'mp'), may hold values from -6 to 6
- norm_gains: float32 [5, 1024], replicated, may hold values from 0.25 to 1.75
- ffn1_up: bfloat16 [1024, 4096], P('dp', 'mp'), may hold values from -0.1875 to 0.1875
- ffn1_down: bfloat16 [4096, 1024], P('mp', 'dp'), may hold values from -0.09375 to 0.09375
- attn_in: bfloat16 [1024, 3, 1024], P('dp', None, 'mp'), may hold values from -0.1875 to 0.1875
- pos_proj: bfloat16 [1024, 1024], P('dp', 'mp'), may hold values from -0.1875 to 0.1875
- pos_bias: bfloat16 [2, 1024], P(None, ('mp', 'dp')), may hold values from -3 to 3
- attn_out: bfloat16 [1024, 1024], P('mp', 'dp'), may hold values from -1.5 to 1.5
- conv_in: bfloat16 [1024, 2, 1024], P('dp', None, 'mp'), may hold values from -0.1875 to 0.1875
- depthwise: bfloat16 [5, 1024], P(None, ('mp', 'dp')), may hold values from -2.5 to 2.5
- bn_scale: bfloat16 [1024], P(('mp', 'dp')), may hold values from 0.25 to 1.75
- bn_shift: bfloat16 [1024], P(('mp', 'dp')), may hold values from -3 to 3
- conv_out: bfloat16 [1024, 1024], P('mp', 'dp'), may hold values from -0.1875 to 0.1875
- ffn2_up: bfloat16 [1024, 4096], P('dp', 'mp'), may hold values from -0.1875 to 0.1875
- ffn2_down: bfloat16 [4096, 1024], P('mp', 'dp'), may hold values from -0.09375 to 0.09375
Outputs:
- block_out: bfloat16 [8, 512, 1024], P('dp', 'mp')
- in_grad: float32 [8, 512, 1024], P('dp', 'mp')
- grad_norm_gains: float32 [5, 1024], replicated
- grad_ffn1_up: float32 [1024, 4096], P('dp', 'mp')
- grad_ffn1_down: float32 [4096, 1024], P('mp', 'dp')
- grad_attn_in: float32 [1024, 3, 1024], P('dp', None, 'mp')
- grad_pos_proj: float32 [1024, 1024], P('dp', 'mp')
- grad_pos_bias: float32 [2, 1024], P(None, ('mp', 'dp'))
- grad_attn_out: float32 [1024, 1024], P('mp', 'dp')
- grad_conv_in: float32 [1024, 2, 1024], P('dp', None, 'mp')
- grad_depthwise: float32 [5, 1024], P(None, ('mp', 'dp'))
- grad_bn_scale: float32 [1024], P(('mp', 'dp'))
- grad_bn_shift: float32 [1024], P(('mp', 'dp'))
- grad_conv_out: float32 [1024, 1024], P('mp', 'dp')
- grad_ffn2_up: float32 [1024, 4096], P('dp', 'mp')
- grad_ffn2_down: float32 [4096, 1024], P('mp', 'dp')
The draws below stay inside these ranges and needn't reach their ends.
Inputs may be any that keep to these rules, and one draw needn't show every extreme that they name: Frames 0 to lengths[s] - 1 of slot s hold the utterance and the rest is padding; some slot holds 512 frames.
All inputs are finite; a program needn't handle non-finite values.
Results may differ from the reference program's by a relative error of at most 0.03.
Values may be sent and summed in bfloat16 or wider, within the bound.
A program may use at most 128 MiB of HBM per device.

```python
import math
import jax
import jax.numpy as jnp
from jax import lax

D = 1024
FF = 4096
HEADS = 8
KERNEL = 5
HEAD = 128
FRAMES = 512
SEQS = 8


def draw_lengths(key, part):
    first_key, second_key = jax.random.split(key)
    slot_index = jnp.arange(SEQS)
    rising = slot_index * (FRAMES - FRAMES // 4) // SEQS
    jitter = jax.random.randint(first_key, (SEQS,), 0, FRAMES // 4 + 1)
    drawn_len = jnp.minimum(FRAMES // 4 + rising + jitter, FRAMES)
    longest = jax.random.randint(second_key, (), 0, SEQS)
    return jnp.where(slot_index == longest, FRAMES, drawn_len).astype(jnp.int32)


def shard_levels(stream_key, dims, pieces, low, largest):
    def one(axis_at, shards_of):
        draws = jax.random.uniform(jax.random.fold_in(jax.random.fold_in(stream_key, 6), axis_at), (shards_of,), jnp.float32, low / len(pieces), largest / len(pieces))
        return jnp.repeat(jnp.exp(draws), dims[axis_at] // shards_of).reshape((-1,) + (1,) * (len(dims) - axis_at - 1))

    level = one(*pieces[0])
    for cut in pieces[1:]:
        level = level * one(*cut)
    return level


def bell_draw(own_key, shape, deviation, limit, cuts=(), held_as=jnp.bfloat16):
    values = deviation * jax.random.normal(own_key, shape, jnp.float32)
    if cuts:
        values = values * shard_levels(own_key, shape, cuts, -0.22, 0.18)
    return jnp.clip(values, -limit, limit).astype(held_as)


def setup_inputs(seed: int = 0) -> dict:
    key_of = jax.random.split(jax.random.key(seed), 18)
    return {
        "frames_in": bell_draw(key_of[0], (SEQS, FRAMES, D), 1.0, 6.0, ((0, 8), (1, 4))),
        "lengths": draw_lengths(jax.random.fold_in(key_of[17], 71), 0),
        "out_grad": bell_draw(key_of[2], (SEQS, FRAMES, D), 1.0, 6.0, ((0, 8), (1, 4))),
        "norm_gains": jnp.clip(1.0 + 0.15 * jax.random.normal(key_of[3], (5, D), jnp.float32), 0.25, 1.75),
        "ffn1_up": bell_draw(key_of[4], (D, FF), D ** -0.5, 0.1875, ((0, 8), (1, 4))),
        "ffn1_down": bell_draw(key_of[5], (FF, D), FF ** -0.5, 0.09375, ((0, 4), (1, 8))),
        "attn_in": bell_draw(key_of[6], (D, 3, D), D ** -0.5, 0.1875, ((0, 8), (2, 4))),
        "pos_proj": bell_draw(key_of[7], (D, D), D ** -0.5, 0.1875, ((0, 8), (1, 4))),
        "pos_bias": bell_draw(key_of[8], (2, D), 0.5, 3.0, ((1, 32),)),
        "attn_out": bell_draw(key_of[9], (D, D), (D // 64) ** -0.5, 1.5, ((0, 4), (1, 8))),
        "conv_in": bell_draw(key_of[10], (D, 2, D), D ** -0.5, 0.1875, ((0, 8), (2, 4))),
        "depthwise": bell_draw(key_of[11], (KERNEL, D), KERNEL ** -0.5, 2.5, ((1, 32),)),
        "bn_scale": jnp.clip(1.0 + 0.15 * jax.random.normal(key_of[12], (D,), jnp.float32), 0.25, 1.75).astype(jnp.bfloat16),
        "bn_shift": bell_draw(key_of[13], (D,), 0.5, 3.0, ((0, 32),)),
        "conv_out": bell_draw(key_of[14], (D, D), D ** -0.5, 0.1875, ((0, 4), (1, 8))),
        "ffn2_up": bell_draw(key_of[15], (D, FF), D ** -0.5, 0.1875, ((0, 8), (1, 4))),
        "ffn2_down": bell_draw(key_of[16], (FF, D), FF ** -0.5, 0.09375, ((0, 4), (1, 8))),
    }


@jax.custom_vjp
def low(v):
    return lax.optimization_barrier(v.astype(jnp.bfloat16)).astype(jnp.float32)

@jax.custom_vjp
def low_back(v):
    return v

def low_keep(v):
    return (low(v), None)

def low_pass(kept, grad):
    return (grad,)

def back_keep(v):
    return (v, None)

def back_low(kept, grad):
    return (low(grad),)
low.defvjp(low_keep, low_pass)
low_back.defvjp(back_keep, back_low)
norm_eps = 1e-05
batch_eps = 1e-05
masked_score = -1000000000.0
highest = lax.Precision.HIGHEST

def matmul(left, right):
    return jnp.dot(left, right, precision=highest, preferred_element_type=jnp.float32)

def layer_norm(values, norm_gain):
    average = lax.optimization_barrier(jnp.mean(values, axis=-1, keepdims=True))
    centred = values - average
    inv_std = lax.rsqrt(lax.optimization_barrier(jnp.mean(centred * centred, axis=-1, keepdims=True)) + norm_eps)
    return centred * inv_std * norm_gain

def position_table(seq_len, model_width):
    distance = (jnp.arange(2 * seq_len - 1) - (seq_len - 1)).astype(jnp.float32)
    frequency = jnp.exp(jnp.arange(model_width // 2).astype(jnp.float32) * (-2.0 * math.log(10000.0) / model_width))
    angles = distance[:, None] * frequency[None, :]
    return jnp.stack([jnp.sin(angles), jnp.cos(angles)], axis=-1).reshape(2 * seq_len - 1, model_width)

def feed_forward(residual, norm_gain, w_up, w_down):
    normed = low(layer_norm(residual, norm_gain))
    hidden = low_back(matmul(normed, w_up))
    return matmul(low(jax.nn.silu(hidden)), w_down)

def attention(residual, valid_frames, norm_gain, w_in, w_pos, bias_pair, w_out):
    seq_len = residual.shape[0]
    normed = low(layer_norm(residual, norm_gain))
    projected = matmul(normed, w_in.reshape(D, 3 * D))
    queries = low_back(projected[:, :D])
    key_rows = low(low_back(projected[:, D:2 * D])).reshape(seq_len, HEADS, HEAD)
    value_rows = low(low_back(projected[:, 2 * D:])).reshape(seq_len, HEADS, HEAD)
    scaling = HEAD ** (-0.5)
    query_u = low((queries + bias_pair[0]) * scaling).reshape(seq_len, HEADS, HEAD)
    query_v = low((queries + bias_pair[1]) * scaling).reshape(seq_len, HEADS, HEAD)
    position = low(low_back(matmul(low(position_table(seq_len, D)), w_pos))).reshape(2 * seq_len - 1, HEADS, HEAD)
    content = jnp.einsum('ihd,jhd->hij', query_u, key_rows, precision=highest)
    spread = jnp.einsum('ihd,thd->hit', query_v, position, precision=highest)
    offsets = jnp.arange(seq_len)[:, None] - jnp.arange(seq_len)[None, :] + seq_len - 1
    shifted = jnp.take_along_axis(spread, jnp.broadcast_to(offsets[None], (HEADS, seq_len, seq_len)), axis=2)
    scores = low_back(jnp.where(valid_frames[None, None, :], content + shifted, masked_score))
    top_score = lax.optimization_barrier(jnp.max(scores, axis=-1, keepdims=True))
    exponent = jnp.exp(scores - top_score)
    softmax_out = low(exponent / lax.optimization_barrier(jnp.sum(exponent, axis=-1, keepdims=True)))
    context = jnp.einsum('hij,jhd->ihd', softmax_out, value_rows, precision=highest).reshape(seq_len, D)
    return matmul(low(low_back(context)), w_out)

def conv_front(residual, valid_frames, norm_gain, w_in, kernel):
    seq_len = residual.shape[0]
    normed = low(layer_norm(residual, norm_gain))
    glu_in = low_back(matmul(normed, w_in.reshape(D, 2 * D)))
    glu_out = glu_in[:, :D] * jax.nn.sigmoid(glu_in[:, D:]) * valid_frames[:, None].astype(jnp.float32)
    half_taps = (KERNEL - 1) // 2
    padded = jnp.pad(glu_out, ((half_taps, half_taps), (0, 0)))
    conved = kernel[0] * padded[0:seq_len]
    for tap_index in range(1, KERNEL):
        conved = conved + kernel[tap_index] * padded[tap_index:tap_index + seq_len]
    return conved

def conv_tail(conved, average, inv_std, bn_gain, bn_bias, w_out):
    normed_b = (conved - average) * inv_std * bn_gain + bn_bias
    return matmul(low(jax.nn.silu(normed_b)), w_out)

def layer(frames, lengths, norm_gains, ffn1_up, ffn1_down, attn_in, pos_proj, pos_bias, attn_out, conv_in, depthwise, bn_scale, bn_shift, conv_out, ffn2_up, ffn2_down):
    valid_frames = jnp.arange(FRAMES)[None, :] < lengths[:, None]
    frame_count = jnp.sum(lengths).astype(jnp.float32)
    first_out = lax.map(jax.checkpoint(lambda residual: feed_forward(residual, norm_gains[0], ffn1_up, ffn1_down)), frames)
    after_first = frames + 0.5 * low_back(first_out)
    attn_branch = lax.map(jax.checkpoint(lambda pair_in: attention(pair_in[0], pair_in[1], norm_gains[1], attn_in, pos_proj, pos_bias, attn_out)), (after_first, valid_frames))
    after_attn = after_first + low_back(attn_branch)
    conved = lax.map(jax.checkpoint(lambda pair_in: conv_front(pair_in[0], pair_in[1], norm_gains[2], conv_in, depthwise)), (after_attn, valid_frames))
    weight_mask = valid_frames[:, :, None].astype(jnp.float32)
    average = lax.optimization_barrier(jnp.sum(conved * weight_mask, axis=(0, 1))) / frame_count
    variance = lax.optimization_barrier(jnp.sum(conved * conved * weight_mask, axis=(0, 1))) / frame_count - average * average
    inv_std = lax.rsqrt(variance + batch_eps)
    conv_branch = lax.map(jax.checkpoint(lambda conv_piece: conv_tail(conv_piece, average, inv_std, bn_scale, bn_shift, conv_out)), conved)
    after_conv = after_attn + low_back(conv_branch)
    second_out = lax.map(jax.checkpoint(lambda residual: feed_forward(residual, norm_gains[3], ffn2_up, ffn2_down)), after_conv)
    after_second = after_conv + 0.5 * low_back(second_out)
    return layer_norm(after_second, norm_gains[4])

def reference(frames_in, lengths, out_grad, norm_gains, ffn1_up, ffn1_down, attn_in, pos_proj, pos_bias, attn_out, conv_in, depthwise, bn_scale, bn_shift, conv_out, ffn2_up, ffn2_down):

    def forward(frames, gains_all, first_up, first_down, proj_in, proj_pos, bias_pair, proj_out, glu_proj, kernel, bn_gain, bn_bias, conv_proj, second_up, second_down):
        return layer(frames, lengths, gains_all, first_up, first_down, proj_in, proj_pos, bias_pair, proj_out, glu_proj, kernel, bn_gain, bn_bias, conv_proj, second_up, second_down)
    result, pullback = jax.vjp(forward, frames_in.astype(jnp.float32), norm_gains.astype(jnp.float32), ffn1_up.astype(jnp.float32), ffn1_down.astype(jnp.float32), attn_in.astype(jnp.float32), pos_proj.astype(jnp.float32), pos_bias.astype(jnp.float32), attn_out.astype(jnp.float32), conv_in.astype(jnp.float32), depthwise.astype(jnp.float32), bn_scale.astype(jnp.float32), bn_shift.astype(jnp.float32), conv_out.astype(jnp.float32), ffn2_up.astype(jnp.float32), ffn2_down.astype(jnp.float32))
    gradients = pullback(out_grad.astype(jnp.float32))
    return (result.astype(jnp.bfloat16), gradients[0], gradients[1], gradients[2], gradients[3], gradients[4], gradients[5], gradients[6], gradients[7], gradients[8], gradients[9], gradients[10], gradients[11], gradients[12], gradients[13], gradients[14])
```

```python
import math

import jax
import jax.numpy as jnp
from jax import lax
from jax.sharding import PartitionSpec as P

HEAD = 128


norm_eps = 1e-05
batch_eps = 1e-05
masked_score = -1000000000.0


def matmul(left, right):
    return jnp.dot(left, right, preferred_element_type=jnp.float32)


def contract_rows(left, right):
    return lax.dot_general(
        left, right, (((0,), (0,)), ((), ())), preferred_element_type=jnp.float32
    )


def contract_cols(left, right):
    return lax.dot_general(
        left, right, (((1,), (1,)), ((), ())), preferred_element_type=jnp.float32
    )


def layer_norm(values, norm_gain):
    average = jnp.mean(values, axis=-1, keepdims=True)
    centred = values - average
    inv_std = lax.rsqrt(jnp.mean(centred * centred, axis=-1, keepdims=True) + norm_eps)
    return centred * inv_std * norm_gain


def norm_back(values, norm_gain, upstream):
    unused, pullback = jax.vjp(layer_norm, values, norm_gain)
    return pullback(upstream)


def silu_slope(values):
    logistic = jax.nn.sigmoid(values)
    return logistic * (1.0 + values * (1.0 - logistic))


def position_table(seq_len, model_width):
    distance = (seq_len - 1 - jnp.arange(2 * seq_len)).astype(jnp.float32)
    frequency = jnp.exp(
        jnp.arange(model_width // 2).astype(jnp.float32) * (-2.0 * math.log(10000.0) / model_width)
    )
    angles = distance[:, None] * frequency[None, :]
    return jnp.stack([jnp.sin(angles), jnp.cos(angles)], axis=-1).reshape(2 * seq_len, model_width)


def spread_rows(normed):
    return lax.all_gather(normed, "mp", axis=0, tiled=True)


def enter_block(residual, norm_gain):
    return spread_rows(layer_norm(residual, norm_gain).astype(jnp.bfloat16))


def branch_total(partial_value):
    return lax.psum_scatter(
        partial_value.astype(jnp.bfloat16), "mp", scatter_dimension=0, tiled=True
    ).astype(jnp.float32)


def spread_grads(upstream):
    return lax.all_gather(upstream, "mp", axis=0, tiled=True)


def input_total(partial_value):
    return lax.psum_scatter(
        partial_value.astype(jnp.bfloat16), "mp", scatter_dimension=0, tiled=True
    ).astype(jnp.float32)


def grad_total(partial_value, dimension):
    return lax.psum_scatter(
        partial_value.astype(jnp.bfloat16), "dp", scatter_dimension=dimension, tiled=True
    ).astype(jnp.float32)


def ffn_fetch(w_up, w_down):
    return (
        lax.all_gather(w_up, "dp", axis=0, tiled=True),
        lax.all_gather(w_down, "dp", axis=1, tiled=True),
    )


def attn_fetch(w_in, w_pos, bias_pair, w_out):
    return (
        lax.all_gather(w_in, "dp", axis=0, tiled=True),
        lax.all_gather(w_pos, "dp", axis=0, tiled=True),
        lax.all_gather(bias_pair, "dp", axis=1, tiled=True),
        lax.all_gather(w_out, "dp", axis=1, tiled=True),
    )


def conv_fetch(w_in, kernel, bn_gain, bn_bias, w_out):
    return (
        lax.all_gather(w_in, "dp", axis=0, tiled=True),
        lax.all_gather(kernel, "dp", axis=1, tiled=True),
        lax.all_gather(bn_gain, "dp", axis=0, tiled=True),
        lax.all_gather(bn_bias, "dp", axis=0, tiled=True),
        lax.all_gather(w_out, "dp", axis=1, tiled=True),
    )


def ffn_forward(whole, weights):
    w_up, w_down = weights
    hidden = matmul(whole, w_up)
    return matmul(jax.nn.silu(hidden).astype(jnp.bfloat16), w_down)


def ffn_backward(whole, weights, grad_whole):
    w_up, w_down = weights
    hidden = matmul(whole, w_up)
    active = jax.nn.silu(hidden).astype(jnp.bfloat16)
    grad_down = contract_rows(active, grad_whole)
    d_hidden = (contract_cols(grad_whole, w_down) * silu_slope(hidden)).astype(jnp.bfloat16)
    grad_up = contract_rows(whole, d_hidden)
    return (contract_cols(d_hidden, w_up), grad_up, grad_down)


def attention_setup(whole, weights):
    w_in, w_pos, bias_pair, w_out = weights
    seq_len, model_width = whole.shape
    local_width = w_in.shape[2]
    heads_here = local_width // HEAD
    projected = matmul(whole, w_in.reshape(model_width, 3 * local_width))
    queries = projected[:, :local_width]
    key_rows = (
        projected[:, local_width : 2 * local_width]
        .astype(jnp.bfloat16)
        .reshape(seq_len, heads_here, HEAD)
    )
    value_rows = (
        projected[:, 2 * local_width :].astype(jnp.bfloat16).reshape(seq_len, heads_here, HEAD)
    )
    scaling = HEAD ** (-0.5)
    bias_float = bias_pair.astype(jnp.float32)
    query_u = (
        ((queries + bias_float[0]) * scaling)
        .astype(jnp.bfloat16)
        .reshape(seq_len, heads_here, HEAD)
    )
    query_v = (
        ((queries + bias_float[1]) * scaling)
        .astype(jnp.bfloat16)
        .reshape(seq_len, heads_here, HEAD)
    )
    table_low = position_table(seq_len, model_width).astype(jnp.bfloat16)
    position = matmul(table_low, w_pos).astype(jnp.bfloat16).reshape(2 * seq_len, heads_here, HEAD)
    return (query_u, query_v, key_rows, value_rows, table_low, position)


def skew_rows(zeds, block_rows, seq_len):
    heads_here = zeds.shape[0]
    window = block_rows + seq_len - 1
    flat = zeds.reshape(heads_here, block_rows * window)
    flat = flat[:, block_rows - 1 : block_rows - 1 + block_rows * (window - 1)]
    return flat.reshape(heads_here, block_rows, window - 1)[:, :, :seq_len]


def unskew_rows(grads_in, block_rows, seq_len):
    heads_here = grads_in.shape[0]
    window = block_rows + seq_len - 1
    padded = jnp.pad(grads_in, ((0, 0), (0, 0), (0, window - 1 - seq_len)))
    flat = padded.reshape(heads_here, block_rows * (window - 1))
    flat = jnp.pad(flat, ((0, 0), (block_rows - 1, 1)))
    return flat.reshape(heads_here, block_rows, window)


def block_scores(query_u, query_v, key_rows, position, valid_keys, offset, block_rows):
    seq_len = key_rows.shape[0]
    window = block_rows + seq_len - 1
    lowest = seq_len - offset - block_rows
    nearby = position[lowest : lowest + window]
    content = jnp.einsum("bhd,jhd->hbj", query_u, key_rows, preferred_element_type=jnp.float32)
    zeds = jnp.einsum("bhd,whd->hbw", query_v, nearby, preferred_element_type=jnp.float32)
    scores = jnp.where(
        valid_keys[None, None, :], content + skew_rows(zeds, block_rows, seq_len), masked_score
    )
    top_score = jnp.max(scores, axis=-1, keepdims=True)
    exponent = jnp.exp(scores - top_score)
    softmax_out = exponent / jnp.sum(exponent, axis=-1, keepdims=True)
    return (softmax_out, query_u, query_v, nearby, lowest)


def attention_forward(whole, weights, valid_keys, block_rows):
    seq_len = whole.shape[0]
    query_u, query_v, key_rows, value_rows, table_low, position = attention_setup(whole, weights)
    softmax_out, part_u, part_v, nearby, lowest = block_scores(
        query_u, query_v, key_rows, position, valid_keys, 0, block_rows
    )
    contexts = jnp.einsum(
        "hbj,jhd->bhd",
        softmax_out.astype(jnp.bfloat16),
        value_rows,
        preferred_element_type=jnp.float32,
    )
    context = contexts.reshape(seq_len, -1).astype(jnp.bfloat16)
    return matmul(context, weights[3])


def attention_backward(whole, weights, valid_keys, block_rows, grad_whole):
    w_in, w_pos, bias_pair, w_out = weights
    seq_len, model_width = whole.shape
    query_u, query_v, key_rows, value_rows, table_low, position = attention_setup(whole, weights)
    heads_here = key_rows.shape[1]
    local_width = w_in.shape[2]
    scaling = HEAD ** (-0.5)
    window = block_rows + seq_len - 1
    d_context = (
        contract_cols(grad_whole, w_out).astype(jnp.bfloat16).reshape(seq_len, heads_here, HEAD)
    )
    d_position = jnp.zeros(position.shape, jnp.float32)
    softmax_out, part_u, part_v, nearby, lowest = block_scores(
        query_u, query_v, key_rows, position, valid_keys, 0, block_rows
    )
    soft_low = softmax_out.astype(jnp.bfloat16)
    contexts = jnp.einsum("hbj,jhd->bhd", soft_low, value_rows, preferred_element_type=jnp.float32)
    d_soft = jnp.einsum("bhd,jhd->hbj", d_context, value_rows, preferred_element_type=jnp.float32)
    inner = jnp.sum(softmax_out * d_soft, axis=-1, keepdims=True)
    d_scores = (softmax_out * (d_soft - inner)).astype(jnp.bfloat16)
    d_query_u = jnp.einsum("hbj,jhd->bhd", d_scores, key_rows, preferred_element_type=jnp.float32)
    d_keys = jnp.einsum("hbj,bhd->jhd", d_scores, part_u, preferred_element_type=jnp.float32)
    d_values = jnp.einsum("hbj,bhd->jhd", soft_low, d_context, preferred_element_type=jnp.float32)
    d_zeds = unskew_rows(d_scores, block_rows, seq_len)
    d_query_v = jnp.einsum("hbw,whd->bhd", d_zeds, nearby, preferred_element_type=jnp.float32)
    d_position = d_position.at[lowest : lowest + window].add(
        jnp.einsum("hbw,bhd->whd", d_zeds, part_v, preferred_element_type=jnp.float32)
    )
    grad_u = d_query_u.reshape(seq_len, local_width) * scaling
    grad_v = d_query_v.reshape(seq_len, local_width) * scaling
    d_queries = (grad_u + grad_v).astype(jnp.bfloat16)
    grad_bias = jnp.stack([jnp.sum(grad_u, axis=0), jnp.sum(grad_v, axis=0)])
    d_projected = jnp.concatenate(
        [
            d_queries,
            d_keys.reshape(seq_len, local_width).astype(jnp.bfloat16),
            d_values.reshape(seq_len, local_width).astype(jnp.bfloat16),
        ],
        axis=1,
    )
    grad_in = contract_rows(whole, d_projected).reshape(model_width, 3, local_width)
    d_normed = contract_cols(d_projected, w_in.reshape(model_width, 3 * local_width))
    grad_pos = contract_rows(
        table_low, d_position.reshape(2 * seq_len, local_width).astype(jnp.bfloat16)
    )
    context = contexts.reshape(seq_len, local_width).astype(jnp.bfloat16)
    grad_out = contract_rows(context, grad_whole)
    return (d_normed, grad_in, grad_pos, grad_bias, grad_out)


def conv_front(whole, w_in, kernel, mask_col):
    seq_len, model_width = whole.shape
    local_width = w_in.shape[2]
    glu_in = matmul(whole, w_in.reshape(model_width, 2 * local_width))
    gate_value = glu_in[:, :local_width]
    logistic = jax.nn.sigmoid(glu_in[:, local_width:])
    glu_out = gate_value * logistic * mask_col
    tap_count = kernel.shape[0]
    half_taps = (tap_count - 1) // 2
    padded = jnp.pad(glu_out, ((half_taps, half_taps), (0, 0)))
    kernel_float = kernel.astype(jnp.float32)
    conved = kernel_float[0] * padded[0:seq_len]
    for tap_index in range(1, tap_count):
        conved = conved + kernel_float[tap_index] * padded[tap_index : tap_index + seq_len]
    return (gate_value, logistic, padded, conved)


def batch_stats(conved, mask_col, frame_count):
    local_sum = jnp.sum(conved * mask_col, axis=0)
    local_squares = jnp.sum(conved * conved * mask_col, axis=0)
    total_sum, total_squares = lax.psum((local_sum, local_squares), "dp")
    average = total_sum / frame_count
    variance = total_squares / frame_count - average * average
    return (average, lax.rsqrt(variance + batch_eps))


def conv_tail(conved, stats, bn_gain, bn_bias):
    average, inv_std = stats
    normed_b = (conved - average) * inv_std * bn_gain.astype(jnp.float32) + bn_bias.astype(
        jnp.float32
    )
    return (normed_b, jax.nn.silu(normed_b).astype(jnp.bfloat16))


def conv_backward(whole, weights, mask_col, stats, frame_count, grad_whole):
    w_in, kernel, bn_gain, bn_bias, w_out = weights
    seq_len, model_width = whole.shape
    local_width = w_in.shape[2]
    gate_value, logistic, padded, conved = conv_front(whole, w_in, kernel, mask_col)
    normed_b, active = conv_tail(conved, stats, bn_gain, bn_bias)
    average, inv_std = stats
    grad_out = contract_rows(active, grad_whole)
    d_normed = contract_cols(grad_whole, w_out) * silu_slope(normed_b)
    centred = (conved - average) * inv_std
    bias_total, gain_total = lax.psum(
        (jnp.sum(d_normed, axis=0), jnp.sum(d_normed * centred, axis=0)), "dp"
    )
    d_conved = (
        bn_gain.astype(jnp.float32)
        * inv_std
        * (d_normed - mask_col * (bias_total + centred * gain_total) / frame_count)
    )
    tap_count = kernel.shape[0]
    half_taps = (tap_count - 1) // 2
    kernel_float = kernel.astype(jnp.float32)
    d_padded = jnp.pad(d_conved, ((half_taps, half_taps), (0, 0)))
    d_glu = kernel_float[0] * d_padded[tap_count - 1 : tap_count - 1 + seq_len]
    for tap_index in range(1, tap_count):
        d_glu = (
            d_glu
            + kernel_float[tap_index]
            * d_padded[tap_count - 1 - tap_index : tap_count - 1 - tap_index + seq_len]
        )
    grad_kernel = jnp.stack(
        [
            jnp.sum(d_conved * padded[tap_index : tap_index + seq_len], axis=0)
            for tap_index in range(tap_count)
        ]
    )
    d_glu = d_glu * mask_col
    d_pair = jnp.concatenate(
        [d_glu * logistic, d_glu * gate_value * logistic * (1.0 - logistic)], axis=1
    ).astype(jnp.bfloat16)
    grad_in = contract_rows(whole, d_pair).reshape(model_width, 2, local_width)
    d_normed_in = contract_cols(d_pair, w_in.reshape(model_width, 2 * local_width))
    return (d_normed_in, grad_in, grad_kernel, grad_out, gain_total, bias_total)


def body(
    frames_in,
    lengths,
    out_grad,
    norm_gains,
    ffn1_up,
    ffn1_down,
    attn_in,
    pos_proj,
    pos_bias,
    attn_out,
    conv_in,
    depthwise,
    bn_scale,
    bn_shift,
    conv_out,
    ffn2_up,
    ffn2_down,
):
    unused, local_rows, model_width = frames_in.shape
    seq_len = local_rows * lax.axis_size("mp")
    block_rows = min(seq_len, 512)
    dp_index = lax.axis_index("dp")
    own_length = lax.dynamic_slice_in_dim(lengths, dp_index, 1)[0]
    valid_keys = jnp.arange(seq_len) < own_length
    mask_col = valid_keys.astype(jnp.float32)[:, None]
    frame_count = jnp.sum(lengths).astype(jnp.float32)
    layer_input = frames_in.reshape(local_rows, model_width).astype(jnp.float32)
    ffn_first = ffn_fetch(ffn1_up, ffn1_down)
    after_first = layer_input + 0.5 * branch_total(
        ffn_forward(enter_block(layer_input, norm_gains[0]), ffn_first)
    )
    attn_held = attn_fetch(attn_in, pos_proj, pos_bias, attn_out)
    after_attn = after_first + branch_total(
        attention_forward(
            enter_block(after_first, norm_gains[1]), attn_held, valid_keys, block_rows
        )
    )
    conv_held = conv_fetch(conv_in, depthwise, bn_scale, bn_shift, conv_out)
    gate_value, logistic, padded, conved = conv_front(
        enter_block(after_attn, norm_gains[2]), conv_held[0], conv_held[1], mask_col
    )
    stats = batch_stats(conved, mask_col, frame_count)
    normed_b, active = conv_tail(conved, stats, conv_held[2], conv_held[3])
    after_conv = after_attn + branch_total(matmul(active, conv_held[4]))
    ffn_second = ffn_fetch(ffn2_up, ffn2_down)
    after_second = after_conv + 0.5 * branch_total(
        ffn_forward(enter_block(after_conv, norm_gains[3]), ffn_second)
    )
    block_out = layer_norm(after_second, norm_gains[4]).astype(jnp.bfloat16)
    d_second, gain_five = norm_back(
        after_second, norm_gains[4], out_grad.reshape(local_rows, model_width).astype(jnp.float32)
    )
    ffn_back_two = ffn_fetch(ffn2_up, ffn2_down)
    d_normed, grad_up_two, grad_down_two = ffn_backward(
        enter_block(after_conv, norm_gains[3]),
        ffn_back_two,
        spread_grads((0.5 * d_second).astype(jnp.bfloat16)),
    )
    d_branch, gain_four = norm_back(after_conv, norm_gains[3], input_total(d_normed))
    d_conv = d_second + d_branch
    conv_back_held = conv_fetch(conv_in, depthwise, bn_scale, bn_shift, conv_out)
    d_normed, grad_conv_in, grad_kernel, grad_conv_out, gain_total, bias_total = conv_backward(
        enter_block(after_attn, norm_gains[2]),
        conv_back_held,
        mask_col,
        stats,
        frame_count,
        spread_grads(d_conv.astype(jnp.bfloat16)),
    )
    d_branch, gain_three = norm_back(after_attn, norm_gains[2], input_total(d_normed))
    d_attn = d_conv + d_branch
    attn_back_held = attn_fetch(attn_in, pos_proj, pos_bias, attn_out)
    d_normed, grad_attn_in, grad_pos, grad_bias, grad_attn_out = attention_backward(
        enter_block(after_first, norm_gains[1]),
        attn_back_held,
        valid_keys,
        block_rows,
        spread_grads(d_attn.astype(jnp.bfloat16)),
    )
    d_branch, gain_two = norm_back(after_first, norm_gains[1], input_total(d_normed))
    d_first = d_attn + d_branch
    ffn_back_one = ffn_fetch(ffn1_up, ffn1_down)
    d_normed, grad_up_one, grad_down_one = ffn_backward(
        enter_block(layer_input, norm_gains[0]),
        ffn_back_one,
        spread_grads((0.5 * d_first).astype(jnp.bfloat16)),
    )
    d_branch, gain_one = norm_back(layer_input, norm_gains[0], input_total(d_normed))
    in_grad = d_first + d_branch
    summed = (
        grad_total(grad_up_one, 0),
        grad_total(grad_down_one, 1),
        grad_total(grad_attn_in, 0),
        grad_total(grad_pos, 0),
        grad_total(grad_bias, 1),
        grad_total(grad_attn_out, 1),
        grad_total(grad_conv_in, 0),
        grad_total(grad_kernel, 1),
        grad_total(grad_conv_out, 1),
        grad_total(grad_up_two, 0),
        grad_total(grad_down_two, 1),
    )
    gain_sum = lax.psum(
        jnp.stack([gain_one, gain_two, gain_three, gain_four, gain_five]), ("dp", "mp")
    )
    piece_len = bn_scale.shape[0]
    grad_scale = lax.dynamic_slice_in_dim(gain_total, dp_index * piece_len, piece_len)
    grad_shift = lax.dynamic_slice_in_dim(bias_total, dp_index * piece_len, piece_len)
    return (
        block_out.reshape(1, local_rows, model_width),
        in_grad.reshape(1, local_rows, model_width),
        gain_sum,
        summed[0],
        summed[1],
        summed[2],
        summed[3],
        summed[4],
        summed[5],
        summed[6],
        summed[7],
        grad_scale,
        grad_shift,
        summed[8],
        summed[9],
        summed[10],
    )


def solution(mesh):
    placed = (
        P("dp", "mp", None),
        P(),
        P("dp", "mp", None),
        P(),
        P("dp", "mp"),
        P("mp", "dp"),
        P("dp", None, "mp"),
        P("dp", "mp"),
        P(None, ("mp", "dp")),
        P("mp", "dp"),
        P("dp", None, "mp"),
        P(None, ("mp", "dp")),
        P(("mp", "dp")),
        P(("mp", "dp")),
        P("mp", "dp"),
        P("dp", "mp"),
        P("mp", "dp"),
    )
    return jax.shard_map(
        body,
        mesh=mesh,
        in_specs=placed,
        out_specs=(
            P("dp", "mp", None),
            P("dp", "mp", None),
            P(),
            P("dp", "mp"),
            P("mp", "dp"),
            P("dp", None, "mp"),
            P("dp", "mp"),
            P(None, ("mp", "dp")),
            P("mp", "dp"),
            P("dp", None, "mp"),
            P(None, ("mp", "dp")),
            P(("mp", "dp")),
            P(("mp", "dp")),
            P("mp", "dp"),
            P("dp", "mp"),
            P("mp", "dp"),
        ),
        check_vma=False,
    )
```

```python
import functools
import math

import jax
import jax.numpy as jnp
from jax import lax
from jax.experimental import pallas as pl
from jax.experimental.pallas import tpu as pltpu
from jax.sharding import PartitionSpec as P

HEAD = 128


norm_eps = 1e-05
batch_eps = 1e-05
masked_score = -1000000000.0


def matmul(left, right):
    return jnp.dot(left, right, preferred_element_type=jnp.float32)


def contract_rows(left, right):
    return lax.dot_general(
        left, right, (((0,), (0,)), ((), ())), preferred_element_type=jnp.float32
    )


def contract_cols(left, right):
    return lax.dot_general(
        left, right, (((1,), (1,)), ((), ())), preferred_element_type=jnp.float32
    )


def layer_norm(values, norm_gain):
    average = jnp.mean(values, axis=-1, keepdims=True)
    centred = values - average
    inv_std = lax.rsqrt(jnp.mean(centred * centred, axis=-1, keepdims=True) + norm_eps)
    return centred * inv_std * norm_gain


def norm_back(values, norm_gain, upstream):
    unused, pullback = jax.vjp(layer_norm, values, norm_gain)
    return pullback(upstream)


def silu_slope(values):
    logistic = jax.nn.sigmoid(values)
    return logistic * (1.0 + values * (1.0 - logistic))


def position_table(seq_len, model_width):
    distance = (seq_len - 1 - jnp.arange(2 * seq_len)).astype(jnp.float32)
    frequency = jnp.exp(
        jnp.arange(model_width // 2).astype(jnp.float32) * (-2.0 * math.log(10000.0) / model_width)
    )
    angles = distance[:, None] * frequency[None, :]
    return jnp.stack([jnp.sin(angles), jnp.cos(angles)], axis=-1).reshape(2 * seq_len, model_width)


MESH = pl.DeviceIdType.MESH
VMEM_LIMIT = 60 * 1024 * 1024


def neighbour_barrier(axis):
    me = lax.axis_index(axis)
    size = lax.axis_size(axis)
    barrier = pltpu.get_barrier_semaphore()

    @pl.when(me > 0)
    def _():
        pl.semaphore_signal(barrier, inc=1, device_id={axis: me - 1}, device_id_type=MESH)

    @pl.when(me < size - 1)
    def _():
        pl.semaphore_signal(barrier, inc=1, device_id={axis: me + 1}, device_id_type=MESH)

    peers = jnp.minimum(me, 1) + jnp.minimum(size - 1 - me, 1)
    pl.semaphore_wait(barrier, peers)


def line_copy(src, dst, sems, index, axis, target):
    return pltpu.make_async_remote_copy(
        src_ref=src,
        dst_ref=dst,
        send_sem=sems.at[0, index],
        recv_sem=sems.at[1, index],
        device_id={axis: target},
        device_id_type=MESH,
    )


def line_gather_kernel(axis, in_ref, out_ref, sems):
    size = lax.axis_size(axis)
    me = lax.axis_index(axis)
    rows = in_ref.shape[0]
    steps = size - 1
    neighbour_barrier(axis)

    def piece(index):
        return out_ref.at[pl.ds(index * rows, rows)]

    def leaving(way, step):
        index = me - step if way == 0 else me + step
        return line_copy(
            in_ref if step == 0 else piece(index), piece(index), sems,
            way * steps + step, axis, me + 1 if way == 0 else me - 1,
        )

    def arriving(way, step):
        index = me - 1 - step if way == 0 else me + 1 + step
        return line_copy(in_ref, piece(index), sems, way * steps + step, axis, me)

    def go_right(step):
        return jnp.logical_and(me - step >= 0, me + 1 < size)

    def go_left(step):
        return jnp.logical_and(me + step < size, me > 0)

    for step in range(steps):
        if step > 0:
            @pl.when(me - step >= 0)
            def _():
                arriving(0, step - 1).wait_recv()

        @pl.when(go_right(step))
        def _():
            leaving(0, step).start()

        if step > 0:
            @pl.when(me + step < size)
            def _():
                arriving(1, step - 1).wait_recv()

        @pl.when(go_left(step))
        def _():
            leaving(1, step).start()

        if step == 0:
            out_ref[pl.ds(pl.multiple_of(me * rows, rows), rows), :] = in_ref[...]

    @pl.when(me - steps >= 0)
    def _():
        arriving(0, steps - 1).wait_recv()

    @pl.when(me + steps < size)
    def _():
        arriving(1, steps - 1).wait_recv()

    for step in range(steps):
        @pl.when(go_right(step))
        def _():
            leaving(0, step).wait_send()

        @pl.when(go_left(step))
        def _():
            leaving(1, step).wait_send()


def line_gather(values, axis, collective_id):
    size = lax.axis_size(axis)
    rows, width = values.shape
    return pl.pallas_call(
        functools.partial(line_gather_kernel, axis),
        out_shape=jax.ShapeDtypeStruct((size * rows, width), values.dtype),
        in_specs=[pl.BlockSpec(memory_space=pltpu.VMEM)],
        out_specs=pl.BlockSpec(memory_space=pltpu.VMEM),
        scratch_shapes=[pltpu.SemaphoreType.DMA((2, 2 * (size - 1)))],
        compiler_params=pltpu.CompilerParams(
            collective_id=collective_id, has_side_effects=True
        ),
        name="line_gather",
    )(values)


def line_scatter_kernel(axis, in_ref, out_ref, slots, staged, sems):
    size = lax.axis_size(axis)
    me = lax.axis_index(axis)
    rows = out_ref.shape[0]
    neighbour_barrier(axis)

    def own(index):
        return in_ref[index * rows : (index + 1) * rows, :].astype(jnp.float32)

    def copy(way, owner, src):
        return line_copy(
            src, slots.at[way, owner], sems, way * size + owner, axis,
            me + 1 if way == 0 else me - 1,
        )

    def hop(way, owner):
        first = me == (0 if way == 0 else size - 1)
        passes = me < owner if way == 0 else me > owner

        @pl.when(jnp.logical_and(passes, first))
        def _():
            copy(way, owner, in_ref.at[owner * rows : (owner + 1) * rows]).start()

        @pl.when(jnp.logical_and(passes, jnp.logical_not(first)))
        def _():
            copy(way, owner, staged.at[way, owner]).wait_recv()
            staged[way, owner] = (own(owner) + slots[way, owner].astype(jnp.float32)).astype(
                staged.dtype
            )
            copy(way, owner, staged.at[way, owner]).start()

    def order(first_way):
        for index in range(size - 1):
            owners = (size - 1 - index, index)
            hop(first_way, owners[first_way])
            hop(1 - first_way, owners[1 - first_way])

    @pl.when(me < size // 2)
    def _():
        order(0)

    @pl.when(me >= size // 2)
    def _():
        order(1)

    for owner in range(size):
        @pl.when(me == owner)
        def _():
            total = own(owner)
            if owner > 0:
                copy(0, owner, staged.at[0, owner]).wait_recv()
            if owner < size - 1:
                copy(1, owner, staged.at[1, owner]).wait_recv()
            if owner > 0:
                total = total + slots[0, owner].astype(jnp.float32)
            if owner < size - 1:
                total = total + slots[1, owner].astype(jnp.float32)
            out_ref[...] = total

    for owner in range(size):
        @pl.when(me < owner)
        def _():
            copy(0, owner, staged.at[0, owner]).wait_send()

        @pl.when(me > owner)
        def _():
            copy(1, owner, staged.at[1, owner]).wait_send()


def line_scatter(values, axis, collective_id):
    size = lax.axis_size(axis)
    rows, width = values.shape[0] // size, values.shape[1]
    return pl.pallas_call(
        functools.partial(line_scatter_kernel, axis),
        out_shape=jax.ShapeDtypeStruct((rows, width), jnp.float32),
        in_specs=[pl.BlockSpec(memory_space=pltpu.VMEM)],
        out_specs=pl.BlockSpec(memory_space=pltpu.VMEM),
        scratch_shapes=[
            pltpu.VMEM((2, size, rows, width), values.dtype),
            pltpu.VMEM((2, size, rows, width), values.dtype),
            pltpu.SemaphoreType.DMA((2, 2 * size)),
        ],
        compiler_params=pltpu.CompilerParams(
            collective_id=collective_id, has_side_effects=True
        ),
        name="line_scatter",
    )(values)


def bit_of(index, bit):
    return lax.rem(lax.div(index, bit), 2)


def partner(index, bit):
    return index + bit - 2 * bit * bit_of(index, bit)


def cube_bits(size, swap):
    bits = []
    bit = 2
    while bit < size:
        bits.append(bit)
        bit *= 2
    if swap:
        bits.reverse()
    return bits + [1]


def cube_copy(src, dst, sems, index, axis, target):
    return line_copy(src, dst, sems, index, axis, target)


def cube_barrier(axis):
    me = lax.axis_index(axis)
    bits = cube_bits(lax.axis_size(axis), False)
    barrier = pltpu.get_barrier_semaphore()
    for bit in bits:
        pl.semaphore_signal(
            barrier, inc=1, device_id={axis: partner(me, bit)}, device_id_type=MESH
        )
    pl.semaphore_wait(barrier, len(bits))


def block_at(ref, dim, index, width):
    start = pl.multiple_of(index * width, width)
    return ref.at[pl.ds(start, width)] if dim == 0 else ref.at[:, pl.ds(start, width)]


def cube_gather_kernel(axis, dims, ways, *refs):
    count = len(dims)
    ins, outs, (sems,) = refs[:count], refs[count : 2 * count], refs[2 * count :]
    size = lax.axis_size(axis)
    me = lax.axis_index(axis)
    stages = len(cube_bits(size, False))
    cube_barrier(axis)
    started = []
    waiting = [None] * count
    per = size - 1
    for stage in range(stages):
        for which in range(count):
            width = ins[which].shape[dims[which]]
            bits = cube_bits(size, ways[which])
            if stage == 0:
                block_at(outs[which], dims[which], me, width)[...] = ins[which][...]
            else:
                for copy in waiting[which]:
                    copy.wait_recv()
            held = [me]
            for bit in bits[:stage]:
                held = held + [partner(index, bit) for index in held]
            target = partner(me, bits[stage])
            new = []
            for number, index in enumerate(held):
                place = block_at(outs[which], dims[which], index, width)
                src = ins[which] if stage == 0 else place
                copy = cube_copy(
                    src, place, sems, which * per + 2**stage - 1 + number, axis, target
                )
                copy.start()
                new.append(copy)
            waiting[which] = new
            started.extend(new)
    for which in range(count):
        for copy in waiting[which]:
            copy.wait_recv()
    for copy in started:
        copy.wait_send()


def cube_gather(arrays, dims, ways, axis, collective_id):
    size = lax.axis_size(axis)
    count = len(arrays)
    shapes = []
    for array, dim in zip(arrays, dims):
        shape = list(array.shape)
        shape[dim] *= size
        shapes.append(jax.ShapeDtypeStruct(tuple(shape), array.dtype))
    return pl.pallas_call(
        functools.partial(cube_gather_kernel, axis, dims, ways),
        out_shape=shapes,
        in_specs=[pl.BlockSpec(memory_space=pltpu.VMEM)] * count,
        out_specs=[pl.BlockSpec(memory_space=pltpu.VMEM)] * count,
        scratch_shapes=[pltpu.SemaphoreType.DMA((2, count * (size - 1)))],
        compiler_params=pltpu.CompilerParams(
            collective_id=collective_id, has_side_effects=True, vmem_limit_bytes=VMEM_LIMIT
        ),
        name="cube_gather",
    )(*arrays)


def cube_scatter_kernel(axis, dims, ways, *refs):
    count = len(dims)
    ins, outs = refs[:count], refs[count : 2 * count]
    slots, sems = refs[2 * count : 3 * count], refs[3 * count]
    size = lax.axis_size(axis)
    me = lax.axis_index(axis)
    stages = len(cube_bits(size, False))
    per = size - 1
    cube_barrier(axis)
    started = []

    def slot(which, stage, number):
        return slots[which].at[size - size // 2**stage + number]

    def sets(which, stage):
        bits = cube_bits(size, ways[which])[::-1]
        held = [me]
        for bit in bits[stage + 1 :]:
            held = held + [partner(index, bit) for index in held]
        return bits[stage], held

    def send(which, stage):
        width = outs[which].shape[dims[which]]
        bit, held = sets(which, stage)
        target = partner(me, bit)
        for number, index in enumerate(held):
            if stage == 0:
                src = block_at(ins[which], dims[which], partner(index, bit), width)
            else:
                src = slot(which, stage - 1, 2 * number + 1)
            copy = cube_copy(
                src, slot(which, stage, number), sems,
                which * per + size - size // 2**stage + number, axis, target,
            )
            copy.start()
            started.append((which, stage, copy))

    def receive(which, stage):
        width = outs[which].shape[dims[which]]
        bit, held = sets(which, stage)
        for copy in [c for w, s, c in started if (w, s) == (which, stage)]:
            copy.wait_recv()
        for number, index in enumerate(held):
            got = slot(which, stage, number)[...].astype(jnp.float32)
            if stage == 0:
                mine = block_at(ins[which], dims[which], index, width)[...]
            else:
                mine = slot(which, stage - 1, 2 * number)[...]
            total = got + mine.astype(jnp.float32)
            if stage == stages - 1:
                outs[which][...] = total
            else:
                slot(which, stage, number)[...] = total.astype(slots[which].dtype)

    for stage in range(stages):
        for which in range(count):
            if stage > 0:
                receive(which, stage - 1)
            send(which, stage)
    for which in range(count):
        receive(which, stages - 1)
    for which, stage, copy in started:
        copy.wait_send()


def cube_scatter(arrays, dims, ways, axis, collective_id):
    size = lax.axis_size(axis)
    count = len(arrays)
    shapes, slots = [], []
    for array, dim in zip(arrays, dims):
        shape = list(array.shape)
        shape[dim] //= size
        shapes.append(jax.ShapeDtypeStruct(tuple(shape), jnp.float32))
        slots.append(pltpu.VMEM((size - 1, *shape), array.dtype))
    return pl.pallas_call(
        functools.partial(cube_scatter_kernel, axis, dims, ways),
        out_shape=shapes,
        in_specs=[pl.BlockSpec(memory_space=pltpu.VMEM)] * count,
        out_specs=[pl.BlockSpec(memory_space=pltpu.VMEM)] * count,
        scratch_shapes=slots + [pltpu.SemaphoreType.DMA((2, count * (size - 1)))],
        compiler_params=pltpu.CompilerParams(
            collective_id=collective_id, has_side_effects=True, vmem_limit_bytes=VMEM_LIMIT
        ),
        name="cube_scatter",
    )(*arrays)


def all_total_kernel(axis, in_ref, out_ref, slots, sems):
    size = lax.axis_size(axis)
    me = lax.axis_index(axis)
    barrier = pltpu.get_barrier_semaphore()
    targets = [lax.rem(me + step, size) for step in range(1, size)]
    for target in targets:
        pl.semaphore_signal(barrier, inc=1, device_id={axis: target}, device_id_type=MESH)
    pl.semaphore_wait(barrier, size - 1)
    copies = []
    for number, target in enumerate(targets):
        copy = line_copy(in_ref, slots.at[me], sems, number, axis, target)
        copy.start()
        copies.append(copy)
    slots[me] = in_ref[...]
    for copy in copies:
        copy.wait_recv()
    total = slots[0]
    for source in range(1, size):
        total = total + slots[source]
    out_ref[...] = total
    for copy in copies:
        copy.wait_send()


def all_total(values, axis, collective_id):
    size = lax.axis_size(axis)
    return pl.pallas_call(
        functools.partial(all_total_kernel, axis),
        out_shape=jax.ShapeDtypeStruct(values.shape, values.dtype),
        in_specs=[pl.BlockSpec(memory_space=pltpu.VMEM)],
        out_specs=pl.BlockSpec(memory_space=pltpu.VMEM),
        scratch_shapes=[
            pltpu.VMEM((size, *values.shape), values.dtype),
            pltpu.SemaphoreType.DMA((2, size - 1)),
        ],
        compiler_params=pltpu.CompilerParams(
            collective_id=collective_id, has_side_effects=True
        ),
        name="all_total",
    )(values)


def direct(block):
    size = lax.axis_size("dp")
    return size & (size - 1) == 0 and block % 128 == 0


def spread_rows(normed):
    if direct(normed.shape[1] // lax.axis_size("dp")):
        return line_gather(normed, "mp", 0)
    return lax.all_gather(normed, "mp", axis=0, tiled=True)


def enter_block(residual, norm_gain):
    return spread_rows(layer_norm(residual, norm_gain).astype(jnp.bfloat16))


def branch_total(partial_value):
    partial_value = partial_value.astype(jnp.bfloat16)
    if direct(partial_value.shape[1] // lax.axis_size("dp")):
        return line_scatter(partial_value, "mp", 1)
    return lax.psum_scatter(partial_value, "mp", scatter_dimension=0, tiled=True).astype(
        jnp.float32
    )


def spread_grads(upstream):
    return spread_rows(upstream)


def input_total(partial_value):
    return branch_total(partial_value)


def dp_total(values):
    if direct(128):
        return all_total(values, "dp", 2)
    return lax.psum(values, "dp")


def fetch_now(arrays, dims, small):
    if direct(arrays[0].shape[dims[0]]):
        lanes = small.shape[1]
        packed = jnp.pad(small, ((0, 16 - small.shape[0]), (0, 128 - lanes)))
        *whole, rows = cube_gather(
            [*arrays, packed], (*dims, 0), [index % 2 == 1 for index in range(len(dims) + 1)],
            "dp", 3,
        )
        size = lax.axis_size("dp")
        rows = rows.reshape(size, 16, 128)[:, : small.shape[0], :lanes]
        return whole, rows.transpose(1, 0, 2).reshape(small.shape[0], size * lanes)
    return (
        [lax.all_gather(array, "dp", axis=dim, tiled=True) for array, dim in zip(arrays, dims)],
        lax.all_gather(small, "dp", axis=1, tiled=True),
    )


def grad_totals(grads, dims, ways, small, gains):
    dp_size = lax.axis_size("dp")
    piece_len = small.shape[1] // dp_size
    grads = [grad.astype(jnp.bfloat16) for grad in grads]
    if direct(grads[0].shape[dims[0]] // dp_size):
        totals = cube_scatter(grads, dims, ways, "dp", 4)
        small = all_total(small, "dp", 5)
        gains = all_total(all_total(gains, "dp", 6), "mp", 7)
    else:
        totals = [
            lax.psum_scatter(grad, "dp", scatter_dimension=dim, tiled=True).astype(jnp.float32)
            for grad, dim in zip(grads, dims)
        ]
        small = lax.psum(small, "dp")
        gains = lax.psum(gains, ("dp", "mp"))
    start = lax.axis_index("dp") * piece_len
    return totals, lax.dynamic_slice_in_dim(small, start, piece_len, axis=1), gains


def ffn_forward(whole, weights):
    w_up, w_down = weights
    hidden = matmul(whole, w_up)
    return matmul(jax.nn.silu(hidden).astype(jnp.bfloat16), w_down)


def ffn_backward(whole, weights, grad_whole):
    w_up, w_down = weights
    hidden = matmul(whole, w_up)
    active = jax.nn.silu(hidden).astype(jnp.bfloat16)
    grad_down = contract_rows(active, grad_whole)
    d_hidden = (contract_cols(grad_whole, w_down) * silu_slope(hidden)).astype(jnp.bfloat16)
    grad_up = contract_rows(whole, d_hidden)
    return (contract_cols(d_hidden, w_up), grad_up, grad_down)


def attention_setup(whole, weights):
    w_in, w_pos, bias_pair, w_out = weights
    seq_len, model_width = whole.shape
    local_width = w_in.shape[2]
    heads_here = local_width // HEAD
    projected = matmul(whole, w_in.reshape(model_width, 3 * local_width))
    queries = projected[:, :local_width]
    key_rows = (
        projected[:, local_width : 2 * local_width]
        .astype(jnp.bfloat16)
        .reshape(seq_len, heads_here, HEAD)
    )
    value_rows = (
        projected[:, 2 * local_width :].astype(jnp.bfloat16).reshape(seq_len, heads_here, HEAD)
    )
    scaling = HEAD ** (-0.5)
    bias_float = bias_pair.astype(jnp.float32)
    query_u = (
        ((queries + bias_float[0]) * scaling)
        .astype(jnp.bfloat16)
        .reshape(seq_len, heads_here, HEAD)
    )
    query_v = (
        ((queries + bias_float[1]) * scaling)
        .astype(jnp.bfloat16)
        .reshape(seq_len, heads_here, HEAD)
    )
    table_low = position_table(seq_len, model_width).astype(jnp.bfloat16)
    position = matmul(table_low, w_pos).astype(jnp.bfloat16).reshape(2 * seq_len, heads_here, HEAD)
    return (query_u, query_v, key_rows, value_rows, table_low, position)


def skew_rows(zeds, block_rows, seq_len):
    heads_here = zeds.shape[0]
    window = block_rows + seq_len - 1
    flat = zeds.reshape(heads_here, block_rows * window)
    flat = flat[:, block_rows - 1 : block_rows - 1 + block_rows * (window - 1)]
    return flat.reshape(heads_here, block_rows, window - 1)[:, :, :seq_len]


def unskew_rows(grads_in, block_rows, seq_len):
    heads_here = grads_in.shape[0]
    window = block_rows + seq_len - 1
    padded = jnp.pad(grads_in, ((0, 0), (0, 0), (0, window - 1 - seq_len)))
    flat = padded.reshape(heads_here, block_rows * (window - 1))
    flat = jnp.pad(flat, ((0, 0), (block_rows - 1, 1)))
    return flat.reshape(heads_here, block_rows, window)


def block_scores(query_u, query_v, key_rows, position, valid_keys, offset, block_rows):
    seq_len = key_rows.shape[0]
    window = block_rows + seq_len - 1
    lowest = seq_len - offset - block_rows
    nearby = position[lowest : lowest + window]
    content = jnp.einsum("bhd,jhd->hbj", query_u, key_rows, preferred_element_type=jnp.float32)
    zeds = jnp.einsum("bhd,whd->hbw", query_v, nearby, preferred_element_type=jnp.float32)
    scores = jnp.where(
        valid_keys[None, None, :], content + skew_rows(zeds, block_rows, seq_len), masked_score
    )
    top_score = jnp.max(scores, axis=-1, keepdims=True)
    exponent = jnp.exp(scores - top_score)
    softmax_out = exponent / jnp.sum(exponent, axis=-1, keepdims=True)
    return (softmax_out, query_u, query_v, nearby, lowest)


def attention_forward(whole, weights, valid_keys, block_rows):
    seq_len = whole.shape[0]
    query_u, query_v, key_rows, value_rows, table_low, position = attention_setup(whole, weights)
    softmax_out, part_u, part_v, nearby, lowest = block_scores(
        query_u, query_v, key_rows, position, valid_keys, 0, block_rows
    )
    contexts = jnp.einsum(
        "hbj,jhd->bhd",
        softmax_out.astype(jnp.bfloat16),
        value_rows,
        preferred_element_type=jnp.float32,
    )
    context = contexts.reshape(seq_len, -1).astype(jnp.bfloat16)
    return matmul(context, weights[3])


def attention_backward(whole, weights, valid_keys, block_rows, grad_whole):
    w_in, w_pos, bias_pair, w_out = weights
    seq_len, model_width = whole.shape
    query_u, query_v, key_rows, value_rows, table_low, position = attention_setup(whole, weights)
    heads_here = key_rows.shape[1]
    local_width = w_in.shape[2]
    scaling = HEAD ** (-0.5)
    window = block_rows + seq_len - 1
    d_context = (
        contract_cols(grad_whole, w_out).astype(jnp.bfloat16).reshape(seq_len, heads_here, HEAD)
    )
    d_position = jnp.zeros(position.shape, jnp.float32)
    softmax_out, part_u, part_v, nearby, lowest = block_scores(
        query_u, query_v, key_rows, position, valid_keys, 0, block_rows
    )
    soft_low = softmax_out.astype(jnp.bfloat16)
    contexts = jnp.einsum("hbj,jhd->bhd", soft_low, value_rows, preferred_element_type=jnp.float32)
    d_soft = jnp.einsum("bhd,jhd->hbj", d_context, value_rows, preferred_element_type=jnp.float32)
    inner = jnp.sum(softmax_out * d_soft, axis=-1, keepdims=True)
    d_scores = (softmax_out * (d_soft - inner)).astype(jnp.bfloat16)
    d_query_u = jnp.einsum("hbj,jhd->bhd", d_scores, key_rows, preferred_element_type=jnp.float32)
    d_keys = jnp.einsum("hbj,bhd->jhd", d_scores, part_u, preferred_element_type=jnp.float32)
    d_values = jnp.einsum("hbj,bhd->jhd", soft_low, d_context, preferred_element_type=jnp.float32)
    d_zeds = unskew_rows(d_scores, block_rows, seq_len)
    d_query_v = jnp.einsum("hbw,whd->bhd", d_zeds, nearby, preferred_element_type=jnp.float32)
    d_position = d_position.at[lowest : lowest + window].add(
        jnp.einsum("hbw,bhd->whd", d_zeds, part_v, preferred_element_type=jnp.float32)
    )
    grad_u = d_query_u.reshape(seq_len, local_width) * scaling
    grad_v = d_query_v.reshape(seq_len, local_width) * scaling
    d_queries = (grad_u + grad_v).astype(jnp.bfloat16)
    grad_bias = jnp.stack([jnp.sum(grad_u, axis=0), jnp.sum(grad_v, axis=0)])
    d_projected = jnp.concatenate(
        [
            d_queries,
            d_keys.reshape(seq_len, local_width).astype(jnp.bfloat16),
            d_values.reshape(seq_len, local_width).astype(jnp.bfloat16),
        ],
        axis=1,
    )
    grad_in = contract_rows(whole, d_projected).reshape(model_width, 3, local_width)
    d_normed = contract_cols(d_projected, w_in.reshape(model_width, 3 * local_width))
    grad_pos = contract_rows(
        table_low, d_position.reshape(2 * seq_len, local_width).astype(jnp.bfloat16)
    )
    context = contexts.reshape(seq_len, local_width).astype(jnp.bfloat16)
    grad_out = contract_rows(context, grad_whole)
    return (d_normed, grad_in, grad_pos, grad_bias, grad_out)


def conv_front(whole, w_in, kernel, mask_col):
    seq_len, model_width = whole.shape
    local_width = w_in.shape[2]
    glu_in = matmul(whole, w_in.reshape(model_width, 2 * local_width))
    gate_value = glu_in[:, :local_width]
    logistic = jax.nn.sigmoid(glu_in[:, local_width:])
    glu_out = gate_value * logistic * mask_col
    tap_count = kernel.shape[0]
    half_taps = (tap_count - 1) // 2
    padded = jnp.pad(glu_out, ((half_taps, half_taps), (0, 0)))
    kernel_float = kernel.astype(jnp.float32)
    conved = kernel_float[0] * padded[0:seq_len]
    for tap_index in range(1, tap_count):
        conved = conved + kernel_float[tap_index] * padded[tap_index : tap_index + seq_len]
    return (gate_value, logistic, padded, conved)


def batch_stats(conved, mask_col, frame_count):
    local_sum = jnp.sum(conved * mask_col, axis=0)
    local_squares = jnp.sum(conved * conved * mask_col, axis=0)
    total_sum, total_squares = dp_total(jnp.stack([local_sum, local_squares]))
    average = total_sum / frame_count
    variance = total_squares / frame_count - average * average
    return (average, lax.rsqrt(variance + batch_eps))


def conv_tail(conved, stats, bn_gain, bn_bias):
    average, inv_std = stats
    normed_b = (conved - average) * inv_std * bn_gain.astype(jnp.float32) + bn_bias.astype(
        jnp.float32
    )
    return (normed_b, jax.nn.silu(normed_b).astype(jnp.bfloat16))


def conv_backward(whole, weights, mask_col, stats, frame_count, grad_whole):
    w_in, kernel, bn_gain, bn_bias, w_out = weights
    seq_len, model_width = whole.shape
    local_width = w_in.shape[2]
    gate_value, logistic, padded, conved = conv_front(whole, w_in, kernel, mask_col)
    normed_b, active = conv_tail(conved, stats, bn_gain, bn_bias)
    average, inv_std = stats
    grad_out = contract_rows(active, grad_whole)
    d_normed = contract_cols(grad_whole, w_out) * silu_slope(normed_b)
    centred = (conved - average) * inv_std
    bias_total, gain_total = dp_total(
        jnp.stack([jnp.sum(d_normed, axis=0), jnp.sum(d_normed * centred, axis=0)])
    )
    d_conved = (
        bn_gain.astype(jnp.float32)
        * inv_std
        * (d_normed - mask_col * (bias_total + centred * gain_total) / frame_count)
    )
    tap_count = kernel.shape[0]
    half_taps = (tap_count - 1) // 2
    kernel_float = kernel.astype(jnp.float32)
    d_padded = jnp.pad(d_conved, ((half_taps, half_taps), (0, 0)))
    d_glu = kernel_float[0] * d_padded[tap_count - 1 : tap_count - 1 + seq_len]
    for tap_index in range(1, tap_count):
        d_glu = (
            d_glu
            + kernel_float[tap_index]
            * d_padded[tap_count - 1 - tap_index : tap_count - 1 - tap_index + seq_len]
        )
    grad_kernel = jnp.stack(
        [
            jnp.sum(d_conved * padded[tap_index : tap_index + seq_len], axis=0)
            for tap_index in range(tap_count)
        ]
    )
    d_glu = d_glu * mask_col
    d_pair = jnp.concatenate(
        [d_glu * logistic, d_glu * gate_value * logistic * (1.0 - logistic)], axis=1
    ).astype(jnp.bfloat16)
    grad_in = contract_rows(whole, d_pair).reshape(model_width, 2, local_width)
    d_normed_in = contract_cols(d_pair, w_in.reshape(model_width, 2 * local_width))
    return (d_normed_in, grad_in, grad_kernel, grad_out, gain_total, bias_total)


def body(
    frames_in,
    lengths,
    out_grad,
    norm_gains,
    ffn1_up,
    ffn1_down,
    attn_in,
    pos_proj,
    pos_bias,
    attn_out,
    conv_in,
    depthwise,
    bn_scale,
    bn_shift,
    conv_out,
    ffn2_up,
    ffn2_down,
):
    unused, local_rows, model_width = frames_in.shape
    seq_len = local_rows * lax.axis_size("mp")
    block_rows = min(seq_len, 512)
    dp_index = lax.axis_index("dp")
    own_length = lax.dynamic_slice_in_dim(lengths, dp_index, 1)[0]
    valid_keys = jnp.arange(seq_len) < own_length
    mask_col = valid_keys.astype(jnp.float32)[:, None]
    frame_count = jnp.sum(lengths).astype(jnp.float32)
    layer_input = frames_in.reshape(local_rows, model_width).astype(jnp.float32)
    (up_one, down_one, pos_whole, attn_out_whole, conv_out_whole), small = fetch_now(
        [ffn1_up, ffn1_down, pos_proj, attn_out, conv_out],
        (0, 1, 0, 1, 1),
        jnp.concatenate([pos_bias, depthwise, bn_scale[None], bn_shift[None]], axis=0),
    )
    taps = depthwise.shape[0]
    ffn_first = (up_one, down_one)
    attn_held = (
        lax.all_gather(attn_in, "dp", axis=0, tiled=True),
        pos_whole,
        small[:2],
        attn_out_whole,
    )
    conv_held = (
        lax.all_gather(conv_in, "dp", axis=0, tiled=True),
        small[2 : 2 + taps],
        small[2 + taps],
        small[3 + taps],
        conv_out_whole,
    )
    ffn_second = (
        lax.all_gather(ffn2_up, "dp", axis=0, tiled=True),
        lax.all_gather(ffn2_down, "dp", axis=1, tiled=True),
    )
    whole_first = enter_block(layer_input, norm_gains[0])
    after_first = layer_input + 0.5 * branch_total(ffn_forward(whole_first, ffn_first))
    whole_attn = enter_block(after_first, norm_gains[1])
    after_attn = after_first + branch_total(
        attention_forward(whole_attn, attn_held, valid_keys, block_rows)
    )
    whole_conv = enter_block(after_attn, norm_gains[2])
    gate_value, logistic, padded, conved = conv_front(
        whole_conv, conv_held[0], conv_held[1], mask_col
    )
    stats = batch_stats(conved, mask_col, frame_count)
    normed_b, active = conv_tail(conved, stats, conv_held[2], conv_held[3])
    after_conv = after_attn + branch_total(matmul(active, conv_held[4]))
    whole_second = enter_block(after_conv, norm_gains[3])
    after_second = after_conv + 0.5 * branch_total(ffn_forward(whole_second, ffn_second))
    block_out = layer_norm(after_second, norm_gains[4]).astype(jnp.bfloat16)
    d_second, gain_five = norm_back(
        after_second, norm_gains[4], out_grad.reshape(local_rows, model_width).astype(jnp.float32)
    )
    d_normed, grad_up_two, grad_down_two = ffn_backward(
        whole_second,
        ffn_second,
        spread_grads((0.5 * d_second).astype(jnp.bfloat16)),
    )
    d_branch, gain_four = norm_back(after_conv, norm_gains[3], input_total(d_normed))
    d_conv = d_second + d_branch
    d_normed, grad_conv_in, grad_kernel, grad_conv_out, gain_total, bias_total = conv_backward(
        whole_conv,
        conv_held,
        mask_col,
        stats,
        frame_count,
        spread_grads(d_conv.astype(jnp.bfloat16)),
    )
    d_branch, gain_three = norm_back(after_attn, norm_gains[2], input_total(d_normed))
    d_attn = d_conv + d_branch
    d_normed, grad_attn_in, grad_pos, grad_bias, grad_attn_out = attention_backward(
        whole_attn,
        attn_held,
        valid_keys,
        block_rows,
        spread_grads(d_attn.astype(jnp.bfloat16)),
    )
    d_branch, gain_two = norm_back(after_first, norm_gains[1], input_total(d_normed))
    d_first = d_attn + d_branch
    d_normed, grad_up_one, grad_down_one = ffn_backward(
        whole_first,
        ffn_first,
        spread_grads((0.5 * d_first).astype(jnp.bfloat16)),
    )
    d_branch, gain_one = norm_back(layer_input, norm_gains[0], input_total(d_normed))
    in_grad = d_first + d_branch
    totals, small_grads, gain_sum = grad_totals(
        [
            grad_up_two,
            grad_down_two,
            grad_conv_in.reshape(model_width, -1),
            grad_conv_out,
            grad_attn_in.reshape(model_width, -1),
            grad_attn_out,
            grad_pos,
            grad_up_one,
            grad_down_one,
        ],
        (0, 1, 0, 1, 0, 1, 0, 0, 1),
        (False, True, True, True, False, True, False, False, True),
        jnp.concatenate([grad_bias, grad_kernel], axis=0),
        jnp.stack([gain_one, gain_two, gain_three, gain_four, gain_five]),
    )
    block = model_width // lax.axis_size("dp")
    summed = (
        totals[7],
        totals[8],
        totals[4].reshape(block, 3, -1),
        totals[6],
        small_grads[:2],
        totals[5],
        totals[2].reshape(block, 2, -1),
        small_grads[2:],
        totals[3],
        totals[0],
        totals[1],
    )
    piece_len = bn_scale.shape[0]
    grad_scale = lax.dynamic_slice_in_dim(gain_total, dp_index * piece_len, piece_len)
    grad_shift = lax.dynamic_slice_in_dim(bias_total, dp_index * piece_len, piece_len)
    return (
        block_out.reshape(1, local_rows, model_width),
        in_grad.reshape(1, local_rows, model_width),
        gain_sum,
        summed[0],
        summed[1],
        summed[2],
        summed[3],
        summed[4],
        summed[5],
        summed[6],
        summed[7],
        grad_scale,
        grad_shift,
        summed[8],
        summed[9],
        summed[10],
    )


def solution(mesh):
    placed = (
        P("dp", "mp", None),
        P(),
        P("dp", "mp", None),
        P(),
        P("dp", "mp"),
        P("mp", "dp"),
        P("dp", None, "mp"),
        P("dp", "mp"),
        P(None, ("mp", "dp")),
        P("mp", "dp"),
        P("dp", None, "mp"),
        P(None, ("mp", "dp")),
        P(("mp", "dp")),
        P(("mp", "dp")),
        P("mp", "dp"),
        P("dp", "mp"),
        P("mp", "dp"),
    )
    return jax.shard_map(
        body,
        mesh=mesh,
        in_specs=placed,
        out_specs=(
            P("dp", "mp", None),
            P("dp", "mp", None),
            P(),
            P("dp", "mp"),
            P("mp", "dp"),
            P("dp", None, "mp"),
            P("dp", "mp"),
            P(None, ("mp", "dp")),
            P("mp", "dp"),
            P("dp", None, "mp"),
            P(None, ("mp", "dp")),
            P(("mp", "dp")),
            P(("mp", "dp")),
            P("mp", "dp"),
            P("dp", "mp"),
            P("mp", "dp"),
        ),
        check_vma=False,
    )
```

```python
import functools
import math

import jax
import jax.numpy as jnp
from jax import lax
from jax.experimental import pallas as pl
from jax.experimental.pallas import tpu as pltpu
from jax.sharding import PartitionSpec as P

HEAD = 128


norm_eps = 1e-05
batch_eps = 1e-05
masked_score = -1000000000.0


def matmul(left, right):
    return jnp.dot(left, right, preferred_element_type=jnp.float32)


def contract_rows(left, right):
    return lax.dot_general(
        left, right, (((0,), (0,)), ((), ())), preferred_element_type=jnp.float32
    )


def contract_cols(left, right):
    return lax.dot_general(
        left, right, (((1,), (1,)), ((), ())), preferred_element_type=jnp.float32
    )


def layer_norm(values, norm_gain):
    average = jnp.mean(values, axis=-1, keepdims=True)
    centred = values - average
    inv_std = lax.rsqrt(jnp.mean(centred * centred, axis=-1, keepdims=True) + norm_eps)
    return centred * inv_std * norm_gain


def norm_back(values, norm_gain, upstream):
    unused, pullback = jax.vjp(layer_norm, values, norm_gain)
    return pullback(upstream)


def silu_slope(values):
    logistic = jax.nn.sigmoid(values)
    return logistic * (1.0 + values * (1.0 - logistic))


def position_table(seq_len, model_width):
    fine = 32
    lane = jnp.arange(model_width)
    frequency = jnp.exp((lane // 2).astype(jnp.float32) * (-2.0 * math.log(10000.0) / model_width))
    coarse = (seq_len - 1 - fine * jnp.arange(2 * seq_len // fine)).astype(jnp.float32)
    wide = coarse[:, None] * frequency[None, :]
    small = -jnp.arange(fine).astype(jnp.float32)[:, None] * frequency[None, :]
    even = (lane % 2 == 0)[None, :]
    wide_sin, wide_cos = jnp.sin(wide), jnp.cos(wide)
    high = jnp.where(even, wide_sin, wide_cos)
    side = jnp.where(even, wide_cos, -wide_sin)
    table = high[:, None, :] * jnp.cos(small)[None] + side[:, None, :] * jnp.sin(small)[None]
    return table.reshape(2 * seq_len, model_width)


MESH = pl.DeviceIdType.MESH
VMEM_LIMIT = 60 * 1024 * 1024


def neighbour_barrier(axis):
    me = lax.axis_index(axis)
    size = lax.axis_size(axis)
    barrier = pltpu.get_barrier_semaphore()

    @pl.when(me > 0)
    def _():
        pl.semaphore_signal(barrier, inc=1, device_id={axis: me - 1}, device_id_type=MESH)

    @pl.when(me < size - 1)
    def _():
        pl.semaphore_signal(barrier, inc=1, device_id={axis: me + 1}, device_id_type=MESH)

    peers = jnp.minimum(me, 1) + jnp.minimum(size - 1 - me, 1)
    pl.semaphore_wait(barrier, peers)


def line_copy(src, dst, sems, index, axis, target):
    return pltpu.make_async_remote_copy(
        src_ref=src,
        dst_ref=dst,
        send_sem=sems.at[0, index],
        recv_sem=sems.at[1, index],
        device_id={axis: target},
        device_id_type=MESH,
    )


def line_gather_kernel(axis, in_ref, out_ref, sems):
    size = lax.axis_size(axis)
    me = lax.axis_index(axis)
    rows = in_ref.shape[0]
    steps = size - 1
    neighbour_barrier(axis)

    def piece(index):
        return out_ref.at[pl.ds(index * rows, rows)]

    def leaving(way, step):
        index = me - step if way == 0 else me + step
        return line_copy(
            in_ref if step == 0 else piece(index), piece(index), sems,
            way * steps + step, axis, me + 1 if way == 0 else me - 1,
        )

    def arriving(way, step):
        index = me - 1 - step if way == 0 else me + 1 + step
        return line_copy(in_ref, piece(index), sems, way * steps + step, axis, me)

    def go_right(step):
        return jnp.logical_and(me - step >= 0, me + 1 < size)

    def go_left(step):
        return jnp.logical_and(me + step < size, me > 0)

    for step in range(steps):
        if step > 0:
            @pl.when(me - step >= 0)
            def _():
                arriving(0, step - 1).wait_recv()

        @pl.when(go_right(step))
        def _():
            leaving(0, step).start()

        if step > 0:
            @pl.when(me + step < size)
            def _():
                arriving(1, step - 1).wait_recv()

        @pl.when(go_left(step))
        def _():
            leaving(1, step).start()

        if step == 0:
            out_ref[pl.ds(pl.multiple_of(me * rows, rows), rows), :] = in_ref[...]

    @pl.when(me - steps >= 0)
    def _():
        arriving(0, steps - 1).wait_recv()

    @pl.when(me + steps < size)
    def _():
        arriving(1, steps - 1).wait_recv()

    for step in range(steps):
        @pl.when(go_right(step))
        def _():
            leaving(0, step).wait_send()

        @pl.when(go_left(step))
        def _():
            leaving(1, step).wait_send()


def line_gather(values, axis, collective_id):
    size = lax.axis_size(axis)
    rows, width = values.shape
    return pl.pallas_call(
        functools.partial(line_gather_kernel, axis),
        out_shape=jax.ShapeDtypeStruct((size * rows, width), values.dtype),
        in_specs=[pl.BlockSpec(memory_space=pltpu.VMEM)],
        out_specs=pl.BlockSpec(memory_space=pltpu.VMEM),
        scratch_shapes=[pltpu.SemaphoreType.DMA((2, 2 * (size - 1)))],
        compiler_params=pltpu.CompilerParams(
            collective_id=collective_id, has_side_effects=True
        ),
        name="line_gather",
    )(values)


def line_scatter_kernel(axis, in_ref, out_ref, slots, staged, sems):
    size = lax.axis_size(axis)
    me = lax.axis_index(axis)
    rows = out_ref.shape[0]
    neighbour_barrier(axis)

    def own(index):
        return in_ref[index * rows : (index + 1) * rows, :].astype(jnp.float32)

    def copy(way, owner, src):
        return line_copy(
            src, slots.at[way, owner], sems, way * size + owner, axis,
            me + 1 if way == 0 else me - 1,
        )

    def hop(way, owner):
        first = me == (0 if way == 0 else size - 1)
        passes = me < owner if way == 0 else me > owner

        @pl.when(jnp.logical_and(passes, first))
        def _():
            copy(way, owner, in_ref.at[owner * rows : (owner + 1) * rows]).start()

        @pl.when(jnp.logical_and(passes, jnp.logical_not(first)))
        def _():
            copy(way, owner, staged.at[way, owner]).wait_recv()
            staged[way, owner] = (own(owner) + slots[way, owner].astype(jnp.float32)).astype(
                staged.dtype
            )
            copy(way, owner, staged.at[way, owner]).start()

    def order(first_way):
        for index in range(size - 1):
            owners = (size - 1 - index, index)
            hop(first_way, owners[first_way])
            hop(1 - first_way, owners[1 - first_way])

    @pl.when(me < size // 2)
    def _():
        order(0)

    @pl.when(me >= size // 2)
    def _():
        order(1)

    for owner in range(size):
        @pl.when(me == owner)
        def _():
            total = own(owner)
            if owner > 0:
                copy(0, owner, staged.at[0, owner]).wait_recv()
            if owner < size - 1:
                copy(1, owner, staged.at[1, owner]).wait_recv()
            if owner > 0:
                total = total + slots[0, owner].astype(jnp.float32)
            if owner < size - 1:
                total = total + slots[1, owner].astype(jnp.float32)
            out_ref[...] = total

    for owner in range(size):
        @pl.when(me < owner)
        def _():
            copy(0, owner, staged.at[0, owner]).wait_send()

        @pl.when(me > owner)
        def _():
            copy(1, owner, staged.at[1, owner]).wait_send()


def line_scatter(values, axis, collective_id):
    size = lax.axis_size(axis)
    rows, width = values.shape[0] // size, values.shape[1]
    return pl.pallas_call(
        functools.partial(line_scatter_kernel, axis),
        out_shape=jax.ShapeDtypeStruct((rows, width), jnp.float32),
        in_specs=[pl.BlockSpec(memory_space=pltpu.VMEM)],
        out_specs=pl.BlockSpec(memory_space=pltpu.VMEM),
        scratch_shapes=[
            pltpu.VMEM((2, size, rows, width), values.dtype),
            pltpu.VMEM((2, size, rows, width), values.dtype),
            pltpu.SemaphoreType.DMA((2, 2 * size)),
        ],
        compiler_params=pltpu.CompilerParams(
            collective_id=collective_id, has_side_effects=True
        ),
        name="line_scatter",
    )(values)


def bit_of(index, bit):
    return lax.rem(lax.div(index, bit), 2)


def partner(index, bit):
    return index + bit - 2 * bit * bit_of(index, bit)


def cube_bits(size, swap):
    bits = []
    bit = 2
    while bit < size:
        bits.append(bit)
        bit *= 2
    if swap:
        bits.reverse()
    return bits + [1]


def cube_copy(src, dst, sems, index, axis, target):
    return line_copy(src, dst, sems, index, axis, target)


def cube_barrier(axis):
    me = lax.axis_index(axis)
    bits = cube_bits(lax.axis_size(axis), False)
    barrier = pltpu.get_barrier_semaphore()
    for bit in bits:
        pl.semaphore_signal(
            barrier, inc=1, device_id={axis: partner(me, bit)}, device_id_type=MESH
        )
    pl.semaphore_wait(barrier, len(bits))


def block_at(ref, dim, index, width):
    start = pl.multiple_of(index * width, width)
    return ref.at[pl.ds(start, width)] if dim == 0 else ref.at[:, pl.ds(start, width)]


def cube_gather_kernel(axis, dims, ways, *refs):
    count = len(dims)
    ins, outs, (sems,) = refs[:count], refs[count : 2 * count], refs[2 * count :]
    size = lax.axis_size(axis)
    me = lax.axis_index(axis)
    stages = len(cube_bits(size, False))
    cube_barrier(axis)
    started = []
    waiting = [None] * count
    per = size - 1
    for stage in range(stages):
        for which in range(count):
            width = ins[which].shape[dims[which]]
            bits = cube_bits(size, ways[which])
            if stage == 0:
                block_at(outs[which], dims[which], me, width)[...] = ins[which][...]
            else:
                for copy in waiting[which]:
                    copy.wait_recv()
            held = [me]
            for bit in bits[:stage]:
                held = held + [partner(index, bit) for index in held]
            target = partner(me, bits[stage])
            new = []
            for number, index in enumerate(held):
                place = block_at(outs[which], dims[which], index, width)
                src = ins[which] if stage == 0 else place
                copy = cube_copy(
                    src, place, sems, which * per + 2**stage - 1 + number, axis, target
                )
                copy.start()
                new.append(copy)
            waiting[which] = new
            started.extend(new)
    for which in range(count):
        for copy in waiting[which]:
            copy.wait_recv()
    for copy in started:
        copy.wait_send()


def cube_gather(arrays, dims, ways, axis, collective_id):
    size = lax.axis_size(axis)
    count = len(arrays)
    shapes = []
    for array, dim in zip(arrays, dims):
        shape = list(array.shape)
        shape[dim] *= size
        shapes.append(jax.ShapeDtypeStruct(tuple(shape), array.dtype))
    return pl.pallas_call(
        functools.partial(cube_gather_kernel, axis, dims, ways),
        out_shape=shapes,
        in_specs=[pl.BlockSpec(memory_space=pltpu.VMEM)] * count,
        out_specs=[pl.BlockSpec(memory_space=pltpu.VMEM)] * count,
        scratch_shapes=[pltpu.SemaphoreType.DMA((2, count * (size - 1)))],
        compiler_params=pltpu.CompilerParams(
            collective_id=collective_id, has_side_effects=True, vmem_limit_bytes=VMEM_LIMIT
        ),
        name="cube_gather",
    )(*arrays)


def cube_scatter_kernel(axis, dims, ways, *refs):
    count = len(dims)
    ins, outs = refs[:count], refs[count : 2 * count]
    slots, sems = refs[2 * count : 3 * count], refs[3 * count]
    size = lax.axis_size(axis)
    me = lax.axis_index(axis)
    stages = len(cube_bits(size, False))
    per = size - 1
    cube_barrier(axis)
    started = []

    def slot(which, stage, number):
        return slots[which].at[size - size // 2**stage + number]

    def sets(which, stage):
        bits = cube_bits(size, ways[which])[::-1]
        held = [me]
        for bit in bits[stage + 1 :]:
            held = held + [partner(index, bit) for index in held]
        return bits[stage], held

    def send(which, stage):
        width = outs[which].shape[dims[which]]
        bit, held = sets(which, stage)
        target = partner(me, bit)
        for number, index in enumerate(held):
            if stage == 0:
                src = block_at(ins[which], dims[which], partner(index, bit), width)
            else:
                src = slot(which, stage - 1, 2 * number + 1)
            copy = cube_copy(
                src, slot(which, stage, number), sems,
                which * per + size - size // 2**stage + number, axis, target,
            )
            copy.start()
            started.append((which, stage, copy))

    def receive(which, stage):
        width = outs[which].shape[dims[which]]
        bit, held = sets(which, stage)
        for copy in [c for w, s, c in started if (w, s) == (which, stage)]:
            copy.wait_recv()
        for number, index in enumerate(held):
            got = slot(which, stage, number)[...].astype(jnp.float32)
            if stage == 0:
                mine = block_at(ins[which], dims[which], index, width)[...]
            else:
                mine = slot(which, stage - 1, 2 * number)[...]
            total = got + mine.astype(jnp.float32)
            if stage == stages - 1:
                outs[which][...] = total
            else:
                slot(which, stage, number)[...] = total.astype(slots[which].dtype)

    for stage in range(stages):
        for which in range(count):
            if stage > 0:
                receive(which, stage - 1)
            send(which, stage)
    for which in range(count):
        receive(which, stages - 1)
    for which, stage, copy in started:
        copy.wait_send()


def cube_scatter(arrays, dims, ways, axis, collective_id):
    size = lax.axis_size(axis)
    count = len(arrays)
    shapes, slots = [], []
    for array, dim in zip(arrays, dims):
        shape = list(array.shape)
        shape[dim] //= size
        shapes.append(jax.ShapeDtypeStruct(tuple(shape), jnp.float32))
        slots.append(pltpu.VMEM((size - 1, *shape), array.dtype))
    return pl.pallas_call(
        functools.partial(cube_scatter_kernel, axis, dims, ways),
        out_shape=shapes,
        in_specs=[pl.BlockSpec(memory_space=pltpu.VMEM)] * count,
        out_specs=[pl.BlockSpec(memory_space=pltpu.VMEM)] * count,
        scratch_shapes=slots + [pltpu.SemaphoreType.DMA((2, count * (size - 1)))],
        compiler_params=pltpu.CompilerParams(
            collective_id=collective_id, has_side_effects=True, vmem_limit_bytes=VMEM_LIMIT
        ),
        name="cube_scatter",
    )(*arrays)


def all_total_kernel(axis, in_ref, out_ref, slots, sems):
    size = lax.axis_size(axis)
    me = lax.axis_index(axis)
    barrier = pltpu.get_barrier_semaphore()
    targets = [lax.rem(me + step, size) for step in range(1, size)]
    for target in targets:
        pl.semaphore_signal(barrier, inc=1, device_id={axis: target}, device_id_type=MESH)
    pl.semaphore_wait(barrier, size - 1)
    copies = []
    for number, target in enumerate(targets):
        copy = line_copy(in_ref, slots.at[me], sems, number, axis, target)
        copy.start()
        copies.append(copy)
    slots[me] = in_ref[...]
    for copy in copies:
        copy.wait_recv()
    total = slots[0]
    for source in range(1, size):
        total = total + slots[source]
    out_ref[...] = total
    for copy in copies:
        copy.wait_send()


def all_total(values, axis, collective_id):
    size = lax.axis_size(axis)
    return pl.pallas_call(
        functools.partial(all_total_kernel, axis),
        out_shape=jax.ShapeDtypeStruct(values.shape, values.dtype),
        in_specs=[pl.BlockSpec(memory_space=pltpu.VMEM)],
        out_specs=pl.BlockSpec(memory_space=pltpu.VMEM),
        scratch_shapes=[
            pltpu.VMEM((size, *values.shape), values.dtype),
            pltpu.SemaphoreType.DMA((2, size - 1)),
        ],
        compiler_params=pltpu.CompilerParams(
            collective_id=collective_id, has_side_effects=True
        ),
        name="all_total",
    )(values)


def direct(block):
    size = lax.axis_size("dp")
    return size & (size - 1) == 0 and block % 128 == 0


def spread_rows(normed):
    if direct(normed.shape[1] // lax.axis_size("dp")):
        return line_gather(normed, "mp", 0)
    return lax.all_gather(normed, "mp", axis=0, tiled=True)


def enter_block(residual, norm_gain):
    return spread_rows(layer_norm(residual, norm_gain).astype(jnp.bfloat16))


def branch_total(partial_value):
    partial_value = partial_value.astype(jnp.bfloat16)
    if direct(partial_value.shape[1] // lax.axis_size("dp")):
        return line_scatter(partial_value, "mp", 1)
    return lax.psum_scatter(partial_value, "mp", scatter_dimension=0, tiled=True).astype(
        jnp.float32
    )


def spread_grads(upstream):
    return spread_rows(upstream)


def input_total(partial_value):
    return branch_total(partial_value)


def dp_total(values):
    if direct(128):
        return all_total(values, "dp", 2)
    return lax.psum(values, "dp")


def fetch_now(arrays, dims, small):
    if direct(arrays[0].shape[dims[0]]):
        lanes = small.shape[1]
        packed = jnp.pad(small, ((0, 16 - small.shape[0]), (0, 128 - lanes)))
        *whole, rows = cube_gather(
            [*arrays, packed], (*dims, 0), [index % 2 == 1 for index in range(len(dims) + 1)],
            "dp", 3,
        )
        size = lax.axis_size("dp")
        rows = rows.reshape(size, 16, 128)[:, : small.shape[0], :lanes]
        return whole, rows.transpose(1, 0, 2).reshape(small.shape[0], size * lanes)
    return (
        [lax.all_gather(array, "dp", axis=dim, tiled=True) for array, dim in zip(arrays, dims)],
        lax.all_gather(small, "dp", axis=1, tiled=True),
    )


def grad_totals(grads, dims, ways, small, gains):
    dp_size = lax.axis_size("dp")
    piece_len = small.shape[1] // dp_size
    grads = [grad.astype(jnp.bfloat16) for grad in grads]
    if direct(grads[0].shape[dims[0]] // dp_size):
        totals = cube_scatter(grads, dims, ways, "dp", 4)
        small = all_total(small, "dp", 5)
        gains = all_total(all_total(gains, "dp", 6), "mp", 7)
    else:
        totals = [
            lax.psum_scatter(grad, "dp", scatter_dimension=dim, tiled=True).astype(jnp.float32)
            for grad, dim in zip(grads, dims)
        ]
        small = lax.psum(small, "dp")
        gains = lax.psum(gains, ("dp", "mp"))
    start = lax.axis_index("dp") * piece_len
    return totals, lax.dynamic_slice_in_dim(small, start, piece_len, axis=1), gains


def ffn_forward(whole, weights):
    w_up, w_down = weights
    hidden = matmul(whole, w_up)
    return matmul(jax.nn.silu(hidden).astype(jnp.bfloat16), w_down)


def ffn_backward(whole, weights, grad_whole):
    w_up, w_down = weights
    hidden = matmul(whole, w_up)
    active = jax.nn.silu(hidden).astype(jnp.bfloat16)
    grad_down = contract_rows(active, grad_whole)
    d_hidden = (contract_cols(grad_whole, w_down) * silu_slope(hidden)).astype(jnp.bfloat16)
    grad_up = contract_rows(whole, d_hidden)
    return (contract_cols(d_hidden, w_up), grad_up, grad_down)


def place_position(position_ref, block, rows, seq_len):
    start = pl.multiple_of(seq_len - rows - block * rows, rows)
    return position_ref.at[pl.ds(start, seq_len + rows)]


def attention_kernel(
    scaling, length_ref, whole_ref, in_ref, bias_ref, position_ref, out_w_ref,
    partial_ref, probs_ref, context_ref, query_u_ref, query_v_ref, key_ref, value_ref,
):
    block = pl.program_id(0)
    seq_len, local_width = key_ref.shape
    rows = partial_ref.shape[0]

    @pl.when(block == 0)
    def _():
        projected = matmul(whole_ref[...], in_ref[...])
        queries = projected[:, :local_width]
        query_u_ref[...] = ((queries + bias_ref[0:1]) * scaling).astype(jnp.bfloat16)
        query_v_ref[...] = ((queries + bias_ref[1:2]) * scaling).astype(jnp.bfloat16)
        key_ref[...] = projected[:, local_width : 2 * local_width].astype(jnp.bfloat16)
        value_ref[...] = projected[:, 2 * local_width :].astype(jnp.bfloat16)

    here = pl.ds(pl.multiple_of(block * rows, rows), rows)
    valid = lax.broadcasted_iota(jnp.int32, (rows, seq_len), 1) < length_ref[0]
    nearby = place_position(position_ref, block, rows, seq_len)
    pieces = []
    for head in range(local_width // HEAD):
        lanes = slice(head * HEAD, (head + 1) * HEAD)
        content = contract_cols(query_u_ref[here, lanes], key_ref[:, lanes])
        zeds = contract_cols(query_v_ref[here, lanes], nearby[:, lanes])
        shifted = pltpu.roll(zeds, seq_len + 1, 1, stride=1, stride_axis=0)[:, :seq_len]
        scores = jnp.where(valid, content + shifted, masked_score)
        exponent = jnp.exp(scores - jnp.max(scores, axis=-1, keepdims=True))
        probs = exponent / jnp.sum(exponent, axis=-1, keepdims=True)
        probs_ref[head] = probs
        pieces.append(matmul(probs.astype(jnp.bfloat16), value_ref[:, lanes]).astype(jnp.bfloat16))
    context = jnp.concatenate(pieces, axis=1)
    context_ref[...] = context
    partial_ref[...] = matmul(context, out_w_ref[...]).astype(jnp.bfloat16)


def attention_forward(whole, weights, position, own_length):
    w_in, w_pos, bias_pair, w_out = weights
    seq_len, model_width = whole.shape
    local_width = w_out.shape[0]
    heads_here = local_width // HEAD
    rows = 128
    full = pl.BlockSpec(memory_space=pltpu.VMEM)
    low = jnp.bfloat16
    return pl.pallas_call(
        functools.partial(attention_kernel, HEAD ** (-0.5)),
        grid=(seq_len // rows,),
        out_shape=[
            jax.ShapeDtypeStruct((seq_len, model_width), low),
            jax.ShapeDtypeStruct((heads_here, seq_len, seq_len), jnp.float32),
        ]
        + [jax.ShapeDtypeStruct((seq_len, local_width), low)] * 5,
        in_specs=[pl.BlockSpec(memory_space=pltpu.SMEM)] + [full] * 5,
        out_specs=[
            pl.BlockSpec((rows, model_width), lambda block: (block, 0)),
            pl.BlockSpec((heads_here, rows, seq_len), lambda block: (0, block, 0)),
            pl.BlockSpec((rows, local_width), lambda block: (block, 0)),
        ]
        + [full] * 4,
        compiler_params=pltpu.CompilerParams(vmem_limit_bytes=VMEM_LIMIT),
        name="attention_forward",
    )(own_length, whole, w_in, bias_pair.astype(jnp.float32), position, w_out)


def attention_back_kernel(
    scaling, grad_ref, out_w_ref, probs_ref, query_u_ref, query_v_ref, key_ref, value_ref,
    position_ref, d_projected_ref, d_position_ref, bias_ref, d_keys, d_values, d_places,
):
    block = pl.program_id(0)
    seq_len, local_width = key_ref.shape
    rows = grad_ref.shape[0]

    @pl.when(block == 0)
    def _():
        d_keys[...] = jnp.zeros_like(d_keys)
        d_values[...] = jnp.zeros_like(d_values)
        d_places[...] = jnp.zeros_like(d_places)
        bias_ref[...] = jnp.zeros_like(bias_ref)

    here = pl.ds(pl.multiple_of(block * rows, rows), rows)
    nearby = place_position(position_ref, block, rows, seq_len)
    d_nearby = place_position(d_places, block, rows, seq_len)
    upside = (
        lax.broadcasted_iota(jnp.int32, (rows, rows), 0)
        + lax.broadcasted_iota(jnp.int32, (rows, rows), 1)
        == rows - 1
    ).astype(jnp.bfloat16)
    d_context_all = contract_cols(grad_ref[...], out_w_ref[...]).astype(jnp.bfloat16)
    for head in range(local_width // HEAD):
        lanes = slice(head * HEAD, (head + 1) * HEAD)
        d_context = d_context_all[:, lanes]
        probs = probs_ref[head]
        d_probs = contract_cols(d_context, value_ref[:, lanes])
        inner = jnp.sum(probs * d_probs, axis=-1, keepdims=True)
        d_scores = (probs * (d_probs - inner)).astype(jnp.bfloat16)
        d_values[:, lanes] += contract_rows(probs.astype(jnp.bfloat16), d_context)
        d_keys[:, lanes] += contract_rows(d_scores, query_u_ref[here, lanes])
        grad_u = matmul(d_scores, key_ref[:, lanes]) * scaling
        turned = matmul(upside, d_scores)
        turned = jnp.concatenate([turned, jnp.zeros((rows, rows), jnp.float32)], axis=1)
        turned = pltpu.roll(turned, 0, 1, stride=1, stride_axis=0).astype(jnp.bfloat16)
        d_zeds = matmul(upside, turned).astype(jnp.bfloat16)
        grad_v = matmul(d_zeds, nearby[:, lanes]) * scaling
        d_nearby[:, lanes] += contract_rows(d_zeds, query_v_ref[here, lanes])
        d_projected_ref[here, lanes] = (grad_u + grad_v).astype(jnp.bfloat16)
        bias_ref[0:1, lanes] += jnp.sum(grad_u, axis=0, keepdims=True)
        bias_ref[1:2, lanes] += jnp.sum(grad_v, axis=0, keepdims=True)

    @pl.when(block == pl.num_programs(0) - 1)
    def _():
        d_projected_ref[:, local_width : 2 * local_width] = d_keys[...].astype(jnp.bfloat16)
        d_projected_ref[:, 2 * local_width :] = d_values[...].astype(jnp.bfloat16)
        d_position_ref[...] = d_places[...].astype(jnp.bfloat16)


def attention_backward(whole, weights, table_low, position, saved, grad_whole):
    w_in, w_pos, bias_pair, w_out = weights
    probs, context, query_u, query_v, key_rows, value_rows = saved
    seq_len, model_width = whole.shape
    local_width = w_out.shape[0]
    heads_here = local_width // HEAD
    rows = 128
    full = pl.BlockSpec(memory_space=pltpu.VMEM)
    d_projected, d_position, grad_bias = pl.pallas_call(
        functools.partial(attention_back_kernel, HEAD ** (-0.5)),
        grid=(seq_len // rows,),
        out_shape=[
            jax.ShapeDtypeStruct((seq_len, 3 * local_width), jnp.bfloat16),
            jax.ShapeDtypeStruct((2 * seq_len, local_width), jnp.bfloat16),
            jax.ShapeDtypeStruct((2, local_width), jnp.float32),
        ],
        in_specs=[
            pl.BlockSpec((rows, model_width), lambda block: (block, 0)),
            full,
            pl.BlockSpec((heads_here, rows, seq_len), lambda block: (0, block, 0)),
        ]
        + [full] * 5,
        out_specs=[full] * 3,
        scratch_shapes=[
            pltpu.VMEM((seq_len, local_width), jnp.float32),
            pltpu.VMEM((seq_len, local_width), jnp.float32),
            pltpu.VMEM((2 * seq_len, local_width), jnp.float32),
        ],
        compiler_params=pltpu.CompilerParams(vmem_limit_bytes=VMEM_LIMIT),
        name="attention_backward",
    )(grad_whole, w_out, probs, query_u, query_v, key_rows, value_rows, position)
    grad_in = contract_rows(whole, d_projected)
    d_normed = contract_cols(d_projected, w_in)
    grad_pos = contract_rows(table_low, d_position)
    grad_out = contract_rows(context, grad_whole)
    return (d_normed, grad_in, grad_pos, grad_bias, grad_out)


def conv_front(whole, w_in, kernel, mask_col):
    seq_len, model_width = whole.shape
    local_width = w_in.shape[2]
    glu_in = matmul(whole, w_in.reshape(model_width, 2 * local_width))
    gate_value = glu_in[:, :local_width]
    logistic = jax.nn.sigmoid(glu_in[:, local_width:])
    glu_out = gate_value * logistic * mask_col
    tap_count = kernel.shape[0]
    half_taps = (tap_count - 1) // 2
    padded = jnp.pad(glu_out, ((half_taps, half_taps), (0, 0)))
    kernel_float = kernel.astype(jnp.float32)
    conved = kernel_float[0] * padded[0:seq_len]
    for tap_index in range(1, tap_count):
        conved = conved + kernel_float[tap_index] * padded[tap_index : tap_index + seq_len]
    return (gate_value, logistic, padded, conved)


def batch_stats(conved, mask_col, frame_count):
    local_sum = jnp.sum(conved * mask_col, axis=0)
    local_squares = jnp.sum(conved * conved * mask_col, axis=0)
    total_sum, total_squares = dp_total(jnp.stack([local_sum, local_squares]))
    average = total_sum / frame_count
    variance = total_squares / frame_count - average * average
    return (average, lax.rsqrt(variance + batch_eps))


def conv_tail(conved, stats, bn_gain, bn_bias):
    average, inv_std = stats
    normed_b = (conved - average) * inv_std * bn_gain.astype(jnp.float32) + bn_bias.astype(
        jnp.float32
    )
    return (normed_b, jax.nn.silu(normed_b).astype(jnp.bfloat16))


def conv_backward(whole, weights, mask_col, stats, frame_count, grad_whole):
    w_in, kernel, bn_gain, bn_bias, w_out = weights
    seq_len, model_width = whole.shape
    local_width = w_in.shape[2]
    gate_value, logistic, padded, conved = conv_front(whole, w_in, kernel, mask_col)
    normed_b, active = conv_tail(conved, stats, bn_gain, bn_bias)
    average, inv_std = stats
    grad_out = contract_rows(active, grad_whole)
    d_normed = contract_cols(grad_whole, w_out) * silu_slope(normed_b)
    centred = (conved - average) * inv_std
    bias_total, gain_total = dp_total(
        jnp.stack([jnp.sum(d_normed, axis=0), jnp.sum(d_normed * centred, axis=0)])
    )
    d_conved = (
        bn_gain.astype(jnp.float32)
        * inv_std
        * (d_normed - mask_col * (bias_total + centred * gain_total) / frame_count)
    )
    tap_count = kernel.shape[0]
    half_taps = (tap_count - 1) // 2
    kernel_float = kernel.astype(jnp.float32)
    d_padded = jnp.pad(d_conved, ((half_taps, half_taps), (0, 0)))
    d_glu = kernel_float[0] * d_padded[tap_count - 1 : tap_count - 1 + seq_len]
    for tap_index in range(1, tap_count):
        d_glu = (
            d_glu
            + kernel_float[tap_index]
            * d_padded[tap_count - 1 - tap_index : tap_count - 1 - tap_index + seq_len]
        )
    grad_kernel = jnp.stack(
        [
            jnp.sum(d_conved * padded[tap_index : tap_index + seq_len], axis=0)
            for tap_index in range(tap_count)
        ]
    )
    d_glu = d_glu * mask_col
    d_pair = jnp.concatenate(
        [d_glu * logistic, d_glu * gate_value * logistic * (1.0 - logistic)], axis=1
    ).astype(jnp.bfloat16)
    grad_in = contract_rows(whole, d_pair).reshape(model_width, 2, local_width)
    d_normed_in = contract_cols(d_pair, w_in.reshape(model_width, 2 * local_width))
    return (d_normed_in, grad_in, grad_kernel, grad_out, gain_total, bias_total)


def body(
    frames_in,
    lengths,
    out_grad,
    norm_gains,
    ffn1_up,
    ffn1_down,
    attn_in,
    pos_proj,
    pos_bias,
    attn_out,
    conv_in,
    depthwise,
    bn_scale,
    bn_shift,
    conv_out,
    ffn2_up,
    ffn2_down,
):
    unused, local_rows, model_width = frames_in.shape
    seq_len = local_rows * lax.axis_size("mp")
    dp_index = lax.axis_index("dp")
    own_length = lax.dynamic_slice_in_dim(lengths, dp_index, 1)[0]
    valid_keys = jnp.arange(seq_len) < own_length
    mask_col = valid_keys.astype(jnp.float32)[:, None]
    frame_count = jnp.sum(lengths).astype(jnp.float32)
    layer_input = frames_in.reshape(local_rows, model_width).astype(jnp.float32)
    (up_one, down_one, pos_whole, attn_out_whole, conv_out_whole), small = fetch_now(
        [ffn1_up, ffn1_down, pos_proj, attn_out, conv_out],
        (0, 1, 0, 1, 1),
        jnp.concatenate([pos_bias, depthwise, bn_scale[None], bn_shift[None]], axis=0),
    )
    taps = depthwise.shape[0]
    ffn_first = (up_one, down_one)
    attn_held = (
        lax.all_gather(
            attn_in.reshape(attn_in.shape[0], -1), "dp", axis=0, tiled=True
        ),
        pos_whole,
        small[:2],
        attn_out_whole,
    )
    conv_held = (
        lax.all_gather(conv_in, "dp", axis=0, tiled=True),
        small[2 : 2 + taps],
        small[2 + taps],
        small[3 + taps],
        conv_out_whole,
    )
    ffn_second = (
        lax.all_gather(ffn2_up, "dp", axis=0, tiled=True),
        lax.all_gather(ffn2_down, "dp", axis=1, tiled=True),
    )
    whole_first = enter_block(layer_input, norm_gains[0])
    after_first = layer_input + 0.5 * branch_total(ffn_forward(whole_first, ffn_first))
    whole_attn = enter_block(after_first, norm_gains[1])
    table_low = position_table(seq_len, model_width).astype(jnp.bfloat16)
    position = matmul(table_low, pos_whole).astype(jnp.bfloat16)
    attn_partial, *attn_saved = attention_forward(
        whole_attn, attn_held, position, own_length[None]
    )
    after_attn = after_first + branch_total(attn_partial)
    whole_conv = enter_block(after_attn, norm_gains[2])
    gate_value, logistic, padded, conved = conv_front(
        whole_conv, conv_held[0], conv_held[1], mask_col
    )
    stats = batch_stats(conved, mask_col, frame_count)
    normed_b, active = conv_tail(conved, stats, conv_held[2], conv_held[3])
    after_conv = after_attn + branch_total(matmul(active, conv_held[4]))
    whole_second = enter_block(after_conv, norm_gains[3])
    after_second = after_conv + 0.5 * branch_total(ffn_forward(whole_second, ffn_second))
    block_out = layer_norm(after_second, norm_gains[4]).astype(jnp.bfloat16)
    d_second, gain_five = norm_back(
        after_second, norm_gains[4], out_grad.reshape(local_rows, model_width).astype(jnp.float32)
    )
    d_normed, grad_up_two, grad_down_two = ffn_backward(
        whole_second,
        ffn_second,
        spread_grads((0.5 * d_second).astype(jnp.bfloat16)),
    )
    d_branch, gain_four = norm_back(after_conv, norm_gains[3], input_total(d_normed))
    d_conv = d_second + d_branch
    d_normed, grad_conv_in, grad_kernel, grad_conv_out, gain_total, bias_total = conv_backward(
        whole_conv,
        conv_held,
        mask_col,
        stats,
        frame_count,
        spread_grads(d_conv.astype(jnp.bfloat16)),
    )
    d_branch, gain_three = norm_back(after_attn, norm_gains[2], input_total(d_normed))
    d_attn = d_conv + d_branch
    d_normed, grad_attn_in, grad_pos, grad_bias, grad_attn_out = attention_backward(
        whole_attn,
        attn_held,
        table_low,
        position,
        attn_saved,
        spread_grads(d_attn.astype(jnp.bfloat16)),
    )
    d_branch, gain_two = norm_back(after_first, norm_gains[1], input_total(d_normed))
    d_first = d_attn + d_branch
    d_normed, grad_up_one, grad_down_one = ffn_backward(
        whole_first,
        ffn_first,
        spread_grads((0.5 * d_first).astype(jnp.bfloat16)),
    )
    d_branch, gain_one = norm_back(layer_input, norm_gains[0], input_total(d_normed))
    in_grad = d_first + d_branch
    totals, small_grads, gain_sum = grad_totals(
        [
            grad_up_two,
            grad_down_two,
            grad_conv_in.reshape(model_width, -1),
            grad_conv_out,
            grad_attn_in,
            grad_attn_out,
            grad_pos,
            grad_up_one,
            grad_down_one,
        ],
        (0, 1, 0, 1, 0, 1, 0, 0, 1),
        (False, True, True, True, False, True, False, False, True),
        jnp.concatenate([grad_bias, grad_kernel], axis=0),
        jnp.stack([gain_one, gain_two, gain_three, gain_four, gain_five]),
    )
    block = model_width // lax.axis_size("dp")
    summed = (
        totals[7],
        totals[8],
        totals[4].reshape(block, 3, -1),
        totals[6],
        small_grads[:2],
        totals[5],
        totals[2].reshape(block, 2, -1),
        small_grads[2:],
        totals[3],
        totals[0],
        totals[1],
    )
    piece_len = bn_scale.shape[0]
    grad_scale = lax.dynamic_slice_in_dim(gain_total, dp_index * piece_len, piece_len)
    grad_shift = lax.dynamic_slice_in_dim(bias_total, dp_index * piece_len, piece_len)
    return (
        block_out.reshape(1, local_rows, model_width),
        in_grad.reshape(1, local_rows, model_width),
        gain_sum,
        summed[0],
        summed[1],
        summed[2],
        summed[3],
        summed[4],
        summed[5],
        summed[6],
        summed[7],
        grad_scale,
        grad_shift,
        summed[8],
        summed[9],
        summed[10],
    )


def solution(mesh):
    placed = (
        P("dp", "mp", None),
        P(),
        P("dp", "mp", None),
        P(),
        P("dp", "mp"),
        P("mp", "dp"),
        P("dp", None, "mp"),
        P("dp", "mp"),
        P(None, ("mp", "dp")),
        P("mp", "dp"),
        P("dp", None, "mp"),
        P(None, ("mp", "dp")),
        P(("mp", "dp")),
        P(("mp", "dp")),
        P("mp", "dp"),
        P("dp", "mp"),
        P("mp", "dp"),
    )
    return jax.shard_map(
        body,
        mesh=mesh,
        in_specs=placed,
        out_specs=(
            P("dp", "mp", None),
            P("dp", "mp", None),
            P(),
            P("dp", "mp"),
            P("mp", "dp"),
            P("dp", None, "mp"),
            P("dp", "mp"),
            P(None, ("mp", "dp")),
            P("mp", "dp"),
            P("dp", None, "mp"),
            P(None, ("mp", "dp")),
            P(("mp", "dp")),
            P(("mp", "dp")),
            P("mp", "dp"),
            P("dp", "mp"),
            P("mp", "dp"),
        ),
        check_vma=False,
    )
```

```python
import functools
import math

import jax
import jax.numpy as jnp
from jax import lax
from jax.experimental import pallas as pl
from jax.experimental.pallas import tpu as pltpu
from jax.sharding import PartitionSpec as P

HEAD = 128


norm_eps = 1e-05
batch_eps = 1e-05
masked_score = -1000000000.0


def matmul(left, right):
    return jnp.dot(left, right, preferred_element_type=jnp.float32)


def contract_rows(left, right):
    return lax.dot_general(
        left, right, (((0,), (0,)), ((), ())), preferred_element_type=jnp.float32
    )


def contract_cols(left, right):
    return lax.dot_general(
        left, right, (((1,), (1,)), ((), ())), preferred_element_type=jnp.float32
    )


def layer_norm(values, norm_gain):
    average = jnp.mean(values, axis=-1, keepdims=True)
    centred = values - average
    inv_std = lax.rsqrt(jnp.mean(centred * centred, axis=-1, keepdims=True) + norm_eps)
    return centred * inv_std * norm_gain


def silu_slope(values):
    logistic = jax.nn.sigmoid(values)
    return logistic * (1.0 + values * (1.0 - logistic))


def position_table(seq_len, model_width):
    fine = 32
    lane = jnp.arange(model_width)
    frequency = jnp.exp((lane // 2).astype(jnp.float32) * (-2.0 * math.log(10000.0) / model_width))
    coarse = (seq_len - 1 - fine * jnp.arange(2 * seq_len // fine)).astype(jnp.float32)
    wide = coarse[:, None] * frequency[None, :]
    small = -jnp.arange(fine).astype(jnp.float32)[:, None] * frequency[None, :]
    even = (lane % 2 == 0)[None, :]
    wide_sin, wide_cos = jnp.sin(wide), jnp.cos(wide)
    high = jnp.where(even, wide_sin, wide_cos)
    side = jnp.where(even, wide_cos, -wide_sin)
    table = high[:, None, :] * jnp.cos(small)[None] + side[:, None, :] * jnp.sin(small)[None]
    return table.reshape(2 * seq_len, model_width)


MESH = pl.DeviceIdType.MESH
VMEM_LIMIT = 60 * 1024 * 1024


def line_copy(src, dst, sems, index, axis, target):
    return pltpu.make_async_remote_copy(
        src_ref=src,
        dst_ref=dst,
        send_sem=sems.at[0, index],
        recv_sem=sems.at[1, index],
        device_id={axis: target},
        device_id_type=MESH,
    )


def bit_of(index, bit):
    return lax.rem(lax.div(index, bit), 2)


def partner(index, bit):
    return index + bit - 2 * bit * bit_of(index, bit)


def cube_bits(size, swap):
    bits = []
    bit = 2
    while bit < size:
        bits.append(bit)
        bit *= 2
    if swap:
        bits.reverse()
    return bits + [1]


def block_at(ref, dim, index, width):
    start = pl.multiple_of(index * width, width)
    return ref.at[pl.ds(start, width)] if dim == 0 else ref.at[:, pl.ds(start, width)]


def all_total_kernel(axis, in_ref, out_ref, slots, sems):
    size = lax.axis_size(axis)
    me = lax.axis_index(axis)
    barrier = pltpu.get_barrier_semaphore()
    targets = [lax.rem(me + step, size) for step in range(1, size)]
    for target in targets:
        pl.semaphore_signal(barrier, inc=1, device_id={axis: target}, device_id_type=MESH)
    pl.semaphore_wait(barrier, size - 1)
    copies = []
    for number, target in enumerate(targets):
        copy = line_copy(in_ref, slots.at[me], sems, number, axis, target)
        copy.start()
        copies.append(copy)
    slots[me] = in_ref[...]
    for copy in copies:
        copy.wait_recv()
    total = slots[0]
    for source in range(1, size):
        total = total + slots[source]
    out_ref[...] = total
    for copy in copies:
        copy.wait_send()


def all_total(values, axis, collective_id):
    size = lax.axis_size(axis)
    return pl.pallas_call(
        functools.partial(all_total_kernel, axis),
        out_shape=jax.ShapeDtypeStruct(values.shape, values.dtype),
        in_specs=[pl.BlockSpec(memory_space=pltpu.VMEM)],
        out_specs=pl.BlockSpec(memory_space=pltpu.VMEM),
        scratch_shapes=[
            pltpu.VMEM((size, *values.shape), values.dtype),
            pltpu.SemaphoreType.DMA((2, size - 1)),
        ],
        compiler_params=pltpu.CompilerParams(
            collective_id=collective_id, has_side_effects=True
        ),
        name="all_total",
    )(values)


def line_peers(axis):
    me, size = lax.axis_index(axis), lax.axis_size(axis)
    return jnp.minimum(me, 1) + jnp.minimum(size - 1 - me, 1)


def greet(line_axis, cube_axis, everyone):
    me, size = lax.axis_index(line_axis), lax.axis_size(line_axis)
    barrier = pltpu.get_barrier_semaphore()
    if everyone:
        for axis in (line_axis, cube_axis):
            here, count = lax.axis_index(axis), lax.axis_size(axis)
            for step in range(1, count):
                pl.semaphore_signal(
                    barrier, inc=1, device_id={axis: lax.rem(here + step, count)},
                    device_id_type=MESH,
                )
        pl.semaphore_wait(barrier, size - 1 + lax.axis_size(cube_axis) - 1)
        return

    @pl.when(me > 0)
    def _():
        pl.semaphore_signal(barrier, inc=1, device_id={line_axis: me - 1}, device_id_type=MESH)

    @pl.when(me < size - 1)
    def _():
        pl.semaphore_signal(barrier, inc=1, device_id={line_axis: me + 1}, device_id_type=MESH)

    bits = cube_bits(lax.axis_size(cube_axis), False) if cube_axis else []
    for bit in bits:
        pl.semaphore_signal(
            barrier, inc=1, device_id={cube_axis: partner(lax.axis_index(cube_axis), bit)},
            device_id_type=MESH,
        )
    pl.semaphore_wait(barrier, line_peers(line_axis) + len(bits))


class LineGather:
    def __init__(self, axis, out_ref, sems):
        self.axis, self.out, self.sems = axis, out_ref, sems
        self.size, self.me = lax.axis_size(axis), lax.axis_index(axis)
        self.rows = out_ref.shape[0] // self.size
        self.steps = self.size - 1

    def piece(self, index):
        return self.out.at[pl.ds(pl.multiple_of(index * self.rows, self.rows), self.rows)]

    def copy(self, way, step, index):
        return line_copy(
            self.piece(index), self.piece(index), self.sems, way * self.steps + step, self.axis,
            self.me + 1 if way == 0 else self.me - 1,
        )

    def index(self, way, step):
        return self.me - step if way == 0 else self.me + step

    def held(self, way, step):
        return self.me >= step if way == 0 else self.me + step < self.size

    def onward(self, way):
        return self.me + 1 < self.size if way == 0 else self.me > 0

    def step(self, step):
        for way in range(2):
            if step > 0:
                @pl.when(self.held(way, step))
                def _():
                    self.copy(way, step - 1, self.index(way, step)).wait_recv()

            if step < self.steps:
                @pl.when(jnp.logical_and(self.held(way, step), self.onward(way)))
                def _():
                    self.copy(way, step, self.index(way, step)).start()

    def finish(self):
        for step in range(self.steps):
            for way in range(2):
                @pl.when(jnp.logical_and(self.held(way, step), self.onward(way)))
                def _():
                    self.copy(way, step, self.index(way, step)).wait_send()


class LineScatter:
    def __init__(self, axis, in_ref, total_ref, slots, staged, sems):
        self.axis, self.ins, self.total = axis, in_ref, total_ref
        self.slots, self.staged, self.sems = slots, staged, sems
        self.size, self.me = lax.axis_size(axis), lax.axis_index(axis)
        self.rows = total_ref.shape[0]
        self.first_way = lax.div(self.me, (self.size + 1) // 2)

    def mine(self, owner):
        return self.ins.at[pl.ds(pl.multiple_of(owner * self.rows, self.rows), self.rows)]

    def copy(self, way, owner, src):
        return line_copy(
            src, self.slots.at[way, owner], self.sems, way * self.size + owner, self.axis,
            self.me + 1 - 2 * way,
        )

    def hop(self, way, step):
        owner = (1 - way) * (self.size - 1 - step) + way * step
        distance = (owner - self.me) * (1 - 2 * way)
        behind = (1 - way) * self.me + way * (self.size - 1 - self.me)

        @pl.when(jnp.logical_and(distance > 0, behind == 0))
        def _():
            self.copy(way, owner, self.mine(owner)).start()

        @pl.when(jnp.logical_and(distance > 0, behind > 0))
        def _():
            self.copy(way, owner, self.staged.at[way, owner]).wait_recv()
            self.staged[way, owner] = (
                self.mine(owner)[...].astype(jnp.float32)
                + self.slots[way, owner].astype(jnp.float32)
            ).astype(self.staged.dtype)
            self.copy(way, owner, self.staged.at[way, owner]).start()

    def step(self, step):
        self.hop(self.first_way, step)
        self.hop(1 - self.first_way, step)

    def result(self):
        self.total[...] = self.mine(self.me)[...].astype(jnp.float32)
        for way in range(2):
            @pl.when(self.me > 0 if way == 0 else self.me < self.size - 1)
            def _():
                self.copy(way, self.me, self.staged.at[way, self.me]).wait_recv()
                self.total[...] += self.slots[way, self.me].astype(jnp.float32)

        return self.total[...]

    def finish(self):
        for owner in range(self.size):
            for way in range(2):
                @pl.when(self.me < owner if way == 0 else self.me > owner)
                def _():
                    self.copy(way, owner, self.staged.at[way, owner]).wait_send()


class CubeGather:
    def __init__(self, axis, dims, ways, ins, outs, sems):
        self.axis, self.dims, self.ways = axis, dims, ways
        self.ins, self.outs, self.sems = ins, outs, sems
        self.size, self.me = lax.axis_size(axis), lax.axis_index(axis)
        self.stages = len(cube_bits(self.size, False))
        self.started = []
        self.waiting = [[] for _ in ins]

    def step(self, stage):
        per = self.size - 1
        for which in range(len(self.ins)):
            width = self.ins[which].shape[self.dims[which]]
            bits = cube_bits(self.size, self.ways[which])
            for copy in self.waiting[which]:
                copy.wait_recv()
            self.waiting[which] = []
            if stage == 0:
                block_at(self.outs[which], self.dims[which], self.me, width)[...] = (
                    self.ins[which][...]
                )
            if stage == self.stages:
                continue
            held = [self.me]
            for bit in bits[:stage]:
                held = held + [partner(index, bit) for index in held]
            for number, index in enumerate(held):
                place = block_at(self.outs[which], self.dims[which], index, width)
                copy = line_copy(
                    self.ins[which] if stage == 0 else place, place, self.sems,
                    which * per + 2**stage - 1 + number, self.axis, partner(self.me, bits[stage]),
                )
                copy.start()
                self.waiting[which].append(copy)
            self.started.extend(self.waiting[which])

    def finish(self):
        for copy in self.started:
            copy.wait_send()


class CubeScatter:
    def __init__(self, axis, dims, ways, ins, outs, slots, sems):
        self.axis, self.dims, self.ways = axis, dims, ways
        self.ins, self.outs, self.slots, self.sems = ins, outs, slots, sems
        self.size, self.me = lax.axis_size(axis), lax.axis_index(axis)
        self.stages = len(cube_bits(self.size, False))
        self.started = []

    def slot(self, which, stage, number):
        return self.slots[which].at[self.size - self.size // 2**stage + number]

    def sets(self, which, stage):
        bits = cube_bits(self.size, self.ways[which])[::-1]
        held = [self.me]
        for bit in bits[stage + 1 :]:
            held = held + [partner(index, bit) for index in held]
        return bits[stage], held

    def send(self, which, stage):
        width = self.outs[which].shape[self.dims[which]]
        bit, held = self.sets(which, stage)
        for number, index in enumerate(held):
            if stage == 0:
                src = block_at(self.ins[which], self.dims[which], partner(index, bit), width)
            else:
                src = self.slot(which, stage - 1, 2 * number + 1)
            copy = line_copy(
                src, self.slot(which, stage, number), self.sems,
                which * (self.size - 1) + self.size - self.size // 2**stage + number,
                self.axis, partner(self.me, bit),
            )
            copy.start()
            self.started.append((which, stage, copy))

    def receive(self, which, stage):
        width = self.outs[which].shape[self.dims[which]]
        _, held = self.sets(which, stage)
        for copy in [c for w, s, c in self.started if (w, s) == (which, stage)]:
            copy.wait_recv()
        for number, index in enumerate(held):
            got = self.slot(which, stage, number)
            if stage == 0:
                mine = block_at(self.ins[which], self.dims[which], index, width)
            else:
                mine = self.slot(which, stage - 1, 2 * number)
            total = got[...].astype(jnp.float32) + mine[...].astype(jnp.float32)
            if stage == self.stages - 1:
                self.outs[which][...] = total
            else:
                got[...] = total.astype(self.slots[which].dtype)

    def step(self, stage):
        for which in range(len(self.ins)):
            if stage > 0:
                self.receive(which, stage - 1)
            if stage < self.stages:
                self.send(which, stage)

    def finish(self):
        for _, _, copy in self.started:
            copy.wait_send()


class AllTotal:
    def __init__(self, axis, slots, sems):
        self.axis, self.slots, self.sems = axis, slots, sems
        self.size, self.me = lax.axis_size(axis), lax.axis_index(axis)
        self.copies = []

    def start(self):
        for step in range(1, self.size):
            copy = line_copy(
                self.slots.at[self.me], self.slots.at[self.me], self.sems, step - 1, self.axis,
                lax.rem(self.me + step, self.size),
            )
            copy.start()
            self.copies.append(copy)

    def result(self):
        for copy in self.copies:
            copy.wait_recv()
        total = self.slots[0]
        for source in range(1, self.size):
            total = total + self.slots[source]
        return total

    def finish(self):
        for copy in self.copies:
            copy.wait_send()


def open_kernel(middle, counts, dims, ways, *refs):
    local_count, mid_count = counts
    count = len(dims)
    refs = list(refs)
    take = lambda number: [refs.pop(0) for _ in range(number)]
    locals_, ins = take(local_count), take(count)
    mids, (whole,), outs = take(mid_count), take(1), take(count)
    gather_sems, cube_sems = refs
    fetch = CubeGather("dp", dims, ways, ins, outs, cube_sems)
    rows = LineGather("mp", whole, gather_sems)
    greet("mp", "dp", False)
    fetch.step(0)
    values, normed = middle(None, *[ref[...] for ref in locals_])
    for ref, value in zip(mids, values):
        ref[...] = value
    rows.piece(rows.me)[...] = normed
    rows.step(0)
    fetch.step(1)
    rows.step(1)
    fetch.step(2)
    for step in range(3, fetch.stages + 1):
        fetch.step(step)
        if step <= rows.steps + 1:
            rows.step(step - 1)
    for step in range(max(2, fetch.stages), rows.steps + 1):
        rows.step(step)
    rows.finish()
    fetch.finish()


def between_kernel(middle, counts, gathers, dims, ways, *refs):
    local_count, mid_count = counts
    count = len(dims)
    refs = list(refs)
    take = lambda number: [refs.pop(0) for _ in range(number)]
    (partial,), locals_, ins = take(1), take(local_count), take(count)
    mids, (whole,), outs = take(mid_count), take(1), take(count)
    (total, slots, staged, scatter_sems, gather_sems), refs = refs[:5], refs[5:]
    sums = LineScatter("mp", partial, total, slots, staged, scatter_sems)
    rows = LineGather("mp", whole, gather_sems)
    grads = CubeScatter("dp", dims, ways, ins, outs, refs[:count], refs[count]) if count else None
    greet("mp", "dp" if count else None, False)
    stage = 0
    for step in range(sums.size - 1):
        sums.step(step)
        if count and step in (0, 2):
            grads.step(stage)
            stage += 1
    values, normed = middle(sums.result(), *[ref[...] for ref in locals_])
    rows.piece(rows.me)[...] = normed
    rows.step(0)
    for ref, value in zip(mids, values):
        ref[...] = value
    for step in range(1, rows.steps + 1):
        if count and stage <= grads.stages:
            grads.step(stage)
            stage += 1
        rows.step(step)
    if count:
        for stage in range(stage, grads.stages + 1):
            grads.step(stage)
        grads.finish()
    sums.finish()
    rows.finish()


def close_kernel(middle, counts, dims, ways, *refs):
    local_count, mid_count = counts
    count = len(dims)
    refs = list(refs)
    take = lambda number: [refs.pop(0) for _ in range(number)]
    (partial, small, gains), locals_, ins = take(3), take(local_count), take(count)
    mids, (small_out, gains_out), outs = take(mid_count), take(2), take(count)
    (total, slots, staged, scatter_sems), refs = refs[:4], refs[4:]
    (small_slots, small_sems, gain_slots, gain_sems, last_slots, last_sems), refs = refs[:6], refs[6:]
    sums = LineScatter("mp", partial, total, slots, staged, scatter_sems)
    grads = CubeScatter("dp", dims, ways, ins, outs, refs[:count], refs[count])
    little = AllTotal("dp", small_slots, small_sems)
    near, far = AllTotal("dp", gain_slots, gain_sems), AllTotal("mp", last_slots, last_sems)
    little.slots[little.me] = small[...]
    greet("mp", "dp", True)
    little.start()
    stage = 0
    for step in range(sums.size - 1):
        sums.step(step)
        if step != 1:
            grads.step(stage)
            stage += 1
    values, gain = middle(sums.result(), *[ref[...] for ref in locals_])
    near.slots[near.me] = jnp.concatenate([gains[...], gain], axis=0)
    near.start()
    for ref, value in zip(mids, values):
        ref[...] = value
    grads.step(stage)
    far.slots[far.me] = near.result()
    far.start()
    for stage in range(stage + 1, grads.stages + 1):
        grads.step(stage)
    small_out[...] = little.result()
    gains_out[...] = far.result()
    for task in (grads, sums, little, near, far):
        task.finish()


def shapes_of(arrays):
    return [jax.ShapeDtypeStruct(value.shape, value.dtype) for value in arrays]


def call_step(kernel, inputs, out_shape, scratch, collective_id, name):
    vmem = pl.BlockSpec(memory_space=pltpu.VMEM)
    return pl.pallas_call(
        kernel,
        out_shape=out_shape,
        in_specs=[vmem] * len(inputs),
        out_specs=[vmem] * len(out_shape),
        scratch_shapes=scratch,
        compiler_params=pltpu.CompilerParams(
            collective_id=collective_id, has_side_effects=True, vmem_limit_bytes=VMEM_LIMIT
        ),
        name=name,
    )(*inputs)


def line_scratch(rows, width):
    size = lax.axis_size("mp")
    return [
        pltpu.VMEM((rows, width), jnp.float32),
        pltpu.VMEM((2, size, rows, width), jnp.bfloat16),
        pltpu.VMEM((2, size, rows, width), jnp.bfloat16),
        pltpu.SemaphoreType.DMA((2, 2 * size)),
    ]


def cube_scratch(arrays, dims):
    size = lax.axis_size("dp")
    shapes, slots = [], []
    for array, dim in zip(arrays, dims):
        shape = list(array.shape)
        shape[dim] //= size
        shapes.append(jax.ShapeDtypeStruct(tuple(shape), jnp.float32))
        slots.append(pltpu.VMEM((size - 1, *shape), array.dtype))
    if arrays:
        slots.append(pltpu.SemaphoreType.DMA((2, len(arrays) * (size - 1))))
    return shapes, slots


def plain_totals(grads, dims):
    return [
        lax.psum_scatter(grad, "dp", scatter_dimension=dim, tiled=True).astype(jnp.float32)
        for grad, dim in zip(grads, dims)
    ]


def direct(block):
    size = lax.axis_size("dp")
    return size & (size - 1) == 0 and block % 128 == 0


def open_step(middle, locals_, arrays, dims, small, collective_id):
    if not direct(arrays[0].shape[dims[0]]):
        mids, normed = middle(None, *locals_)
        whole = [
            lax.all_gather(array, "dp", axis=dim, tiled=True) for array, dim in zip(arrays, dims)
        ]
        return (
            mids,
            lax.all_gather(normed, "mp", axis=0, tiled=True),
            whole,
            lax.all_gather(small, "dp", axis=1, tiled=True),
        )
    size, lanes = lax.axis_size("dp"), small.shape[1]
    arrays = [*arrays, jnp.pad(small, ((0, 16 - small.shape[0]), (0, 128 - lanes)))]
    dims = (*dims, 0)
    ways = [index % 2 == 1 for index in range(len(dims))]
    mid_shapes, normed_shape = jax.eval_shape(functools.partial(middle, None), *locals_)
    outs = []
    for array, dim in zip(arrays, dims):
        shape = list(array.shape)
        shape[dim] *= size
        outs.append(jax.ShapeDtypeStruct(tuple(shape), array.dtype))
    rows, width = normed_shape.shape
    whole_shape = jax.ShapeDtypeStruct((rows * lax.axis_size("mp"), width), normed_shape.dtype)
    result = call_step(
        functools.partial(open_kernel, middle, (len(locals_), len(mid_shapes)), dims, ways),
        [*locals_, *arrays],
        [*mid_shapes, whole_shape, *outs],
        [
            pltpu.SemaphoreType.DMA((2, 2 * (lax.axis_size("mp") - 1))),
            pltpu.SemaphoreType.DMA((2, len(arrays) * (size - 1))),
        ],
        collective_id,
        "open_step",
    )
    mids, (whole, *fetched, packed) = result[: len(mid_shapes)], result[len(mid_shapes) :]
    packed = packed.reshape(size, 16, 128)[:, : small.shape[0], :lanes]
    return mids, whole, fetched, packed.transpose(1, 0, 2).reshape(small.shape[0], size * lanes)


def between_step(middle, partial_value, locals_, grads, dims, ways, collective_id):
    partial_value = partial_value.astype(jnp.bfloat16)
    grads = [grad.astype(jnp.bfloat16) for grad in grads]
    size = lax.axis_size("mp")
    rows, width = partial_value.shape[0] // size, partial_value.shape[1]
    if not direct(width // lax.axis_size("dp")):
        total = lax.psum_scatter(partial_value, "mp", scatter_dimension=0, tiled=True)
        mids, normed = middle(total.astype(jnp.float32), *locals_)
        return mids, lax.all_gather(normed, "mp", axis=0, tiled=True), plain_totals(grads, dims)
    total = jax.ShapeDtypeStruct((rows, width), jnp.float32)
    mid_shapes, normed_shape = jax.eval_shape(middle, total, *locals_)
    shapes, slots = cube_scratch(grads, dims)
    count = len(mid_shapes)
    result = call_step(
        functools.partial(between_kernel, middle, (len(locals_), count), True, dims, ways),
        [partial_value, *locals_, *grads],
        [
            *mid_shapes,
            jax.ShapeDtypeStruct((rows * size, width), normed_shape.dtype),
            *shapes,
        ],
        line_scratch(rows, width) + [pltpu.SemaphoreType.DMA((2, 2 * (size - 1)))] + slots,
        collective_id,
        "between_step",
    )
    return result[:count], result[count], result[count + 1 :]


def close_step(middle, partial_value, small, gains, locals_, grads, dims, ways, collective_id):
    partial_value = partial_value.astype(jnp.bfloat16)
    grads = [grad.astype(jnp.bfloat16) for grad in grads]
    size, dp_size = lax.axis_size("mp"), lax.axis_size("dp")
    rows, width = partial_value.shape[0] // size, partial_value.shape[1]
    if not direct(width // dp_size):
        total = lax.psum_scatter(partial_value, "mp", scatter_dimension=0, tiled=True)
        mids, gain = middle(total.astype(jnp.float32), *locals_)
        gains = lax.psum(jnp.concatenate([gains, gain], axis=0), ("dp", "mp"))
        return mids, lax.psum(small, "dp"), gains, plain_totals(grads, dims)
    total = jax.ShapeDtypeStruct((rows, width), jnp.float32)
    mid_shapes, gain_shape = jax.eval_shape(middle, total, *locals_)
    gains_shape = jax.ShapeDtypeStruct((gains.shape[0] + 1, width), jnp.float32)
    shapes, slots = cube_scratch(grads, dims)
    count = len(mid_shapes)
    result = call_step(
        functools.partial(close_kernel, middle, (len(locals_), count), dims, ways),
        [partial_value, small, gains, *locals_, *grads],
        [*mid_shapes, *shapes_of([small]), gains_shape, *shapes],
        line_scratch(rows, width)
        + [
            pltpu.VMEM((dp_size, *small.shape), jnp.float32),
            pltpu.SemaphoreType.DMA((2, dp_size - 1)),
            pltpu.VMEM((dp_size, *gains_shape.shape), jnp.float32),
            pltpu.SemaphoreType.DMA((2, dp_size - 1)),
            pltpu.VMEM((size, *gains_shape.shape), jnp.float32),
            pltpu.SemaphoreType.DMA((2, size - 1)),
        ]
        + slots,
        collective_id,
        "close_step",
    )
    return result[:count], result[count], result[count + 1], result[count + 2 :]


def forward_middle(scale, row, total, residual, norm_gains):
    residual = residual.astype(jnp.float32)
    if total is not None:
        residual = residual + scale * total
    return [residual], layer_norm(residual, norm_gains[row : row + 1]).astype(jnp.bfloat16)


def open_middle(total, frames, norm_gains):
    return [], layer_norm(frames.astype(jnp.float32), norm_gains[0:1]).astype(jnp.bfloat16)


def norm_back(values, norm_gain, upstream):
    centred = values - jnp.mean(values, axis=-1, keepdims=True)
    inv_std = lax.rsqrt(jnp.mean(centred * centred, axis=-1, keepdims=True) + norm_eps)
    normed = centred * inv_std
    scaled = upstream * norm_gain
    d_values = inv_std * (
        scaled
        - jnp.mean(scaled, axis=-1, keepdims=True)
        - normed * jnp.mean(scaled * normed, axis=-1, keepdims=True)
    )
    return d_values, jnp.sum(upstream * normed, axis=0, keepdims=True)


def turn_middle(total, residual, norm_gains, out_grad):
    after = residual + 0.5 * total
    gain = norm_gains[4:5]
    d_after, d_gain = norm_back(after, gain, out_grad.astype(jnp.float32))
    block_out = layer_norm(after, gain).astype(jnp.bfloat16)
    return [block_out, d_after, d_gain], (0.5 * d_after).astype(jnp.bfloat16)


def backward_middle(scale, row, total, values, norm_gains, upstream):
    d_branch, d_gain = norm_back(values.astype(jnp.float32), norm_gains[row : row + 1], total)
    d_values = upstream + d_branch
    return [d_values, d_gain], (scale * d_values).astype(jnp.bfloat16)


def close_middle(total, values, norm_gains, upstream):
    d_branch, d_gain = norm_back(values.astype(jnp.float32), norm_gains[0:1], total)
    return [upstream + d_branch], d_gain


def dp_total(values):
    if direct(128):
        return all_total(values, "dp", 9)
    return lax.psum(values, "dp")


def ffn_forward(whole, weights):
    w_up, w_down = weights
    hidden = matmul(whole, w_up)
    return matmul(jax.nn.silu(hidden).astype(jnp.bfloat16), w_down)


def ffn_backward(whole, weights, grad_whole):
    w_up, w_down = weights
    hidden = matmul(whole, w_up)
    active = jax.nn.silu(hidden).astype(jnp.bfloat16)
    grad_down = contract_rows(active, grad_whole)
    d_hidden = (contract_cols(grad_whole, w_down) * silu_slope(hidden)).astype(jnp.bfloat16)
    grad_up = contract_rows(whole, d_hidden)
    return (contract_cols(d_hidden, w_up), grad_up, grad_down)


def place_position(position_ref, block, rows, seq_len):
    start = pl.multiple_of(seq_len - rows - block * rows, rows)
    return position_ref.at[pl.ds(start, seq_len + rows)]


def attention_kernel(
    scaling, length_ref, whole_ref, in_ref, bias_ref, position_ref, out_w_ref,
    partial_ref, probs_ref, context_ref, query_u_ref, query_v_ref, key_ref, value_ref,
):
    block = pl.program_id(0)
    seq_len, local_width = key_ref.shape
    rows = partial_ref.shape[0]

    @pl.when(block == 0)
    def _():
        projected = matmul(whole_ref[...], in_ref[...])
        queries = projected[:, :local_width]
        query_u_ref[...] = ((queries + bias_ref[0:1]) * scaling).astype(jnp.bfloat16)
        query_v_ref[...] = ((queries + bias_ref[1:2]) * scaling).astype(jnp.bfloat16)
        key_ref[...] = projected[:, local_width : 2 * local_width].astype(jnp.bfloat16)
        value_ref[...] = projected[:, 2 * local_width :].astype(jnp.bfloat16)

    here = pl.ds(pl.multiple_of(block * rows, rows), rows)
    valid = lax.broadcasted_iota(jnp.int32, (rows, seq_len), 1) < length_ref[0]
    nearby = place_position(position_ref, block, rows, seq_len)
    pieces = []
    for head in range(local_width // HEAD):
        lanes = slice(head * HEAD, (head + 1) * HEAD)
        content = contract_cols(query_u_ref[here, lanes], key_ref[:, lanes])
        zeds = contract_cols(query_v_ref[here, lanes], nearby[:, lanes])
        shifted = pltpu.roll(zeds, seq_len + 1, 1, stride=1, stride_axis=0)[:, :seq_len]
        scores = jnp.where(valid, content + shifted, masked_score)
        exponent = jnp.exp(scores - jnp.max(scores, axis=-1, keepdims=True))
        probs = exponent / jnp.sum(exponent, axis=-1, keepdims=True)
        probs_ref[head] = probs
        pieces.append(matmul(probs.astype(jnp.bfloat16), value_ref[:, lanes]).astype(jnp.bfloat16))
    context = jnp.concatenate(pieces, axis=1)
    context_ref[...] = context
    partial_ref[...] = matmul(context, out_w_ref[...]).astype(jnp.bfloat16)


def attention_forward(whole, weights, position, own_length):
    w_in, w_pos, bias_pair, w_out = weights
    seq_len, model_width = whole.shape
    local_width = w_out.shape[0]
    heads_here = local_width // HEAD
    rows = 128
    full = pl.BlockSpec(memory_space=pltpu.VMEM)
    low = jnp.bfloat16
    return pl.pallas_call(
        functools.partial(attention_kernel, HEAD ** (-0.5)),
        grid=(seq_len // rows,),
        out_shape=[
            jax.ShapeDtypeStruct((seq_len, model_width), low),
            jax.ShapeDtypeStruct((heads_here, seq_len, seq_len), jnp.float32),
        ]
        + [jax.ShapeDtypeStruct((seq_len, local_width), low)] * 5,
        in_specs=[pl.BlockSpec(memory_space=pltpu.SMEM)] + [full] * 5,
        out_specs=[
            pl.BlockSpec((rows, model_width), lambda block: (block, 0)),
            pl.BlockSpec((heads_here, rows, seq_len), lambda block: (0, block, 0)),
            pl.BlockSpec((rows, local_width), lambda block: (block, 0)),
        ]
        + [full] * 4,
        compiler_params=pltpu.CompilerParams(vmem_limit_bytes=VMEM_LIMIT),
        name="attention_forward",
    )(own_length, whole, w_in, bias_pair.astype(jnp.float32), position, w_out)


def attention_back_kernel(
    scaling, grad_ref, out_w_ref, probs_ref, query_u_ref, query_v_ref, key_ref, value_ref,
    position_ref, d_projected_ref, d_position_ref, bias_ref, d_keys, d_values, d_places,
):
    block = pl.program_id(0)
    seq_len, local_width = key_ref.shape
    rows = grad_ref.shape[0]

    @pl.when(block == 0)
    def _():
        d_keys[...] = jnp.zeros_like(d_keys)
        d_values[...] = jnp.zeros_like(d_values)
        d_places[...] = jnp.zeros_like(d_places)
        bias_ref[...] = jnp.zeros_like(bias_ref)

    here = pl.ds(pl.multiple_of(block * rows, rows), rows)
    nearby = place_position(position_ref, block, rows, seq_len)
    d_nearby = place_position(d_places, block, rows, seq_len)
    upside = (
        lax.broadcasted_iota(jnp.int32, (rows, rows), 0)
        + lax.broadcasted_iota(jnp.int32, (rows, rows), 1)
        == rows - 1
    ).astype(jnp.bfloat16)
    d_context_all = contract_cols(grad_ref[...], out_w_ref[...]).astype(jnp.bfloat16)
    for head in range(local_width // HEAD):
        lanes = slice(head * HEAD, (head + 1) * HEAD)
        d_context = d_context_all[:, lanes]
        probs = probs_ref[head]
        d_probs = contract_cols(d_context, value_ref[:, lanes])
        inner = jnp.sum(probs * d_probs, axis=-1, keepdims=True)
        d_scores = (probs * (d_probs - inner)).astype(jnp.bfloat16)
        d_values[:, lanes] += contract_rows(probs.astype(jnp.bfloat16), d_context)
        d_keys[:, lanes] += contract_rows(d_scores, query_u_ref[here, lanes])
        grad_u = matmul(d_scores, key_ref[:, lanes]) * scaling
        turned = matmul(upside, d_scores)
        turned = jnp.concatenate([turned, jnp.zeros((rows, rows), jnp.float32)], axis=1)
        turned = pltpu.roll(turned, 0, 1, stride=1, stride_axis=0).astype(jnp.bfloat16)
        d_zeds = matmul(upside, turned).astype(jnp.bfloat16)
        grad_v = matmul(d_zeds, nearby[:, lanes]) * scaling
        d_nearby[:, lanes] += contract_rows(d_zeds, query_v_ref[here, lanes])
        d_projected_ref[here, lanes] = (grad_u + grad_v).astype(jnp.bfloat16)
        bias_ref[0:1, lanes] += jnp.sum(grad_u, axis=0, keepdims=True)
        bias_ref[1:2, lanes] += jnp.sum(grad_v, axis=0, keepdims=True)

    @pl.when(block == pl.num_programs(0) - 1)
    def _():
        d_projected_ref[:, local_width : 2 * local_width] = d_keys[...].astype(jnp.bfloat16)
        d_projected_ref[:, 2 * local_width :] = d_values[...].astype(jnp.bfloat16)
        d_position_ref[...] = d_places[...].astype(jnp.bfloat16)


def attention_backward(whole, weights, table_low, position, saved, grad_whole):
    w_in, w_pos, bias_pair, w_out = weights
    probs, context, query_u, query_v, key_rows, value_rows = saved
    seq_len, model_width = whole.shape
    local_width = w_out.shape[0]
    heads_here = local_width // HEAD
    rows = 128
    full = pl.BlockSpec(memory_space=pltpu.VMEM)
    d_projected, d_position, grad_bias = pl.pallas_call(
        functools.partial(attention_back_kernel, HEAD ** (-0.5)),
        grid=(seq_len // rows,),
        out_shape=[
            jax.ShapeDtypeStruct((seq_len, 3 * local_width), jnp.bfloat16),
            jax.ShapeDtypeStruct((2 * seq_len, local_width), jnp.bfloat16),
            jax.ShapeDtypeStruct((2, local_width), jnp.float32),
        ],
        in_specs=[
            pl.BlockSpec((rows, model_width), lambda block: (block, 0)),
            full,
            pl.BlockSpec((heads_here, rows, seq_len), lambda block: (0, block, 0)),
        ]
        + [full] * 5,
        out_specs=[full] * 3,
        scratch_shapes=[
            pltpu.VMEM((seq_len, local_width), jnp.float32),
            pltpu.VMEM((seq_len, local_width), jnp.float32),
            pltpu.VMEM((2 * seq_len, local_width), jnp.float32),
        ],
        compiler_params=pltpu.CompilerParams(vmem_limit_bytes=VMEM_LIMIT),
        name="attention_backward",
    )(grad_whole, w_out, probs, query_u, query_v, key_rows, value_rows, position)
    grad_in = contract_rows(whole, d_projected)
    d_normed = contract_cols(d_projected, w_in)
    grad_pos = contract_rows(table_low, d_position)
    grad_out = contract_rows(context, grad_whole)
    return (d_normed, grad_in, grad_pos, grad_bias, grad_out)


def conv_front(whole, w_in, kernel, mask_col):
    seq_len, model_width = whole.shape
    local_width = w_in.shape[2]
    glu_in = matmul(whole, w_in.reshape(model_width, 2 * local_width))
    gate_value = glu_in[:, :local_width]
    logistic = jax.nn.sigmoid(glu_in[:, local_width:])
    glu_out = gate_value * logistic * mask_col
    tap_count = kernel.shape[0]
    half_taps = (tap_count - 1) // 2
    padded = jnp.pad(glu_out, ((half_taps, half_taps), (0, 0)))
    kernel_float = kernel.astype(jnp.float32)
    conved = kernel_float[0] * padded[0:seq_len]
    for tap_index in range(1, tap_count):
        conved = conved + kernel_float[tap_index] * padded[tap_index : tap_index + seq_len]
    return (gate_value, logistic, padded, conved)


def batch_stats(conved, mask_col, frame_count):
    local_sum = jnp.sum(conved * mask_col, axis=0)
    local_squares = jnp.sum(conved * conved * mask_col, axis=0)
    total_sum, total_squares = dp_total(jnp.stack([local_sum, local_squares]))
    average = total_sum / frame_count
    variance = total_squares / frame_count - average * average
    return (average, lax.rsqrt(variance + batch_eps))


def conv_tail(conved, stats, bn_gain, bn_bias):
    average, inv_std = stats
    normed_b = (conved - average) * inv_std * bn_gain.astype(jnp.float32) + bn_bias.astype(
        jnp.float32
    )
    return (normed_b, jax.nn.silu(normed_b).astype(jnp.bfloat16))


def conv_backward(whole, weights, mask_col, stats, frame_count, grad_whole):
    w_in, kernel, bn_gain, bn_bias, w_out = weights
    seq_len, model_width = whole.shape
    local_width = w_in.shape[2]
    gate_value, logistic, padded, conved = conv_front(whole, w_in, kernel, mask_col)
    normed_b, active = conv_tail(conved, stats, bn_gain, bn_bias)
    average, inv_std = stats
    grad_out = contract_rows(active, grad_whole)
    d_normed = contract_cols(grad_whole, w_out) * silu_slope(normed_b)
    centred = (conved - average) * inv_std
    bias_total, gain_total = dp_total(
        jnp.stack([jnp.sum(d_normed, axis=0), jnp.sum(d_normed * centred, axis=0)])
    )
    d_conved = (
        bn_gain.astype(jnp.float32)
        * inv_std
        * (d_normed - mask_col * (bias_total + centred * gain_total) / frame_count)
    )
    tap_count = kernel.shape[0]
    half_taps = (tap_count - 1) // 2
    kernel_float = kernel.astype(jnp.float32)
    d_padded = jnp.pad(d_conved, ((half_taps, half_taps), (0, 0)))
    d_glu = kernel_float[0] * d_padded[tap_count - 1 : tap_count - 1 + seq_len]
    for tap_index in range(1, tap_count):
        d_glu = (
            d_glu
            + kernel_float[tap_index]
            * d_padded[tap_count - 1 - tap_index : tap_count - 1 - tap_index + seq_len]
        )
    grad_kernel = jnp.stack(
        [
            jnp.sum(d_conved * padded[tap_index : tap_index + seq_len], axis=0)
            for tap_index in range(tap_count)
        ]
    )
    d_glu = d_glu * mask_col
    d_pair = jnp.concatenate(
        [d_glu * logistic, d_glu * gate_value * logistic * (1.0 - logistic)], axis=1
    ).astype(jnp.bfloat16)
    grad_in = contract_rows(whole, d_pair).reshape(model_width, 2, local_width)
    d_normed_in = contract_cols(d_pair, w_in.reshape(model_width, 2 * local_width))
    return (d_normed_in, grad_in, grad_kernel, grad_out, gain_total, bias_total)


def body(
    frames_in,
    lengths,
    out_grad,
    norm_gains,
    ffn1_up,
    ffn1_down,
    attn_in,
    pos_proj,
    pos_bias,
    attn_out,
    conv_in,
    depthwise,
    bn_scale,
    bn_shift,
    conv_out,
    ffn2_up,
    ffn2_down,
):
    unused, local_rows, model_width = frames_in.shape
    seq_len = local_rows * lax.axis_size("mp")
    dp_index = lax.axis_index("dp")
    own_length = lax.dynamic_slice_in_dim(lengths, dp_index, 1)[0]
    valid_keys = jnp.arange(seq_len) < own_length
    mask_col = valid_keys.astype(jnp.float32)[:, None]
    frame_count = jnp.sum(lengths).astype(jnp.float32)
    frames = frames_in.reshape(local_rows, model_width)
    _, whole_first, fetched, small = open_step(
        open_middle,
        [frames, norm_gains],
        [ffn1_up, ffn1_down, pos_proj, attn_out, conv_out],
        (0, 1, 0, 1, 1),
        jnp.concatenate([pos_bias, depthwise, bn_scale[None], bn_shift[None]], axis=0),
        0,
    )
    up_one, down_one, pos_whole, attn_out_whole, conv_out_whole = fetched
    taps = depthwise.shape[0]
    ffn_first = (up_one, down_one)
    attn_held = (
        lax.all_gather(attn_in.reshape(attn_in.shape[0], -1), "dp", axis=0, tiled=True),
        pos_whole,
        small[:2],
        attn_out_whole,
    )
    conv_held = (
        lax.all_gather(conv_in, "dp", axis=0, tiled=True),
        small[2 : 2 + taps],
        small[2 + taps],
        small[3 + taps],
        conv_out_whole,
    )
    ffn_second = (
        lax.all_gather(ffn2_up, "dp", axis=0, tiled=True),
        lax.all_gather(ffn2_down, "dp", axis=1, tiled=True),
    )
    table_low = position_table(seq_len, model_width).astype(jnp.bfloat16)
    position = matmul(table_low, pos_whole).astype(jnp.bfloat16)
    (after_first,), whole_attn, _ = between_step(
        functools.partial(forward_middle, 0.5, 1),
        ffn_forward(whole_first, ffn_first),
        [frames, norm_gains],
        [],
        (),
        (),
        1,
    )
    attn_partial, *attn_saved = attention_forward(
        whole_attn, attn_held, position, own_length[None]
    )
    (after_attn,), whole_conv, _ = between_step(
        functools.partial(forward_middle, 1.0, 2),
        attn_partial,
        [after_first, norm_gains],
        [],
        (),
        (),
        2,
    )
    gate_value, logistic, padded, conved = conv_front(
        whole_conv, conv_held[0], conv_held[1], mask_col
    )
    stats = batch_stats(conved, mask_col, frame_count)
    normed_b, active = conv_tail(conved, stats, conv_held[2], conv_held[3])
    (after_conv,), whole_second, _ = between_step(
        functools.partial(forward_middle, 1.0, 3),
        matmul(active, conv_held[4]),
        [after_attn, norm_gains],
        [],
        (),
        (),
        3,
    )
    (block_out, d_second, gain_five), whole_grads, _ = between_step(
        turn_middle,
        ffn_forward(whole_second, ffn_second),
        [after_conv, norm_gains, out_grad.reshape(local_rows, model_width)],
        [],
        (),
        (),
        4,
    )
    d_normed, grad_up, grad_down = ffn_backward(whole_second, ffn_second, whole_grads)
    (d_conv, gain_four), whole_grads, (total_up_two, total_down_two) = between_step(
        functools.partial(backward_middle, 1.0, 3),
        d_normed,
        [after_conv, norm_gains, d_second],
        [grad_up, grad_down],
        (0, 1),
        (False, True),
        5,
    )
    d_normed, grad_conv_in, grad_kernel, grad_conv_out, gain_total, bias_total = conv_backward(
        whole_conv, conv_held, mask_col, stats, frame_count, whole_grads
    )
    (d_attn, gain_three), whole_grads, (total_conv_in, total_conv_out) = between_step(
        functools.partial(backward_middle, 1.0, 2),
        d_normed,
        [after_attn, norm_gains, d_conv],
        [grad_conv_in.reshape(model_width, -1), grad_conv_out],
        (0, 1),
        (False, True),
        6,
    )
    d_normed, grad_attn_in, grad_pos, grad_bias, grad_attn_out = attention_backward(
        whole_attn, attn_held, table_low, position, attn_saved, whole_grads
    )
    (d_first, gain_two), whole_grads, (total_attn_in, total_attn_out, total_pos) = between_step(
        functools.partial(backward_middle, 0.5, 1),
        d_normed,
        [after_first, norm_gains, d_attn],
        [grad_attn_in, grad_attn_out, grad_pos],
        (0, 1, 0),
        (False, True, True),
        7,
    )
    d_normed, grad_up, grad_down = ffn_backward(whole_first, ffn_first, whole_grads)
    (in_grad,), small_grads, gains, (total_up_one, total_down_one) = close_step(
        close_middle,
        d_normed,
        jnp.concatenate([grad_bias, grad_kernel], axis=0),
        jnp.concatenate([gain_two, gain_three, gain_four, gain_five], axis=0),
        [frames, norm_gains, d_first],
        [grad_up, grad_down],
        (0, 1),
        (False, True),
        8,
    )
    gain_sum = jnp.concatenate([gains[4:], gains[:4]], axis=0)
    block = model_width // lax.axis_size("dp")
    piece_len = bn_scale.shape[0]
    own = dp_index * piece_len
    small_grads = lax.dynamic_slice_in_dim(small_grads, own, piece_len, axis=1)
    return (
        block_out.reshape(1, local_rows, model_width),
        in_grad.reshape(1, local_rows, model_width),
        gain_sum,
        total_up_one,
        total_down_one,
        total_attn_in.reshape(block, 3, -1),
        total_pos,
        small_grads[:2],
        total_attn_out,
        total_conv_in.reshape(block, 2, -1),
        small_grads[2:],
        lax.dynamic_slice_in_dim(gain_total, own, piece_len),
        lax.dynamic_slice_in_dim(bias_total, own, piece_len),
        total_conv_out,
        total_up_two,
        total_down_two,
    )


def solution(mesh):
    placed = (
        P("dp", "mp", None),
        P(),
        P("dp", "mp", None),
        P(),
        P("dp", "mp"),
        P("mp", "dp"),
        P("dp", None, "mp"),
        P("dp", "mp"),
        P(None, ("mp", "dp")),
        P("mp", "dp"),
        P("dp", None, "mp"),
        P(None, ("mp", "dp")),
        P(("mp", "dp")),
        P(("mp", "dp")),
        P("mp", "dp"),
        P("dp", "mp"),
        P("mp", "dp"),
    )
    return jax.shard_map(
        body,
        mesh=mesh,
        in_specs=placed,
        out_specs=(
            P("dp", "mp", None),
            P("dp", "mp", None),
            P(),
            P("dp", "mp"),
            P("mp", "dp"),
            P("dp", None, "mp"),
            P("dp", "mp"),
            P(None, ("mp", "dp")),
            P("mp", "dp"),
            P("dp", None, "mp"),
            P(None, ("mp", "dp")),
            P(("mp", "dp")),
            P(("mp", "dp")),
            P("mp", "dp"),
            P("dp", "mp"),
            P("mp", "dp"),
        ),
        check_vma=False,
    )
```

```python
import functools
import math

import jax
import jax.numpy as jnp
from jax import lax
from jax.experimental import pallas as pl
from jax.experimental.pallas import tpu as pltpu
from jax.sharding import PartitionSpec as P

HEAD = 128


norm_eps = 1e-05
batch_eps = 1e-05
masked_score = -1000000000.0


def matmul(left, right):
    return jnp.dot(left, right, preferred_element_type=jnp.float32)


def contract_rows(left, right):
    return lax.dot_general(
        left, right, (((0,), (0,)), ((), ())), preferred_element_type=jnp.float32
    )


def contract_cols(left, right):
    return lax.dot_general(
        left, right, (((1,), (1,)), ((), ())), preferred_element_type=jnp.float32
    )


def layer_norm(values, norm_gain):
    average = jnp.mean(values, axis=-1, keepdims=True)
    centred = values - average
    inv_std = lax.rsqrt(jnp.mean(centred * centred, axis=-1, keepdims=True) + norm_eps)
    return centred * inv_std * norm_gain


def silu_slope(values):
    logistic = jax.nn.sigmoid(values)
    return logistic * (1.0 + values * (1.0 - logistic))


def position_table(seq_len, model_width):
    fine = 32
    lane = jnp.arange(model_width)
    frequency = jnp.exp((lane // 2).astype(jnp.float32) * (-2.0 * math.log(10000.0) / model_width))
    coarse = (seq_len - 1 - fine * jnp.arange(2 * seq_len // fine)).astype(jnp.float32)
    wide = coarse[:, None] * frequency[None, :]
    small = -jnp.arange(fine).astype(jnp.float32)[:, None] * frequency[None, :]
    even = (lane % 2 == 0)[None, :]
    wide_sin, wide_cos = jnp.sin(wide), jnp.cos(wide)
    high = jnp.where(even, wide_sin, wide_cos)
    side = jnp.where(even, wide_cos, -wide_sin)
    table = high[:, None, :] * jnp.cos(small)[None] + side[:, None, :] * jnp.sin(small)[None]
    return table.reshape(2 * seq_len, model_width)


MESH = pl.DeviceIdType.MESH
VMEM_LIMIT = 60 * 1024 * 1024
CHUNKS = 2


def line_copy(src, dst, sems, index, axis, target):
    return pltpu.make_async_remote_copy(
        src_ref=src,
        dst_ref=dst,
        send_sem=sems.at[0, index],
        recv_sem=sems.at[1, index],
        device_id={axis: target},
        device_id_type=MESH,
    )


def bit_of(index, bit):
    return lax.rem(lax.div(index, bit), 2)


def partner(index, bit):
    return index + bit - 2 * bit * bit_of(index, bit)


def cube_bits(size, swap):
    bits = []
    bit = 2
    while bit < size:
        bits.append(bit)
        bit *= 2
    if swap:
        bits.reverse()
    return bits + [1]


def block_at(ref, dim, index, width):
    start = pl.multiple_of(index * width, width)
    return ref.at[pl.ds(start, width)] if dim == 0 else ref.at[:, pl.ds(start, width)]


def all_total_kernel(axis, in_ref, out_ref, slots, sems):
    size = lax.axis_size(axis)
    me = lax.axis_index(axis)
    barrier = pltpu.get_barrier_semaphore()
    targets = [lax.rem(me + step, size) for step in range(1, size)]
    for target in targets:
        pl.semaphore_signal(barrier, inc=1, device_id={axis: target}, device_id_type=MESH)
    pl.semaphore_wait(barrier, size - 1)
    copies = []
    for number, target in enumerate(targets):
        copy = line_copy(in_ref, slots.at[me], sems, number, axis, target)
        copy.start()
        copies.append(copy)
    slots[me] = in_ref[...]
    for copy in copies:
        copy.wait_recv()
    total = slots[0]
    for source in range(1, size):
        total = total + slots[source]
    out_ref[...] = total
    for copy in copies:
        copy.wait_send()


def all_total(values, axis, collective_id):
    size = lax.axis_size(axis)
    return pl.pallas_call(
        functools.partial(all_total_kernel, axis),
        out_shape=jax.ShapeDtypeStruct(values.shape, values.dtype),
        in_specs=[pl.BlockSpec(memory_space=pltpu.VMEM)],
        out_specs=pl.BlockSpec(memory_space=pltpu.VMEM),
        scratch_shapes=[
            pltpu.VMEM((size, *values.shape), values.dtype),
            pltpu.SemaphoreType.DMA((2, size - 1)),
        ],
        compiler_params=pltpu.CompilerParams(
            collective_id=collective_id, has_side_effects=True
        ),
        name="all_total",
    )(values)


def line_peers(axis):
    me, size = lax.axis_index(axis), lax.axis_size(axis)
    return jnp.minimum(me, 1) + jnp.minimum(size - 1 - me, 1)


def greet(line_axis, cube_axis, everyone):
    me, size = lax.axis_index(line_axis), lax.axis_size(line_axis)
    barrier = pltpu.get_barrier_semaphore()
    if everyone:
        for axis in (line_axis, cube_axis):
            here, count = lax.axis_index(axis), lax.axis_size(axis)
            for step in range(1, count):
                pl.semaphore_signal(
                    barrier, inc=1, device_id={axis: lax.rem(here + step, count)},
                    device_id_type=MESH,
                )
        pl.semaphore_wait(barrier, size - 1 + lax.axis_size(cube_axis) - 1)
        return

    @pl.when(me > 0)
    def _():
        pl.semaphore_signal(barrier, inc=1, device_id={line_axis: me - 1}, device_id_type=MESH)

    @pl.when(me < size - 1)
    def _():
        pl.semaphore_signal(barrier, inc=1, device_id={line_axis: me + 1}, device_id_type=MESH)

    bits = cube_bits(lax.axis_size(cube_axis), False) if cube_axis else []
    for bit in bits:
        pl.semaphore_signal(
            barrier, inc=1, device_id={cube_axis: partner(lax.axis_index(cube_axis), bit)},
            device_id_type=MESH,
        )
    pl.semaphore_wait(barrier, line_peers(line_axis) + len(bits))


class LineGather:
    def __init__(self, axis, out_ref, sems, chunks):
        self.axis, self.out, self.sems, self.chunks = axis, out_ref, sems, chunks
        self.size, self.me = lax.axis_size(axis), lax.axis_index(axis)
        self.rows = out_ref.shape[0] // self.size
        self.part = self.rows // chunks
        self.steps = self.size - 1

    def piece(self, index, chunk):
        start = pl.multiple_of(index * self.rows + chunk * self.part, self.part)
        return self.out.at[pl.ds(start, self.part)]

    def copy(self, way, step, index, chunk):
        place = self.piece(index, chunk)
        return line_copy(
            place, place, self.sems, (way * self.steps + step) * self.chunks + chunk, self.axis,
            self.me + 1 if way == 0 else self.me - 1,
        )

    def index(self, way, step):
        return self.me - step if way == 0 else self.me + step

    def held(self, way, step):
        return self.me >= step if way == 0 else self.me + step < self.size

    def onward(self, way):
        return self.me + 1 < self.size if way == 0 else self.me > 0

    def step(self, step, chunk):
        for way in range(2):
            if step > 0:
                @pl.when(self.held(way, step))
                def _():
                    self.copy(way, step - 1, self.index(way, step), chunk).wait_recv()

            if step < self.steps:
                @pl.when(jnp.logical_and(self.held(way, step), self.onward(way)))
                def _():
                    self.copy(way, step, self.index(way, step), chunk).start()

    def finish(self):
        for chunk in range(self.chunks):
            for step in range(self.steps):
                for way in range(2):
                    @pl.when(jnp.logical_and(self.held(way, step), self.onward(way)))
                    def _():
                        self.copy(way, step, self.index(way, step), chunk).wait_send()


class LineScatter:
    def __init__(self, axis, in_ref, total_ref, slots, staged, sems, chunks):
        self.axis, self.ins, self.total, self.chunks = axis, in_ref, total_ref, chunks
        self.slots, self.staged, self.sems = slots, staged, sems
        self.size, self.me = lax.axis_size(axis), lax.axis_index(axis)
        self.rows = total_ref.shape[0]
        self.part = self.rows // chunks
        self.first_way = lax.div(self.me, (self.size + 1) // 2)

    def mine(self, owner, chunk):
        start = pl.multiple_of(owner * self.rows + chunk * self.part, self.part)
        return self.ins.at[pl.ds(start, self.part)]

    def lines(self, chunk):
        return slice(chunk * self.part, (chunk + 1) * self.part)

    def copy(self, way, owner, chunk, src):
        return line_copy(
            src, self.slots.at[way, owner, self.lines(chunk)], self.sems,
            (way * self.size + owner) * self.chunks + chunk, self.axis,
            self.me + 1 - 2 * way,
        )

    def arrived(self, way, owner, chunk):
        return self.copy(way, owner, chunk, self.staged.at[way, owner, self.lines(chunk)])

    def place(self, way, step):
        owner = (1 - way) * (self.size - 1 - step) + way * step
        distance = (owner - self.me) * (1 - 2 * way)
        behind = (1 - way) * self.me + way * (self.size - 1 - self.me)
        return owner, distance, behind

    def lead(self, step, chunk):
        for way in range(2):
            owner, distance, behind = self.place(way, step)

            @pl.when(jnp.logical_and(distance > 0, behind == 0))
            def _():
                self.copy(way, owner, chunk, self.mine(owner, chunk)).start()

    def hop(self, way, step, chunk):
        owner, distance, behind = self.place(way, step)

        @pl.when(jnp.logical_and(distance > 0, behind > 0))
        def _():
            lines = self.lines(chunk)
            self.arrived(way, owner, chunk).wait_recv()
            self.staged[way, owner, lines] = (
                self.mine(owner, chunk)[...].astype(jnp.float32)
                + self.slots[way, owner, lines].astype(jnp.float32)
            ).astype(self.staged.dtype)
            self.arrived(way, owner, chunk).start()

    def run(self):
        marks = [(step, chunk) for step in range(self.size - 1) for chunk in range(self.chunks)]
        for mark in marks:
            self.lead(*mark)
        for number in range(len(marks) + self.chunks):
            if number < len(marks):
                self.hop(self.first_way, *marks[number])
            if number >= self.chunks:
                self.hop(1 - self.first_way, *marks[number - self.chunks])

    def result(self, chunk):
        lines = self.lines(chunk)
        self.total[lines] = self.mine(self.me, chunk)[...].astype(jnp.float32)
        for way in range(2):
            @pl.when(self.me > 0 if way == 0 else self.me < self.size - 1)
            def _():
                self.arrived(way, self.me, chunk).wait_recv()
                self.total[lines] += self.slots[way, self.me, lines].astype(jnp.float32)

        return self.total[lines]

    def finish(self):
        for chunk in range(self.chunks):
            for owner in range(self.size):
                for way in range(2):
                    @pl.when(self.me < owner if way == 0 else self.me > owner)
                    def _():
                        self.arrived(way, owner, chunk).wait_send()


class CubeGather:
    def __init__(self, axis, dims, ways, ins, outs, sems):
        self.axis, self.dims, self.ways = axis, dims, ways
        self.ins, self.outs, self.sems = ins, outs, sems
        self.size, self.me = lax.axis_size(axis), lax.axis_index(axis)
        self.stages = len(cube_bits(self.size, False))
        self.started = []
        self.waiting = [[] for _ in ins]

    def step(self, stage):
        per = self.size - 1
        for which in range(len(self.ins)):
            width = self.ins[which].shape[self.dims[which]]
            bits = cube_bits(self.size, self.ways[which])
            for copy in self.waiting[which]:
                copy.wait_recv()
            self.waiting[which] = []
            if stage == 0:
                block_at(self.outs[which], self.dims[which], self.me, width)[...] = (
                    self.ins[which][...]
                )
            if stage == self.stages:
                continue
            held = [self.me]
            for bit in bits[:stage]:
                held = held + [partner(index, bit) for index in held]
            for number, index in enumerate(held):
                place = block_at(self.outs[which], self.dims[which], index, width)
                copy = line_copy(
                    self.ins[which] if stage == 0 else place, place, self.sems,
                    which * per + 2**stage - 1 + number, self.axis, partner(self.me, bits[stage]),
                )
                copy.start()
                self.waiting[which].append(copy)
            self.started.extend(self.waiting[which])

    def finish(self):
        for copy in self.started:
            copy.wait_send()


class CubeScatter:
    def __init__(self, axis, dims, ways, ins, outs, slots, sems):
        self.axis, self.dims, self.ways = axis, dims, ways
        self.ins, self.outs, self.slots, self.sems = ins, outs, slots, sems
        self.size, self.me = lax.axis_size(axis), lax.axis_index(axis)
        self.stages = len(cube_bits(self.size, False))
        self.started = []

    def slot(self, which, stage, number):
        return self.slots[which].at[self.size - self.size // 2**stage + number]

    def sets(self, which, stage):
        bits = cube_bits(self.size, self.ways[which])[::-1]
        held = [self.me]
        for bit in bits[stage + 1 :]:
            held = held + [partner(index, bit) for index in held]
        return bits[stage], held

    def send(self, which, stage):
        width = self.outs[which].shape[self.dims[which]]
        bit, held = self.sets(which, stage)
        for number, index in enumerate(held):
            if stage == 0:
                src = block_at(self.ins[which], self.dims[which], partner(index, bit), width)
            else:
                src = self.slot(which, stage - 1, 2 * number + 1)
            copy = line_copy(
                src, self.slot(which, stage, number), self.sems,
                which * (self.size - 1) + self.size - self.size // 2**stage + number,
                self.axis, partner(self.me, bit),
            )
            copy.start()
            self.started.append((which, stage, copy))

    def receive(self, which, stage):
        width = self.outs[which].shape[self.dims[which]]
        _, held = self.sets(which, stage)
        for copy in [c for w, s, c in self.started if (w, s) == (which, stage)]:
            copy.wait_recv()
        for number, index in enumerate(held):
            got = self.slot(which, stage, number)
            if stage == 0:
                mine = block_at(self.ins[which], self.dims[which], index, width)
            else:
                mine = self.slot(which, stage - 1, 2 * number)
            total = got[...].astype(jnp.float32) + mine[...].astype(jnp.float32)
            if stage == self.stages - 1:
                self.outs[which][...] = total
            else:
                got[...] = total.astype(self.slots[which].dtype)

    def step(self, stage):
        for which in range(len(self.ins)):
            if stage > 0:
                self.receive(which, stage - 1)
            if stage < self.stages:
                self.send(which, stage)

    def finish(self):
        for _, _, copy in self.started:
            copy.wait_send()


class AllTotal:
    def __init__(self, axis, slots, sems):
        self.axis, self.slots, self.sems = axis, slots, sems
        self.size, self.me = lax.axis_size(axis), lax.axis_index(axis)
        self.copies = []

    def start(self):
        for step in range(1, self.size):
            copy = line_copy(
                self.slots.at[self.me], self.slots.at[self.me], self.sems, step - 1, self.axis,
                lax.rem(self.me + step, self.size),
            )
            copy.start()
            self.copies.append(copy)

    def result(self):
        for copy in self.copies:
            copy.wait_recv()
        total = self.slots[0]
        for source in range(1, self.size):
            total = total + self.slots[source]
        return total

    def finish(self):
        for copy in self.copies:
            copy.wait_send()


def open_kernel(middle, counts, chunks, dims, ways, *refs):
    local_count, mid_count = counts
    count = len(dims)
    refs = list(refs)
    take = lambda number: [refs.pop(0) for _ in range(number)]
    locals_, ins = take(local_count), take(count)
    mids, (whole,), outs = take(mid_count), take(1), take(count)
    gather_sems, cube_sems = refs
    fetch = CubeGather("dp", dims, ways, ins, outs, cube_sems)
    rows = LineGather("mp", whole, gather_sems, chunks)
    greet("mp", "dp", False)
    fetch.step(0)
    values, normed = middle(None, *[ref[...] for ref in locals_])
    for ref, value in zip(mids, values):
        ref[...] = value
    for chunk in range(chunks):
        part = rows.part
        rows.piece(rows.me, chunk)[...] = normed[chunk * part : (chunk + 1) * part]
        rows.step(0, chunk)
    for step in range(1, max(rows.steps, fetch.stages) + 1):
        if step <= fetch.stages:
            fetch.step(step)
        if step <= rows.steps:
            for chunk in range(chunks):
                rows.step(step, chunk)
    rows.finish()
    fetch.finish()


def between_kernel(middle, counts, chunks, fetches, dims, ways, *refs):
    local_count, mid_count = counts
    count = len(dims)
    refs = list(refs)
    take = lambda number: [refs.pop(0) for _ in range(number)]
    (partial,), locals_, ins = take(1), take(local_count), take(count)
    mids, (whole,), outs = take(mid_count), take(1), take(count)
    (total, slots, staged, scatter_sems, gather_sems), refs = refs[:5], refs[5:]
    sums = LineScatter("mp", partial, total, slots, staged, scatter_sems, chunks)
    rows = LineGather("mp", whole, gather_sems, chunks)
    beside, stages = None, 0
    if count:
        if fetches:
            beside = CubeGather("dp", dims, ways, ins, outs, refs[0])
        else:
            beside = CubeScatter("dp", dims, ways, ins, outs, refs[:count], refs[count])
        stages = beside.stages + 1
    greet("mp", "dp" if count else None, False)
    stage = 0
    if stages:
        beside.step(0)
        stage = 1
    sums.run()
    for chunk in range(chunks):
        lines = sums.lines(chunk)
        picked = [ref[lines] if ref.shape[0] == sums.rows else ref[...] for ref in locals_]
        values, normed = middle(sums.result(chunk), *picked)
        rows.piece(rows.me, chunk)[...] = normed
        rows.step(0, chunk)
        for ref, value in zip(mids, values):
            if ref.shape[0] == sums.rows:
                ref[lines] = value
            elif chunk == 0:
                ref[...] = value
            else:
                ref[...] += value
    for step in range(1, rows.steps + 1):
        if stage < stages:
            beside.step(stage)
            stage += 1
        for chunk in range(chunks):
            rows.step(step, chunk)
    for stage in range(stage, stages):
        beside.step(stage)
    if count:
        beside.finish()
    sums.finish()
    rows.finish()


def close_kernel(middle, counts, chunks, dims, ways, *refs):
    local_count, mid_count = counts
    count = len(dims)
    refs = list(refs)
    take = lambda number: [refs.pop(0) for _ in range(number)]
    (partial, small, gains), locals_, ins = take(3), take(local_count), take(count)
    mids, (small_out, gains_out), outs = take(mid_count), take(2), take(count)
    (total, slots, staged, scatter_sems), refs = refs[:4], refs[4:]
    (small_slots, small_sems, gain_slots, gain_sems, last_slots, last_sems), refs = refs[:6], refs[6:]
    sums = LineScatter("mp", partial, total, slots, staged, scatter_sems, chunks)
    grads = CubeScatter("dp", dims, ways, ins, outs, refs[:count], refs[count])
    little = AllTotal("dp", small_slots, small_sems)
    near, far = AllTotal("dp", gain_slots, gain_sems), AllTotal("mp", last_slots, last_sems)
    little.slots[little.me] = small[...]
    greet("mp", "dp", True)
    little.start()
    grads.step(0)
    sums.run()
    grads.step(1)
    total_rows = jnp.concatenate([sums.result(chunk) for chunk in range(chunks)], axis=0)
    values, gain = middle(total_rows, *[ref[...] for ref in locals_])
    near.slots[near.me] = jnp.concatenate([gains[...], gain], axis=0)
    near.start()
    for ref, value in zip(mids, values):
        ref[...] = value
    grads.step(2)
    far.slots[far.me] = near.result()
    far.start()
    for stage in range(3, grads.stages + 1):
        grads.step(stage)
    small_out[...] = little.result()
    gains_out[...] = far.result()
    for task in (grads, sums, little, near, far):
        task.finish()


def shapes_of(arrays):
    return [jax.ShapeDtypeStruct(value.shape, value.dtype) for value in arrays]


def call_step(kernel, inputs, out_shape, scratch, collective_id, name):
    vmem = pl.BlockSpec(memory_space=pltpu.VMEM)
    return pl.pallas_call(
        kernel,
        out_shape=out_shape,
        in_specs=[vmem] * len(inputs),
        out_specs=[vmem] * len(out_shape),
        scratch_shapes=scratch,
        compiler_params=pltpu.CompilerParams(
            collective_id=collective_id, has_side_effects=True, vmem_limit_bytes=VMEM_LIMIT
        ),
        name=name,
    )(*inputs)


def line_scratch(rows, width, chunks):
    size = lax.axis_size("mp")
    return [
        pltpu.VMEM((rows, width), jnp.float32),
        pltpu.VMEM((2, size, rows, width), jnp.bfloat16),
        pltpu.VMEM((2, size, rows, width), jnp.bfloat16),
        pltpu.SemaphoreType.DMA((2, 2 * size * chunks)),
    ]


def cube_scratch(arrays, dims):
    size = lax.axis_size("dp")
    shapes, slots = [], []
    for array, dim in zip(arrays, dims):
        shape = list(array.shape)
        shape[dim] //= size
        shapes.append(jax.ShapeDtypeStruct(tuple(shape), jnp.float32))
        slots.append(pltpu.VMEM((size - 1, *shape), array.dtype))
    if arrays:
        slots.append(pltpu.SemaphoreType.DMA((2, len(arrays) * (size - 1))))
    return shapes, slots


def plain_totals(grads, dims):
    return [
        lax.psum_scatter(grad, "dp", scatter_dimension=dim, tiled=True).astype(jnp.float32)
        for grad, dim in zip(grads, dims)
    ]


def direct(block):
    size = lax.axis_size("dp")
    return size & (size - 1) == 0 and block % 128 == 0


def fetched_shapes(arrays, dims):
    size, shapes = lax.axis_size("dp"), []
    for array, dim in zip(arrays, dims):
        shape = list(array.shape)
        shape[dim] *= size
        shapes.append(jax.ShapeDtypeStruct(tuple(shape), array.dtype))
    return shapes


def plain_fetch(arrays, dims):
    return [lax.all_gather(array, "dp", axis=dim, tiled=True) for array, dim in zip(arrays, dims)]


def packed_rows(small):
    return jnp.pad(small, ((0, 16 - small.shape[0]), (0, 128 - small.shape[1])))


def whole_rows(packed, small):
    size, (count, lanes) = lax.axis_size("dp"), small.shape
    packed = packed.reshape(size, 16, 128)[:, :count, :lanes]
    return packed.transpose(1, 0, 2).reshape(count, size * lanes)


def open_step(middle, locals_, arrays, dims, collective_id):
    if not direct(arrays[0].shape[dims[0]]):
        mids, normed = middle(None, *locals_)
        return mids, lax.all_gather(normed, "mp", axis=0, tiled=True), plain_fetch(arrays, dims)
    ways = [index % 2 == 1 for index in range(len(dims))]
    mid_shapes, normed_shape = jax.eval_shape(functools.partial(middle, None), *locals_)
    rows, width = normed_shape.shape
    whole_shape = jax.ShapeDtypeStruct((rows * lax.axis_size("mp"), width), normed_shape.dtype)
    count = len(mid_shapes)
    result = call_step(
        functools.partial(open_kernel, middle, (len(locals_), count), CHUNKS, dims, ways),
        [*locals_, *arrays],
        [*mid_shapes, whole_shape, *fetched_shapes(arrays, dims)],
        [
            pltpu.SemaphoreType.DMA((2, 2 * (lax.axis_size("mp") - 1) * CHUNKS)),
            pltpu.SemaphoreType.DMA((2, len(arrays) * (lax.axis_size("dp") - 1))),
        ],
        collective_id,
        "open_step",
    )
    return result[:count], result[count], result[count + 1 :]


def between_step(
    middle, partial_value, locals_, collective_id, grads=(), fetch=(), dims=(), ways=()
):
    partial_value = partial_value.astype(jnp.bfloat16)
    grads = [grad.astype(jnp.bfloat16) for grad in grads]
    size = lax.axis_size("mp")
    rows, width = partial_value.shape[0] // size, partial_value.shape[1]
    if not direct(width // lax.axis_size("dp")):
        total = lax.psum_scatter(partial_value, "mp", scatter_dimension=0, tiled=True)
        mids, normed = middle(total.astype(jnp.float32), *locals_)
        others = plain_fetch(fetch, dims) if fetch else plain_totals(grads, dims)
        return mids, lax.all_gather(normed, "mp", axis=0, tiled=True), others
    total = jax.ShapeDtypeStruct((rows, width), jnp.float32)
    mid_shapes, normed_shape = jax.eval_shape(middle, total, *locals_)
    if fetch:
        shapes = fetched_shapes(fetch, dims)
        scratch = [pltpu.SemaphoreType.DMA((2, len(fetch) * (lax.axis_size("dp") - 1)))]
    else:
        shapes, scratch = cube_scratch(grads, dims)
    count = len(mid_shapes)
    result = call_step(
        functools.partial(
            between_kernel, middle, (len(locals_), count), CHUNKS, bool(fetch), dims, ways
        ),
        [partial_value, *locals_, *grads, *fetch],
        [
            *mid_shapes,
            jax.ShapeDtypeStruct((rows * size, width), normed_shape.dtype),
            *shapes,
        ],
        line_scratch(rows, width, CHUNKS)
        + [pltpu.SemaphoreType.DMA((2, 2 * (size - 1) * CHUNKS))]
        + scratch,
        collective_id,
        "between_step",
    )
    return result[:count], result[count], result[count + 1 :]


def close_step(middle, partial_value, small, gains, locals_, grads, dims, ways, collective_id):
    partial_value = partial_value.astype(jnp.bfloat16)
    grads = [grad.astype(jnp.bfloat16) for grad in grads]
    size, dp_size = lax.axis_size("mp"), lax.axis_size("dp")
    rows, width = partial_value.shape[0] // size, partial_value.shape[1]
    if not direct(width // dp_size):
        total = lax.psum_scatter(partial_value, "mp", scatter_dimension=0, tiled=True)
        mids, gain = middle(total.astype(jnp.float32), *locals_)
        gains = lax.psum(jnp.concatenate([gains, gain], axis=0), ("dp", "mp"))
        return mids, lax.psum(small, "dp"), gains, plain_totals(grads, dims)
    total = jax.ShapeDtypeStruct((rows, width), jnp.float32)
    mid_shapes, gain_shape = jax.eval_shape(middle, total, *locals_)
    gains_shape = jax.ShapeDtypeStruct((gains.shape[0] + 1, width), jnp.float32)
    shapes, slots = cube_scratch(grads, dims)
    count = len(mid_shapes)
    result = call_step(
        functools.partial(close_kernel, middle, (len(locals_), count), CHUNKS, dims, ways),
        [partial_value, small, gains, *locals_, *grads],
        [*mid_shapes, *shapes_of([small]), gains_shape, *shapes],
        line_scratch(rows, width, CHUNKS)
        + [
            pltpu.VMEM((dp_size, *small.shape), jnp.float32),
            pltpu.SemaphoreType.DMA((2, dp_size - 1)),
            pltpu.VMEM((dp_size, *gains_shape.shape), jnp.float32),
            pltpu.SemaphoreType.DMA((2, dp_size - 1)),
            pltpu.VMEM((size, *gains_shape.shape), jnp.float32),
            pltpu.SemaphoreType.DMA((2, size - 1)),
        ]
        + slots,
        collective_id,
        "close_step",
    )
    return result[:count], result[count], result[count + 1], result[count + 2 :]


def forward_middle(scale, row, total, residual, norm_gains):
    residual = residual.astype(jnp.float32)
    if total is not None:
        residual = residual + scale * total
    return [residual], layer_norm(residual, norm_gains[row : row + 1]).astype(jnp.bfloat16)


def open_middle(total, frames, norm_gains):
    return [], layer_norm(frames.astype(jnp.float32), norm_gains[0:1]).astype(jnp.bfloat16)


def norm_back(values, norm_gain, upstream):
    centred = values - jnp.mean(values, axis=-1, keepdims=True)
    inv_std = lax.rsqrt(jnp.mean(centred * centred, axis=-1, keepdims=True) + norm_eps)
    normed = centred * inv_std
    scaled = upstream * norm_gain
    d_values = inv_std * (
        scaled
        - jnp.mean(scaled, axis=-1, keepdims=True)
        - normed * jnp.mean(scaled * normed, axis=-1, keepdims=True)
    )
    return d_values, jnp.sum(upstream * normed, axis=0, keepdims=True)


def turn_middle(total, residual, norm_gains, out_grad):
    after = residual + 0.5 * total
    gain = norm_gains[4:5]
    d_after, d_gain = norm_back(after, gain, out_grad.astype(jnp.float32))
    block_out = layer_norm(after, gain).astype(jnp.bfloat16)
    return [block_out, d_after, d_gain], (0.5 * d_after).astype(jnp.bfloat16)


def backward_middle(scale, row, total, values, norm_gains, upstream):
    d_branch, d_gain = norm_back(values.astype(jnp.float32), norm_gains[row : row + 1], total)
    d_values = upstream + d_branch
    return [d_values, d_gain], (scale * d_values).astype(jnp.bfloat16)


def close_middle(total, values, norm_gains, upstream):
    d_branch, d_gain = norm_back(values.astype(jnp.float32), norm_gains[0:1], total)
    return [upstream + d_branch], d_gain


def dp_total(values):
    if direct(128):
        return all_total(values, "dp", 9)
    return lax.psum(values, "dp")


def ffn_forward(whole, weights):
    w_up, w_down = weights
    hidden = matmul(whole, w_up)
    return matmul(jax.nn.silu(hidden).astype(jnp.bfloat16), w_down)


def ffn_backward(whole, weights, grad_whole):
    w_up, w_down = weights
    hidden = matmul(whole, w_up)
    active = jax.nn.silu(hidden).astype(jnp.bfloat16)
    grad_down = contract_rows(active, grad_whole)
    d_hidden = (contract_cols(grad_whole, w_down) * silu_slope(hidden)).astype(jnp.bfloat16)
    grad_up = contract_rows(whole, d_hidden)
    return (contract_cols(d_hidden, w_up), grad_up, grad_down)


def place_position(position_ref, block, rows, seq_len):
    start = pl.multiple_of(seq_len - rows - block * rows, rows)
    return position_ref.at[pl.ds(start, seq_len + rows)]


def attention_kernel(
    scaling, length_ref, whole_ref, in_ref, bias_ref, position_ref, out_w_ref,
    partial_ref, probs_ref, context_ref, query_u_ref, query_v_ref, key_ref, value_ref,
):
    block = pl.program_id(0)
    seq_len, local_width = key_ref.shape
    rows = partial_ref.shape[0]

    @pl.when(block == 0)
    def _():
        projected = matmul(whole_ref[...], in_ref[...])
        queries = projected[:, :local_width]
        query_u_ref[...] = ((queries + bias_ref[0:1]) * scaling).astype(jnp.bfloat16)
        query_v_ref[...] = ((queries + bias_ref[1:2]) * scaling).astype(jnp.bfloat16)
        key_ref[...] = projected[:, local_width : 2 * local_width].astype(jnp.bfloat16)
        value_ref[...] = projected[:, 2 * local_width :].astype(jnp.bfloat16)

    here = pl.ds(pl.multiple_of(block * rows, rows), rows)
    valid = lax.broadcasted_iota(jnp.int32, (rows, seq_len), 1) < length_ref[0]
    nearby = place_position(position_ref, block, rows, seq_len)
    pieces = []
    for head in range(local_width // HEAD):
        lanes = slice(head * HEAD, (head + 1) * HEAD)
        content = contract_cols(query_u_ref[here, lanes], key_ref[:, lanes])
        zeds = contract_cols(query_v_ref[here, lanes], nearby[:, lanes])
        shifted = pltpu.roll(zeds, seq_len + 1, 1, stride=1, stride_axis=0)[:, :seq_len]
        scores = jnp.where(valid, content + shifted, masked_score)
        exponent = jnp.exp(scores - jnp.max(scores, axis=-1, keepdims=True))
        probs = exponent / jnp.sum(exponent, axis=-1, keepdims=True)
        probs_ref[head] = probs
        pieces.append(matmul(probs.astype(jnp.bfloat16), value_ref[:, lanes]).astype(jnp.bfloat16))
    context = jnp.concatenate(pieces, axis=1)
    context_ref[...] = context
    partial_ref[...] = matmul(context, out_w_ref[...]).astype(jnp.bfloat16)


def attention_forward(whole, weights, position, own_length):
    w_in, w_pos, bias_pair, w_out = weights
    seq_len, model_width = whole.shape
    local_width = w_out.shape[0]
    heads_here = local_width // HEAD
    rows = 128
    full = pl.BlockSpec(memory_space=pltpu.VMEM)
    low = jnp.bfloat16
    return pl.pallas_call(
        functools.partial(attention_kernel, HEAD ** (-0.5)),
        grid=(seq_len // rows,),
        out_shape=[
            jax.ShapeDtypeStruct((seq_len, model_width), low),
            jax.ShapeDtypeStruct((heads_here, seq_len, seq_len), jnp.float32),
        ]
        + [jax.ShapeDtypeStruct((seq_len, local_width), low)] * 5,
        in_specs=[pl.BlockSpec(memory_space=pltpu.SMEM)] + [full] * 5,
        out_specs=[
            pl.BlockSpec((rows, model_width), lambda block: (block, 0)),
            pl.BlockSpec((heads_here, rows, seq_len), lambda block: (0, block, 0)),
            pl.BlockSpec((rows, local_width), lambda block: (block, 0)),
        ]
        + [full] * 4,
        compiler_params=pltpu.CompilerParams(vmem_limit_bytes=VMEM_LIMIT),
        name="attention_forward",
    )(own_length, whole, w_in, bias_pair.astype(jnp.float32), position, w_out)


def attention_back_kernel(
    scaling, grad_ref, out_w_ref, probs_ref, query_u_ref, query_v_ref, key_ref, value_ref,
    position_ref, d_projected_ref, d_position_ref, bias_ref, d_keys, d_values, d_places,
):
    block = pl.program_id(0)
    seq_len, local_width = key_ref.shape
    rows = grad_ref.shape[0]

    @pl.when(block == 0)
    def _():
        d_keys[...] = jnp.zeros_like(d_keys)
        d_values[...] = jnp.zeros_like(d_values)
        d_places[...] = jnp.zeros_like(d_places)
        bias_ref[...] = jnp.zeros_like(bias_ref)

    here = pl.ds(pl.multiple_of(block * rows, rows), rows)
    nearby = place_position(position_ref, block, rows, seq_len)
    d_nearby = place_position(d_places, block, rows, seq_len)
    upside = (
        lax.broadcasted_iota(jnp.int32, (rows, rows), 0)
        + lax.broadcasted_iota(jnp.int32, (rows, rows), 1)
        == rows - 1
    ).astype(jnp.bfloat16)
    d_context_all = contract_cols(grad_ref[...], out_w_ref[...]).astype(jnp.bfloat16)
    for head in range(local_width // HEAD):
        lanes = slice(head * HEAD, (head + 1) * HEAD)
        d_context = d_context_all[:, lanes]
        probs = probs_ref[head]
        d_probs = contract_cols(d_context, value_ref[:, lanes])
        inner = jnp.sum(probs * d_probs, axis=-1, keepdims=True)
        d_scores = (probs * (d_probs - inner)).astype(jnp.bfloat16)
        d_values[:, lanes] += contract_rows(probs.astype(jnp.bfloat16), d_context)
        d_keys[:, lanes] += contract_rows(d_scores, query_u_ref[here, lanes])
        grad_u = matmul(d_scores, key_ref[:, lanes]) * scaling
        turned = matmul(upside, d_scores)
        turned = jnp.concatenate([turned, jnp.zeros((rows, rows), jnp.float32)], axis=1)
        turned = pltpu.roll(turned, 0, 1, stride=1, stride_axis=0).astype(jnp.bfloat16)
        d_zeds = matmul(upside, turned).astype(jnp.bfloat16)
        grad_v = matmul(d_zeds, nearby[:, lanes]) * scaling
        d_nearby[:, lanes] += contract_rows(d_zeds, query_v_ref[here, lanes])
        d_projected_ref[here, lanes] = (grad_u + grad_v).astype(jnp.bfloat16)
        bias_ref[0:1, lanes] += jnp.sum(grad_u, axis=0, keepdims=True)
        bias_ref[1:2, lanes] += jnp.sum(grad_v, axis=0, keepdims=True)

    @pl.when(block == pl.num_programs(0) - 1)
    def _():
        d_projected_ref[:, local_width : 2 * local_width] = d_keys[...].astype(jnp.bfloat16)
        d_projected_ref[:, 2 * local_width :] = d_values[...].astype(jnp.bfloat16)
        d_position_ref[...] = d_places[...].astype(jnp.bfloat16)


def attention_backward(whole, weights, table_low, position, saved, grad_whole):
    w_in, w_pos, bias_pair, w_out = weights
    probs, context, query_u, query_v, key_rows, value_rows = saved
    seq_len, model_width = whole.shape
    local_width = w_out.shape[0]
    heads_here = local_width // HEAD
    rows = 128
    full = pl.BlockSpec(memory_space=pltpu.VMEM)
    d_projected, d_position, grad_bias = pl.pallas_call(
        functools.partial(attention_back_kernel, HEAD ** (-0.5)),
        grid=(seq_len // rows,),
        out_shape=[
            jax.ShapeDtypeStruct((seq_len, 3 * local_width), jnp.bfloat16),
            jax.ShapeDtypeStruct((2 * seq_len, local_width), jnp.bfloat16),
            jax.ShapeDtypeStruct((2, local_width), jnp.float32),
        ],
        in_specs=[
            pl.BlockSpec((rows, model_width), lambda block: (block, 0)),
            full,
            pl.BlockSpec((heads_here, rows, seq_len), lambda block: (0, block, 0)),
        ]
        + [full] * 5,
        out_specs=[full] * 3,
        scratch_shapes=[
            pltpu.VMEM((seq_len, local_width), jnp.float32),
            pltpu.VMEM((seq_len, local_width), jnp.float32),
            pltpu.VMEM((2 * seq_len, local_width), jnp.float32),
        ],
        compiler_params=pltpu.CompilerParams(vmem_limit_bytes=VMEM_LIMIT),
        name="attention_backward",
    )(grad_whole, w_out, probs, query_u, query_v, key_rows, value_rows, position)
    grad_in = contract_rows(whole, d_projected)
    d_normed = contract_cols(d_projected, w_in)
    grad_pos = contract_rows(table_low, d_position)
    grad_out = contract_rows(context, grad_whole)
    return (d_normed, grad_in, grad_pos, grad_bias, grad_out)


def conv_front(whole, w_in, kernel, mask_col):
    seq_len, model_width = whole.shape
    local_width = w_in.shape[2]
    glu_in = matmul(whole, w_in.reshape(model_width, 2 * local_width))
    gate_value = glu_in[:, :local_width]
    logistic = jax.nn.sigmoid(glu_in[:, local_width:])
    glu_out = gate_value * logistic * mask_col
    tap_count = kernel.shape[0]
    half_taps = (tap_count - 1) // 2
    padded = jnp.pad(glu_out, ((half_taps, half_taps), (0, 0)))
    kernel_float = kernel.astype(jnp.float32)
    conved = kernel_float[0] * padded[0:seq_len]
    for tap_index in range(1, tap_count):
        conved = conved + kernel_float[tap_index] * padded[tap_index : tap_index + seq_len]
    return (gate_value, logistic, padded, conved)


def batch_stats(conved, mask_col, frame_count):
    local_sum = jnp.sum(conved * mask_col, axis=0)
    local_squares = jnp.sum(conved * conved * mask_col, axis=0)
    total_sum, total_squares = dp_total(jnp.stack([local_sum, local_squares]))
    average = total_sum / frame_count
    variance = total_squares / frame_count - average * average
    return (average, lax.rsqrt(variance + batch_eps))


def conv_tail(conved, stats, bn_gain, bn_bias):
    average, inv_std = stats
    normed_b = (conved - average) * inv_std * bn_gain.astype(jnp.float32) + bn_bias.astype(
        jnp.float32
    )
    return (normed_b, jax.nn.silu(normed_b).astype(jnp.bfloat16))


def conv_backward(whole, weights, mask_col, stats, frame_count, grad_whole):
    w_in, kernel, bn_gain, bn_bias, w_out = weights
    seq_len, model_width = whole.shape
    local_width = w_in.shape[2]
    gate_value, logistic, padded, conved = conv_front(whole, w_in, kernel, mask_col)
    normed_b, active = conv_tail(conved, stats, bn_gain, bn_bias)
    average, inv_std = stats
    grad_out = contract_rows(active, grad_whole)
    d_normed = contract_cols(grad_whole, w_out) * silu_slope(normed_b)
    centred = (conved - average) * inv_std
    bias_total, gain_total = dp_total(
        jnp.stack([jnp.sum(d_normed, axis=0), jnp.sum(d_normed * centred, axis=0)])
    )
    d_conved = (
        bn_gain.astype(jnp.float32)
        * inv_std
        * (d_normed - mask_col * (bias_total + centred * gain_total) / frame_count)
    )
    tap_count = kernel.shape[0]
    half_taps = (tap_count - 1) // 2
    kernel_float = kernel.astype(jnp.float32)
    d_padded = jnp.pad(d_conved, ((half_taps, half_taps), (0, 0)))
    d_glu = kernel_float[0] * d_padded[tap_count - 1 : tap_count - 1 + seq_len]
    for tap_index in range(1, tap_count):
        d_glu = (
            d_glu
            + kernel_float[tap_index]
            * d_padded[tap_count - 1 - tap_index : tap_count - 1 - tap_index + seq_len]
        )
    grad_kernel = jnp.stack(
        [
            jnp.sum(d_conved * padded[tap_index : tap_index + seq_len], axis=0)
            for tap_index in range(tap_count)
        ]
    )
    d_glu = d_glu * mask_col
    d_pair = jnp.concatenate(
        [d_glu * logistic, d_glu * gate_value * logistic * (1.0 - logistic)], axis=1
    ).astype(jnp.bfloat16)
    grad_in = contract_rows(whole, d_pair).reshape(model_width, 2, local_width)
    d_normed_in = contract_cols(d_pair, w_in.reshape(model_width, 2 * local_width))
    return (d_normed_in, grad_in, grad_kernel, grad_out, gain_total, bias_total)


def body(
    frames_in,
    lengths,
    out_grad,
    norm_gains,
    ffn1_up,
    ffn1_down,
    attn_in,
    pos_proj,
    pos_bias,
    attn_out,
    conv_in,
    depthwise,
    bn_scale,
    bn_shift,
    conv_out,
    ffn2_up,
    ffn2_down,
):
    unused, local_rows, model_width = frames_in.shape
    seq_len = local_rows * lax.axis_size("mp")
    dp_index = lax.axis_index("dp")
    own_length = lax.dynamic_slice_in_dim(lengths, dp_index, 1)[0]
    valid_keys = jnp.arange(seq_len) < own_length
    mask_col = valid_keys.astype(jnp.float32)[:, None]
    frame_count = jnp.sum(lengths).astype(jnp.float32)
    frames = frames_in.reshape(local_rows, model_width)
    _, whole_first, ffn_first = open_step(
        open_middle, [frames, norm_gains], [ffn1_up, ffn1_down], (0, 1), 0
    )
    ffn_second = (
        lax.all_gather(ffn2_up, "dp", axis=0, tiled=True),
        lax.all_gather(ffn2_down, "dp", axis=1, tiled=True),
    )
    attn_in_whole = lax.all_gather(
        attn_in.reshape(attn_in.shape[0], -1), "dp", axis=0, tiled=True
    )
    conv_in_whole = lax.all_gather(conv_in, "dp", axis=0, tiled=True)
    small = jnp.concatenate([pos_bias, depthwise, bn_scale[None], bn_shift[None]], axis=0)
    table_low = position_table(seq_len, model_width).astype(jnp.bfloat16)
    if direct(model_width // lax.axis_size("dp")):
        packed = packed_rows(small)
    else:
        packed = small.T
    (after_first,), whole_attn, (pos_whole, attn_out_whole, conv_out_whole, packed) = between_step(
        functools.partial(forward_middle, 0.5, 1),
        ffn_forward(whole_first, ffn_first),
        [frames, norm_gains],
        1,
        fetch=[pos_proj, attn_out, conv_out, packed],
        dims=(0, 1, 1, 0),
        ways=(False, True, False, True),
    )
    if direct(model_width // lax.axis_size("dp")):
        small = whole_rows(packed, small)
    else:
        small = packed.T
    taps = depthwise.shape[0]
    attn_held = (attn_in_whole, pos_whole, small[:2], attn_out_whole)
    conv_held = (
        conv_in_whole,
        small[2 : 2 + taps],
        small[2 + taps],
        small[3 + taps],
        conv_out_whole,
    )
    position = matmul(table_low, pos_whole).astype(jnp.bfloat16)
    attn_partial, *attn_saved = attention_forward(
        whole_attn, attn_held, position, own_length[None]
    )
    (after_attn,), whole_conv, _ = between_step(
        functools.partial(forward_middle, 1.0, 2),
        attn_partial,
        [after_first, norm_gains],
        2,
    )
    gate_value, logistic, padded, conved = conv_front(
        whole_conv, conv_held[0], conv_held[1], mask_col
    )
    stats = batch_stats(conved, mask_col, frame_count)
    normed_b, active = conv_tail(conved, stats, conv_held[2], conv_held[3])
    (after_conv,), whole_second, _ = between_step(
        functools.partial(forward_middle, 1.0, 3),
        matmul(active, conv_held[4]),
        [after_attn, norm_gains],
        3,
    )
    (block_out, d_second, gain_five), whole_grads, _ = between_step(
        turn_middle,
        ffn_forward(whole_second, ffn_second),
        [after_conv, norm_gains, out_grad.reshape(local_rows, model_width)],
        4,
    )
    d_normed, grad_up, grad_down = ffn_backward(whole_second, ffn_second, whole_grads)
    (d_conv, gain_four), whole_grads, (total_up_two, total_down_two) = between_step(
        functools.partial(backward_middle, 1.0, 3),
        d_normed,
        [after_conv, norm_gains, d_second],
        5,
        grads=[grad_up, grad_down],
        dims=(0, 1),
        ways=(False, True),
    )
    d_normed, grad_conv_in, grad_kernel, grad_conv_out, gain_total, bias_total = conv_backward(
        whole_conv, conv_held, mask_col, stats, frame_count, whole_grads
    )
    (d_attn, gain_three), whole_grads, (total_conv_in, total_conv_out) = between_step(
        functools.partial(backward_middle, 1.0, 2),
        d_normed,
        [after_attn, norm_gains, d_conv],
        6,
        grads=[grad_conv_in.reshape(model_width, -1), grad_conv_out],
        dims=(0, 1),
        ways=(False, True),
    )
    d_normed, grad_attn_in, grad_pos, grad_bias, grad_attn_out = attention_backward(
        whole_attn, attn_held, table_low, position, attn_saved, whole_grads
    )
    (d_first, gain_two), whole_grads, (total_attn_in, total_attn_out, total_pos) = between_step(
        functools.partial(backward_middle, 0.5, 1),
        d_normed,
        [after_first, norm_gains, d_attn],
        7,
        grads=[grad_attn_in, grad_attn_out, grad_pos],
        dims=(0, 1, 0),
        ways=(False, True, True),
    )
    d_normed, grad_up, grad_down = ffn_backward(whole_first, ffn_first, whole_grads)
    (in_grad,), small_grads, gains, (total_up_one, total_down_one) = close_step(
        close_middle,
        d_normed,
        jnp.concatenate([grad_bias, grad_kernel], axis=0),
        jnp.concatenate([gain_two, gain_three, gain_four, gain_five], axis=0),
        [frames, norm_gains, d_first],
        [grad_up, grad_down],
        (0, 1),
        (False, True),
        8,
    )
    gain_sum = jnp.concatenate([gains[4:], gains[:4]], axis=0)
    block = model_width // lax.axis_size("dp")
    piece_len = bn_scale.shape[0]
    own = dp_index * piece_len
    small_grads = lax.dynamic_slice_in_dim(small_grads, own, piece_len, axis=1)
    return (
        block_out.reshape(1, local_rows, model_width),
        in_grad.reshape(1, local_rows, model_width),
        gain_sum,
        total_up_one,
        total_down_one,
        total_attn_in.reshape(block, 3, -1),
        total_pos,
        small_grads[:2],
        total_attn_out,
        total_conv_in.reshape(block, 2, -1),
        small_grads[2:],
        lax.dynamic_slice_in_dim(gain_total, own, piece_len),
        lax.dynamic_slice_in_dim(bias_total, own, piece_len),
        total_conv_out,
        total_up_two,
        total_down_two,
    )


def solution(mesh):
    placed = (
        P("dp", "mp", None),
        P(),
        P("dp", "mp", None),
        P(),
        P("dp", "mp"),
        P("mp", "dp"),
        P("dp", None, "mp"),
        P("dp", "mp"),
        P(None, ("mp", "dp")),
        P("mp", "dp"),
        P("dp", None, "mp"),
        P(None, ("mp", "dp")),
        P(("mp", "dp")),
        P(("mp", "dp")),
        P("mp", "dp"),
        P("dp", "mp"),
        P("mp", "dp"),
    )
    return jax.shard_map(
        body,
        mesh=mesh,
        in_specs=placed,
        out_specs=(
            P("dp", "mp", None),
            P("dp", "mp", None),
            P(),
            P("dp", "mp"),
            P("mp", "dp"),
            P("dp", None, "mp"),
            P("dp", "mp"),
            P(None, ("mp", "dp")),
            P("mp", "dp"),
            P("dp", None, "mp"),
            P(None, ("mp", "dp")),
            P(("mp", "dp")),
            P(("mp", "dp")),
            P("mp", "dp"),
            P("dp", "mp"),
            P("mp", "dp"),
        ),
        check_vma=False,
    )
```

```python
import functools
import math

import jax
import jax.numpy as jnp
from jax import lax
from jax.experimental import pallas as pl
from jax.experimental.pallas import tpu as pltpu
from jax.sharding import PartitionSpec as P

HEAD = 128


norm_eps = 1e-05
batch_eps = 1e-05
masked_score = -1000000000.0


def matmul(left, right):
    return jnp.dot(left, right, preferred_element_type=jnp.float32)


def contract_rows(left, right):
    return lax.dot_general(
        left, right, (((0,), (0,)), ((), ())), preferred_element_type=jnp.float32
    )


def contract_cols(left, right):
    return lax.dot_general(
        left, right, (((1,), (1,)), ((), ())), preferred_element_type=jnp.float32
    )


def layer_norm(values, norm_gain):
    average = jnp.mean(values, axis=-1, keepdims=True)
    centred = values - average
    inv_std = lax.rsqrt(jnp.mean(centred * centred, axis=-1, keepdims=True) + norm_eps)
    return centred * inv_std * norm_gain


def silu_slope(values):
    logistic = jax.nn.sigmoid(values)
    return logistic * (1.0 + values * (1.0 - logistic))


def position_table(seq_len, model_width):
    fine = 32
    lane = jnp.arange(model_width)
    frequency = jnp.exp((lane // 2).astype(jnp.float32) * (-2.0 * math.log(10000.0) / model_width))
    coarse = (seq_len - 1 - fine * jnp.arange(2 * seq_len // fine)).astype(jnp.float32)
    wide = coarse[:, None] * frequency[None, :]
    small = -jnp.arange(fine).astype(jnp.float32)[:, None] * frequency[None, :]
    even = (lane % 2 == 0)[None, :]
    wide_sin, wide_cos = jnp.sin(wide), jnp.cos(wide)
    high = jnp.where(even, wide_sin, wide_cos)
    side = jnp.where(even, wide_cos, -wide_sin)
    table = high[:, None, :] * jnp.cos(small)[None] + side[:, None, :] * jnp.sin(small)[None]
    return table.reshape(2 * seq_len, model_width)


MESH = pl.DeviceIdType.MESH
VMEM_LIMIT = 24 * 1024 * 1024
CHUNKS = 2


def line_copy(src, dst, sems, index, axis, target):
    return pltpu.make_async_remote_copy(
        src_ref=src,
        dst_ref=dst,
        send_sem=sems.at[0, index],
        recv_sem=sems.at[1, index],
        device_id={axis: target},
        device_id_type=MESH,
    )


def bit_of(index, bit):
    return lax.rem(lax.div(index, bit), 2)


def partner(index, bit):
    return index + bit - 2 * bit * bit_of(index, bit)


def cube_bits(size, swap):
    bits = []
    bit = 2
    while bit < size:
        bits.append(bit)
        bit *= 2
    if swap:
        bits.reverse()
    return bits + [1]


def block_at(ref, dim, index, width):
    start = pl.multiple_of(index * width, width)
    return ref.at[pl.ds(start, width)] if dim == 0 else ref.at[:, pl.ds(start, width)]


def all_total_kernel(axis, in_ref, out_ref, slots, sems):
    size = lax.axis_size(axis)
    me = lax.axis_index(axis)
    barrier = pltpu.get_barrier_semaphore()
    targets = [lax.rem(me + step, size) for step in range(1, size)]
    for target in targets:
        pl.semaphore_signal(barrier, inc=1, device_id={axis: target}, device_id_type=MESH)
    pl.semaphore_wait(barrier, size - 1)
    copies = []
    for number, target in enumerate(targets):
        copy = line_copy(in_ref, slots.at[me], sems, number, axis, target)
        copy.start()
        copies.append(copy)
    slots[me] = in_ref[...]
    for copy in copies:
        copy.wait_recv()
    total = slots[0]
    for source in range(1, size):
        total = total + slots[source]
    out_ref[...] = total
    for copy in copies:
        copy.wait_send()


def all_total(values, axis, collective_id):
    size = lax.axis_size(axis)
    return pl.pallas_call(
        functools.partial(all_total_kernel, axis),
        out_shape=jax.ShapeDtypeStruct(values.shape, values.dtype),
        in_specs=[pl.BlockSpec(memory_space=pltpu.VMEM)],
        out_specs=pl.BlockSpec(memory_space=pltpu.VMEM),
        scratch_shapes=[
            pltpu.VMEM((size, *values.shape), values.dtype),
            pltpu.SemaphoreType.DMA((2, size - 1)),
        ],
        compiler_params=pltpu.CompilerParams(
            collective_id=collective_id, has_side_effects=True
        ),
        name="all_total",
    )(values)


def line_peers(axis):
    me, size = lax.axis_index(axis), lax.axis_size(axis)
    return jnp.minimum(me, 1) + jnp.minimum(size - 1 - me, 1)


def greet(line_axis, cube_axis, everyone):
    me, size = lax.axis_index(line_axis), lax.axis_size(line_axis)
    barrier = pltpu.get_barrier_semaphore()
    if everyone:
        for axis in (line_axis, cube_axis):
            here, count = lax.axis_index(axis), lax.axis_size(axis)
            for step in range(1, count):
                pl.semaphore_signal(
                    barrier, inc=1, device_id={axis: lax.rem(here + step, count)},
                    device_id_type=MESH,
                )
        pl.semaphore_wait(barrier, size - 1 + lax.axis_size(cube_axis) - 1)
        return

    @pl.when(me > 0)
    def _():
        pl.semaphore_signal(barrier, inc=1, device_id={line_axis: me - 1}, device_id_type=MESH)

    @pl.when(me < size - 1)
    def _():
        pl.semaphore_signal(barrier, inc=1, device_id={line_axis: me + 1}, device_id_type=MESH)

    bits = cube_bits(lax.axis_size(cube_axis), False) if cube_axis else []
    for bit in bits:
        pl.semaphore_signal(
            barrier, inc=1, device_id={cube_axis: partner(lax.axis_index(cube_axis), bit)},
            device_id_type=MESH,
        )
    pl.semaphore_wait(barrier, line_peers(line_axis) + len(bits))


class LineGather:
    def __init__(self, axis, out_ref, sems, chunks):
        self.axis, self.out, self.sems, self.chunks = axis, out_ref, sems, chunks
        self.size, self.me = lax.axis_size(axis), lax.axis_index(axis)
        self.rows = out_ref.shape[0] // self.size
        self.part = self.rows // chunks
        self.steps = self.size - 1

    def piece(self, index, chunk):
        start = pl.multiple_of(index * self.rows + chunk * self.part, self.part)
        return self.out.at[pl.ds(start, self.part)]

    def copy(self, way, step, index, chunk):
        place = self.piece(index, chunk)
        return line_copy(
            place, place, self.sems, (way * self.steps + step) * self.chunks + chunk, self.axis,
            self.me + 1 if way == 0 else self.me - 1,
        )

    def index(self, way, step):
        return self.me - step if way == 0 else self.me + step

    def held(self, way, step):
        return self.me >= step if way == 0 else self.me + step < self.size

    def onward(self, way):
        return self.me + 1 < self.size if way == 0 else self.me > 0

    def step(self, step, chunk):
        for way in range(2):
            if step > 0:
                @pl.when(self.held(way, step))
                def _():
                    self.copy(way, step - 1, self.index(way, step), chunk).wait_recv()

            if step < self.steps:
                @pl.when(jnp.logical_and(self.held(way, step), self.onward(way)))
                def _():
                    self.copy(way, step, self.index(way, step), chunk).start()

    def finish(self):
        for chunk in range(self.chunks):
            for step in range(self.steps):
                for way in range(2):
                    @pl.when(jnp.logical_and(self.held(way, step), self.onward(way)))
                    def _():
                        self.copy(way, step, self.index(way, step), chunk).wait_send()


class LineScatter:
    def __init__(self, axis, in_ref, total_ref, slots, staged, sems, chunks):
        self.axis, self.ins, self.total, self.chunks = axis, in_ref, total_ref, chunks
        self.slots, self.staged, self.sems = slots, staged, sems
        self.size, self.me = lax.axis_size(axis), lax.axis_index(axis)
        self.rows = total_ref.shape[0]
        self.part = self.rows // chunks
        self.first_way = lax.div(self.me, (self.size + 1) // 2)

    def mine(self, owner, chunk):
        start = pl.multiple_of(owner * self.rows + chunk * self.part, self.part)
        return self.ins.at[pl.ds(start, self.part)]

    def lines(self, chunk):
        return slice(chunk * self.part, (chunk + 1) * self.part)

    def copy(self, way, owner, chunk, src):
        return line_copy(
            src, self.slots.at[way, owner, self.lines(chunk)], self.sems,
            (way * self.size + owner) * self.chunks + chunk, self.axis,
            self.me + 1 - 2 * way,
        )

    def arrived(self, way, owner, chunk):
        return self.copy(way, owner, chunk, self.staged.at[way, owner, self.lines(chunk)])

    def place(self, way, step):
        owner = (1 - way) * (self.size - 1 - step) + way * step
        distance = (owner - self.me) * (1 - 2 * way)
        behind = (1 - way) * self.me + way * (self.size - 1 - self.me)
        return owner, distance, behind

    def lead(self, step, chunk):
        for way in range(2):
            owner, distance, behind = self.place(way, step)

            @pl.when(jnp.logical_and(distance > 0, behind == 0))
            def _():
                self.copy(way, owner, chunk, self.mine(owner, chunk)).start()

    def hop(self, way, step, chunk):
        owner, distance, behind = self.place(way, step)

        @pl.when(jnp.logical_and(distance > 0, behind > 0))
        def _():
            lines = self.lines(chunk)
            self.arrived(way, owner, chunk).wait_recv()
            self.staged[way, owner, lines] = (
                self.mine(owner, chunk)[...].astype(jnp.float32)
                + self.slots[way, owner, lines].astype(jnp.float32)
            ).astype(self.staged.dtype)
            self.arrived(way, owner, chunk).start()

    def run(self, halfway=None):
        marks = [(step, chunk) for step in range(self.size - 1) for chunk in range(self.chunks)]
        for mark in marks:
            self.lead(*mark)
        for number in range(len(marks) + self.chunks):
            if halfway and number == len(marks) // 2 + 1:
                halfway()
            if number < len(marks):
                self.hop(self.first_way, *marks[number])
            if number >= self.chunks:
                self.hop(1 - self.first_way, *marks[number - self.chunks])

    def result(self, chunk):
        lines = self.lines(chunk)
        self.total[lines] = self.mine(self.me, chunk)[...].astype(jnp.float32)
        for way in range(2):
            @pl.when(self.me > 0 if way == 0 else self.me < self.size - 1)
            def _():
                self.arrived(way, self.me, chunk).wait_recv()
                self.total[lines] += self.slots[way, self.me, lines].astype(jnp.float32)

        return self.total[lines]

    def finish(self):
        for chunk in range(self.chunks):
            for owner in range(self.size):
                for way in range(2):
                    @pl.when(self.me < owner if way == 0 else self.me > owner)
                    def _():
                        self.arrived(way, owner, chunk).wait_send()


class CubeGather:
    def __init__(self, axis, dims, ways, ins, outs, sems):
        self.axis, self.dims, self.ways = axis, dims, ways
        self.ins, self.outs, self.sems = ins, outs, sems
        self.size, self.me = lax.axis_size(axis), lax.axis_index(axis)
        self.stages = len(cube_bits(self.size, False))
        self.started = []
        self.waiting = [[] for _ in ins]

    def step(self, stage):
        per = self.size - 1
        for which in range(len(self.ins)):
            width = self.ins[which].shape[self.dims[which]]
            bits = cube_bits(self.size, self.ways[which])
            for copy in self.waiting[which]:
                copy.wait_recv()
            self.waiting[which] = []
            if stage == 0:
                block_at(self.outs[which], self.dims[which], self.me, width)[...] = (
                    self.ins[which][...]
                )
            if stage == self.stages:
                continue
            held = [self.me]
            for bit in bits[:stage]:
                held = held + [partner(index, bit) for index in held]
            for number, index in enumerate(held):
                place = block_at(self.outs[which], self.dims[which], index, width)
                copy = line_copy(
                    self.ins[which] if stage == 0 else place, place, self.sems,
                    which * per + 2**stage - 1 + number, self.axis, partner(self.me, bits[stage]),
                )
                copy.start()
                self.waiting[which].append(copy)
            self.started.extend(self.waiting[which])

    def finish(self):
        for copy in self.started:
            copy.wait_send()


class CubeScatter:
    def __init__(self, axis, dims, ways, ins, outs, slots, sems):
        self.axis, self.dims, self.ways = axis, dims, ways
        self.ins, self.outs, self.slots, self.sems = ins, outs, slots, sems
        self.size, self.me = lax.axis_size(axis), lax.axis_index(axis)
        self.stages = len(cube_bits(self.size, False))
        self.started = []

    def slot(self, which, stage, number):
        return self.slots[which].at[self.size - self.size // 2**stage + number]

    def sets(self, which, stage):
        bits = cube_bits(self.size, self.ways[which])[::-1]
        held = [self.me]
        for bit in bits[stage + 1 :]:
            held = held + [partner(index, bit) for index in held]
        return bits[stage], held

    def send(self, which, stage):
        width = self.outs[which].shape[self.dims[which]]
        bit, held = self.sets(which, stage)
        for number, index in enumerate(held):
            if stage == 0:
                src = block_at(self.ins[which], self.dims[which], partner(index, bit), width)
            else:
                src = self.slot(which, stage - 1, 2 * number + 1)
            copy = line_copy(
                src, self.slot(which, stage, number), self.sems,
                which * (self.size - 1) + self.size - self.size // 2**stage + number,
                self.axis, partner(self.me, bit),
            )
            copy.start()
            self.started.append((which, stage, copy))

    def receive(self, which, stage):
        width = self.outs[which].shape[self.dims[which]]
        _, held = self.sets(which, stage)
        for copy in [c for w, s, c in self.started if (w, s) == (which, stage)]:
            copy.wait_recv()
        for number, index in enumerate(held):
            got = self.slot(which, stage, number)
            if stage == 0:
                mine = block_at(self.ins[which], self.dims[which], index, width)
            else:
                mine = self.slot(which, stage - 1, 2 * number)
            total = got[...].astype(jnp.float32) + mine[...].astype(jnp.float32)
            if stage == self.stages - 1:
                self.outs[which][...] = total
            else:
                got[...] = total.astype(self.slots[which].dtype)

    def step(self, stage):
        for which in range(len(self.ins)):
            if stage > 0:
                self.receive(which, stage - 1)
            if stage < self.stages:
                self.send(which, stage)

    def finish(self):
        for _, _, copy in self.started:
            copy.wait_send()


class AllTotal:
    def __init__(self, axis, slots, sems):
        self.axis, self.slots, self.sems = axis, slots, sems
        self.size, self.me = lax.axis_size(axis), lax.axis_index(axis)
        self.copies = []

    def start(self):
        for step in range(1, self.size):
            copy = line_copy(
                self.slots.at[self.me], self.slots.at[self.me], self.sems, step - 1, self.axis,
                lax.rem(self.me + step, self.size),
            )
            copy.start()
            self.copies.append(copy)

    def result(self):
        for copy in self.copies:
            copy.wait_recv()
        total = self.slots[0]
        for source in range(1, self.size):
            total = total + self.slots[source]
        return total

    def finish(self):
        for copy in self.copies:
            copy.wait_send()


def open_kernel(middle, counts, chunks, dims, ways, *refs):
    local_count, mid_count = counts
    count = len(dims)
    refs = list(refs)
    take = lambda number: [refs.pop(0) for _ in range(number)]
    locals_, ins = take(local_count), take(count)
    mids, (whole,), outs = take(mid_count), take(1), take(count)
    gather_sems, cube_sems = refs
    fetch = CubeGather("dp", dims, ways, ins, outs, cube_sems)
    rows = LineGather("mp", whole, gather_sems, chunks)
    greet("mp", "dp", False)
    fetch.step(0)
    values, normed = middle(None, *[ref[...] for ref in locals_])
    for ref, value in zip(mids, values):
        ref[...] = value
    for chunk in range(chunks):
        part = rows.part
        rows.piece(rows.me, chunk)[...] = normed[chunk * part : (chunk + 1) * part]
        rows.step(0, chunk)
    for step in range(1, max(rows.steps, fetch.stages) + 1):
        if step <= fetch.stages:
            fetch.step(step)
        if step <= rows.steps:
            for chunk in range(chunks):
                rows.step(step, chunk)
    rows.finish()
    fetch.finish()


def between_kernel(middle, counts, chunks, fetches, dims, ways, *refs):
    local_count, mid_count = counts
    count = len(dims)
    refs = list(refs)
    take = lambda number: [refs.pop(0) for _ in range(number)]
    (partial,), locals_, ins = take(1), take(local_count), take(count)
    mids, (whole,), outs = take(mid_count), take(1), take(count)
    (total, slots, staged, scatter_sems, gather_sems), refs = refs[:5], refs[5:]
    sums = LineScatter("mp", partial, total, slots, staged, scatter_sems, chunks)
    rows = LineGather("mp", whole, gather_sems, chunks)
    beside, stages = None, 0
    if count:
        if fetches:
            beside = CubeGather("dp", dims, ways, ins, outs, refs[0])
        else:
            beside = CubeScatter("dp", dims, ways, ins, outs, refs[:count], refs[count])
        stages = beside.stages + 1
    greet("mp", "dp" if count else None, False)
    stage = 0
    if stages:
        beside.step(0)
        sums.run(lambda: beside.step(1))
        stage = 2
    else:
        sums.run()
    for chunk in range(chunks):
        lines = sums.lines(chunk)
        picked = [ref[lines] if ref.shape[0] == sums.rows else ref[...] for ref in locals_]
        values, normed = middle(sums.result(chunk), *picked)
        rows.piece(rows.me, chunk)[...] = normed
        rows.step(0, chunk)
        for ref, value in zip(mids, values):
            if ref.shape[0] == sums.rows:
                ref[lines] = value
            elif chunk == 0:
                ref[...] = value
            else:
                ref[...] += value
    for step in range(1, rows.steps + 1):
        if stage < stages:
            beside.step(stage)
            stage += 1
        for chunk in range(chunks):
            rows.step(step, chunk)
    for stage in range(stage, stages):
        beside.step(stage)
    if count:
        beside.finish()
    sums.finish()
    rows.finish()


def close_kernel(middle, counts, chunks, dims, ways, *refs):
    local_count, mid_count = counts
    count = len(dims)
    refs = list(refs)
    take = lambda number: [refs.pop(0) for _ in range(number)]
    (partial, small, gains), locals_, ins = take(3), take(local_count), take(count)
    mids, (small_out, gains_out), outs = take(mid_count), take(2), take(count)
    (total, slots, staged, scatter_sems), refs = refs[:4], refs[4:]
    (small_slots, small_sems, gain_slots, gain_sems, last_slots, last_sems), refs = refs[:6], refs[6:]
    sums = LineScatter("mp", partial, total, slots, staged, scatter_sems, chunks)
    grads = CubeScatter("dp", dims, ways, ins, outs, refs[:count], refs[count])
    little = AllTotal("dp", small_slots, small_sems)
    near, far = AllTotal("dp", gain_slots, gain_sems), AllTotal("mp", last_slots, last_sems)
    little.slots[little.me] = small[...]
    greet("mp", "dp", True)
    little.start()
    grads.step(0)
    sums.run(lambda: grads.step(1))
    total_rows = jnp.concatenate([sums.result(chunk) for chunk in range(chunks)], axis=0)
    values, gain = middle(total_rows, *[ref[...] for ref in locals_])
    near.slots[near.me] = jnp.concatenate([gains[...], gain], axis=0)
    near.start()
    for ref, value in zip(mids, values):
        ref[...] = value
    grads.step(2)
    far.slots[far.me] = near.result()
    far.start()
    for stage in range(3, grads.stages + 1):
        grads.step(stage)
    small_out[...] = little.result()
    gains_out[...] = far.result()
    for task in (grads, sums, little, near, far):
        task.finish()


def shapes_of(arrays):
    return [jax.ShapeDtypeStruct(value.shape, value.dtype) for value in arrays]


def call_step(kernel, inputs, out_shape, scratch, collective_id, name):
    vmem = pl.BlockSpec(memory_space=pltpu.VMEM)
    return pl.pallas_call(
        kernel,
        out_shape=out_shape,
        in_specs=[vmem] * len(inputs),
        out_specs=[vmem] * len(out_shape),
        scratch_shapes=scratch,
        compiler_params=pltpu.CompilerParams(
            collective_id=collective_id, has_side_effects=True, vmem_limit_bytes=VMEM_LIMIT
        ),
        name=name,
    )(*inputs)


def line_scratch(rows, width, chunks):
    size = lax.axis_size("mp")
    return [
        pltpu.VMEM((rows, width), jnp.float32),
        pltpu.VMEM((2, size, rows, width), jnp.bfloat16),
        pltpu.VMEM((2, size, rows, width), jnp.bfloat16),
        pltpu.SemaphoreType.DMA((2, 2 * size * chunks)),
    ]


def cube_scratch(arrays, dims):
    size = lax.axis_size("dp")
    shapes, slots = [], []
    for array, dim in zip(arrays, dims):
        shape = list(array.shape)
        shape[dim] //= size
        shapes.append(jax.ShapeDtypeStruct(tuple(shape), jnp.float32))
        slots.append(pltpu.VMEM((size - 1, *shape), array.dtype))
    if arrays:
        slots.append(pltpu.SemaphoreType.DMA((2, len(arrays) * (size - 1))))
    return shapes, slots


def plain_totals(grads, dims):
    return [
        lax.psum_scatter(grad, "dp", scatter_dimension=dim, tiled=True).astype(jnp.float32)
        for grad, dim in zip(grads, dims)
    ]


def direct(block):
    size = lax.axis_size("dp")
    return size & (size - 1) == 0 and block % 128 == 0


def fetched_shapes(arrays, dims):
    size, shapes = lax.axis_size("dp"), []
    for array, dim in zip(arrays, dims):
        shape = list(array.shape)
        shape[dim] *= size
        shapes.append(jax.ShapeDtypeStruct(tuple(shape), array.dtype))
    return shapes


def plain_fetch(arrays, dims):
    return [lax.all_gather(array, "dp", axis=dim, tiled=True) for array, dim in zip(arrays, dims)]


def packed_rows(small):
    return jnp.pad(small, ((0, 16 - small.shape[0]), (0, 128 - small.shape[1])))


def whole_rows(packed, small):
    size, (count, lanes) = lax.axis_size("dp"), small.shape
    packed = packed.reshape(size, 16, 128)[:, :count, :lanes]
    return packed.transpose(1, 0, 2).reshape(count, size * lanes)


def open_step(middle, locals_, arrays, dims, collective_id):
    if not direct(arrays[0].shape[dims[0]]):
        mids, normed = middle(None, *locals_)
        return mids, lax.all_gather(normed, "mp", axis=0, tiled=True), plain_fetch(arrays, dims)
    ways = [index % 2 == 1 for index in range(len(dims))]
    mid_shapes, normed_shape = jax.eval_shape(functools.partial(middle, None), *locals_)
    rows, width = normed_shape.shape
    whole_shape = jax.ShapeDtypeStruct((rows * lax.axis_size("mp"), width), normed_shape.dtype)
    count = len(mid_shapes)
    result = call_step(
        functools.partial(open_kernel, middle, (len(locals_), count), CHUNKS, dims, ways),
        [*locals_, *arrays],
        [*mid_shapes, whole_shape, *fetched_shapes(arrays, dims)],
        [
            pltpu.SemaphoreType.DMA((2, 2 * (lax.axis_size("mp") - 1) * CHUNKS)),
            pltpu.SemaphoreType.DMA((2, len(arrays) * (lax.axis_size("dp") - 1))),
        ],
        collective_id,
        "open_step",
    )
    return result[:count], result[count], result[count + 1 :]


def between_step(
    middle, partial_value, locals_, collective_id, grads=(), fetch=(), dims=(), ways=()
):
    partial_value = partial_value.astype(jnp.bfloat16)
    grads = [grad.astype(jnp.bfloat16) for grad in grads]
    size = lax.axis_size("mp")
    rows, width = partial_value.shape[0] // size, partial_value.shape[1]
    if not direct(width // lax.axis_size("dp")):
        total = lax.psum_scatter(partial_value, "mp", scatter_dimension=0, tiled=True)
        mids, normed = middle(total.astype(jnp.float32), *locals_)
        others = plain_fetch(fetch, dims) if fetch else plain_totals(grads, dims)
        return mids, lax.all_gather(normed, "mp", axis=0, tiled=True), others
    total = jax.ShapeDtypeStruct((rows, width), jnp.float32)
    mid_shapes, normed_shape = jax.eval_shape(middle, total, *locals_)
    if fetch:
        shapes = fetched_shapes(fetch, dims)
        scratch = [pltpu.SemaphoreType.DMA((2, len(fetch) * (lax.axis_size("dp") - 1)))]
    else:
        shapes, scratch = cube_scratch(grads, dims)
    count = len(mid_shapes)
    result = call_step(
        functools.partial(
            between_kernel, middle, (len(locals_), count), CHUNKS, bool(fetch), dims, ways
        ),
        [partial_value, *locals_, *grads, *fetch],
        [
            *mid_shapes,
            jax.ShapeDtypeStruct((rows * size, width), normed_shape.dtype),
            *shapes,
        ],
        line_scratch(rows, width, CHUNKS)
        + [pltpu.SemaphoreType.DMA((2, 2 * (size - 1) * CHUNKS))]
        + scratch,
        collective_id,
        "between_step",
    )
    return result[:count], result[count], result[count + 1 :]


def close_step(middle, partial_value, small, gains, locals_, grads, dims, ways, collective_id):
    partial_value = partial_value.astype(jnp.bfloat16)
    grads = [grad.astype(jnp.bfloat16) for grad in grads]
    size, dp_size = lax.axis_size("mp"), lax.axis_size("dp")
    rows, width = partial_value.shape[0] // size, partial_value.shape[1]
    if not direct(width // dp_size):
        total = lax.psum_scatter(partial_value, "mp", scatter_dimension=0, tiled=True)
        mids, gain = middle(total.astype(jnp.float32), *locals_)
        gains = lax.psum(jnp.concatenate([gains, gain], axis=0), ("dp", "mp"))
        return mids, lax.psum(small, "dp"), gains, plain_totals(grads, dims)
    total = jax.ShapeDtypeStruct((rows, width), jnp.float32)
    mid_shapes, gain_shape = jax.eval_shape(middle, total, *locals_)
    gains_shape = jax.ShapeDtypeStruct((gains.shape[0] + 1, width), jnp.float32)
    shapes, slots = cube_scratch(grads, dims)
    count = len(mid_shapes)
    result = call_step(
        functools.partial(close_kernel, middle, (len(locals_), count), CHUNKS, dims, ways),
        [partial_value, small, gains, *locals_, *grads],
        [*mid_shapes, *shapes_of([small]), gains_shape, *shapes],
        line_scratch(rows, width, CHUNKS)
        + [
            pltpu.VMEM((dp_size, *small.shape), jnp.float32),
            pltpu.SemaphoreType.DMA((2, dp_size - 1)),
            pltpu.VMEM((dp_size, *gains_shape.shape), jnp.float32),
            pltpu.SemaphoreType.DMA((2, dp_size - 1)),
            pltpu.VMEM((size, *gains_shape.shape), jnp.float32),
            pltpu.SemaphoreType.DMA((2, size - 1)),
        ]
        + slots,
        collective_id,
        "close_step",
    )
    return result[:count], result[count], result[count + 1], result[count + 2 :]


def forward_middle(scale, row, total, residual, norm_gains):
    residual = residual.astype(jnp.float32)
    if total is not None:
        residual = residual + scale * total
    return [residual], layer_norm(residual, norm_gains[row : row + 1]).astype(jnp.bfloat16)


def open_middle(total, frames, norm_gains):
    return [], layer_norm(frames.astype(jnp.float32), norm_gains[0:1]).astype(jnp.bfloat16)


def norm_back(values, norm_gain, upstream):
    centred = values - jnp.mean(values, axis=-1, keepdims=True)
    inv_std = lax.rsqrt(jnp.mean(centred * centred, axis=-1, keepdims=True) + norm_eps)
    normed = centred * inv_std
    scaled = upstream * norm_gain
    d_values = inv_std * (
        scaled
        - jnp.mean(scaled, axis=-1, keepdims=True)
        - normed * jnp.mean(scaled * normed, axis=-1, keepdims=True)
    )
    return d_values, jnp.sum(upstream * normed, axis=0, keepdims=True)


def turn_middle(total, residual, norm_gains, out_grad):
    after = residual + 0.5 * total
    gain = norm_gains[4:5]
    d_after, d_gain = norm_back(after, gain, out_grad.astype(jnp.float32))
    block_out = layer_norm(after, gain).astype(jnp.bfloat16)
    return [block_out, d_after, d_gain], (0.5 * d_after).astype(jnp.bfloat16)


def backward_middle(scale, row, total, values, norm_gains, upstream):
    d_branch, d_gain = norm_back(values.astype(jnp.float32), norm_gains[row : row + 1], total)
    d_values = upstream + d_branch
    return [d_values, d_gain], (scale * d_values).astype(jnp.bfloat16)


def close_middle(total, values, norm_gains, upstream):
    d_branch, d_gain = norm_back(values.astype(jnp.float32), norm_gains[0:1], total)
    return [upstream + d_branch], d_gain


def dp_total(values):
    if direct(128):
        return all_total(values, "dp", 9)
    return lax.psum(values, "dp")


def ffn_forward(whole, weights):
    w_up, w_down = weights
    hidden = matmul(whole, w_up)
    return matmul(jax.nn.silu(hidden).astype(jnp.bfloat16), w_down)


def ffn_backward(whole, weights, grad_whole):
    w_up, w_down = weights
    hidden = matmul(whole, w_up)
    active = jax.nn.silu(hidden).astype(jnp.bfloat16)
    grad_down = contract_rows(active, grad_whole)
    d_hidden = (contract_cols(grad_whole, w_down) * silu_slope(hidden)).astype(jnp.bfloat16)
    grad_up = contract_rows(whole, d_hidden)
    return (contract_cols(d_hidden, w_up), grad_up, grad_down)


def place_position(position_ref, block, rows, seq_len):
    start = pl.multiple_of(seq_len - rows - block * rows, rows)
    return position_ref.at[pl.ds(start, seq_len + rows)]


def attention_kernel(
    scaling, length_ref, whole_ref, in_ref, bias_ref, position_ref, out_w_ref,
    partial_ref, probs_ref, context_ref, query_u_ref, query_v_ref, key_ref, value_ref,
):
    block = pl.program_id(0)
    seq_len, local_width = key_ref.shape
    rows = partial_ref.shape[0]

    @pl.when(block == 0)
    def _():
        projected = matmul(whole_ref[...], in_ref[...])
        queries = projected[:, :local_width]
        query_u_ref[...] = ((queries + bias_ref[0:1]) * scaling).astype(jnp.bfloat16)
        query_v_ref[...] = ((queries + bias_ref[1:2]) * scaling).astype(jnp.bfloat16)
        key_ref[...] = projected[:, local_width : 2 * local_width].astype(jnp.bfloat16)
        value_ref[...] = projected[:, 2 * local_width :].astype(jnp.bfloat16)

    here = pl.ds(pl.multiple_of(block * rows, rows), rows)
    valid = lax.broadcasted_iota(jnp.int32, (rows, seq_len), 1) < length_ref[0]
    nearby = place_position(position_ref, block, rows, seq_len)
    pieces = []
    for head in range(local_width // HEAD):
        lanes = slice(head * HEAD, (head + 1) * HEAD)
        content = contract_cols(query_u_ref[here, lanes], key_ref[:, lanes])
        zeds = contract_cols(query_v_ref[here, lanes], nearby[:, lanes])
        shifted = pltpu.roll(zeds, seq_len + 1, 1, stride=1, stride_axis=0)[:, :seq_len]
        scores = jnp.where(valid, content + shifted, masked_score)
        exponent = jnp.exp(scores - jnp.max(scores, axis=-1, keepdims=True))
        probs = exponent / jnp.sum(exponent, axis=-1, keepdims=True)
        probs_ref[head] = probs
        pieces.append(matmul(probs.astype(jnp.bfloat16), value_ref[:, lanes]).astype(jnp.bfloat16))
    context = jnp.concatenate(pieces, axis=1)
    context_ref[...] = context
    partial_ref[...] = matmul(context, out_w_ref[...]).astype(jnp.bfloat16)


def attention_forward(whole, weights, position, own_length):
    w_in, w_pos, bias_pair, w_out = weights
    seq_len, model_width = whole.shape
    local_width = w_out.shape[0]
    heads_here = local_width // HEAD
    rows = 128
    full = pl.BlockSpec(memory_space=pltpu.VMEM)
    low = jnp.bfloat16
    return pl.pallas_call(
        functools.partial(attention_kernel, HEAD ** (-0.5)),
        grid=(seq_len // rows,),
        out_shape=[
            jax.ShapeDtypeStruct((seq_len, model_width), low),
            jax.ShapeDtypeStruct((heads_here, seq_len, seq_len), jnp.float32),
        ]
        + [jax.ShapeDtypeStruct((seq_len, local_width), low)] * 5,
        in_specs=[pl.BlockSpec(memory_space=pltpu.SMEM)] + [full] * 5,
        out_specs=[
            pl.BlockSpec((rows, model_width), lambda block: (block, 0)),
            pl.BlockSpec((heads_here, rows, seq_len), lambda block: (0, block, 0)),
            pl.BlockSpec((rows, local_width), lambda block: (block, 0)),
        ]
        + [full] * 4,
        compiler_params=pltpu.CompilerParams(vmem_limit_bytes=VMEM_LIMIT),
        name="attention_forward",
    )(own_length, whole, w_in, bias_pair.astype(jnp.float32), position, w_out)


def attention_back_kernel(
    scaling, grad_ref, out_w_ref, probs_ref, query_u_ref, query_v_ref, key_ref, value_ref,
    position_ref, d_projected_ref, d_position_ref, bias_ref, d_keys, d_values, d_places,
):
    block = pl.program_id(0)
    seq_len, local_width = key_ref.shape
    rows = grad_ref.shape[0]

    @pl.when(block == 0)
    def _():
        d_keys[...] = jnp.zeros_like(d_keys)
        d_values[...] = jnp.zeros_like(d_values)
        d_places[...] = jnp.zeros_like(d_places)
        bias_ref[...] = jnp.zeros_like(bias_ref)

    here = pl.ds(pl.multiple_of(block * rows, rows), rows)
    nearby = place_position(position_ref, block, rows, seq_len)
    d_nearby = place_position(d_places, block, rows, seq_len)
    upside = (
        lax.broadcasted_iota(jnp.int32, (rows, rows), 0)
        + lax.broadcasted_iota(jnp.int32, (rows, rows), 1)
        == rows - 1
    ).astype(jnp.bfloat16)
    d_context_all = contract_cols(grad_ref[...], out_w_ref[...]).astype(jnp.bfloat16)
    for head in range(local_width // HEAD):
        lanes = slice(head * HEAD, (head + 1) * HEAD)
        d_context = d_context_all[:, lanes]
        probs = probs_ref[head]
        d_probs = contract_cols(d_context, value_ref[:, lanes])
        inner = jnp.sum(probs * d_probs, axis=-1, keepdims=True)
        d_scores = (probs * (d_probs - inner)).astype(jnp.bfloat16)
        d_values[:, lanes] += contract_rows(probs.astype(jnp.bfloat16), d_context)
        d_keys[:, lanes] += contract_rows(d_scores, query_u_ref[here, lanes])
        grad_u = matmul(d_scores, key_ref[:, lanes]) * scaling
        turned = matmul(upside, d_scores)
        turned = jnp.concatenate([turned, jnp.zeros((rows, rows), jnp.float32)], axis=1)
        turned = pltpu.roll(turned, 0, 1, stride=1, stride_axis=0).astype(jnp.bfloat16)
        d_zeds = matmul(upside, turned).astype(jnp.bfloat16)
        grad_v = matmul(d_zeds, nearby[:, lanes]) * scaling
        d_nearby[:, lanes] += contract_rows(d_zeds, query_v_ref[here, lanes])
        d_projected_ref[here, lanes] = (grad_u + grad_v).astype(jnp.bfloat16)
        bias_ref[0:1, lanes] += jnp.sum(grad_u, axis=0, keepdims=True)
        bias_ref[1:2, lanes] += jnp.sum(grad_v, axis=0, keepdims=True)

    @pl.when(block == pl.num_programs(0) - 1)
    def _():
        d_projected_ref[:, local_width : 2 * local_width] = d_keys[...].astype(jnp.bfloat16)
        d_projected_ref[:, 2 * local_width :] = d_values[...].astype(jnp.bfloat16)
        d_position_ref[...] = d_places[...].astype(jnp.bfloat16)


def attention_backward(whole, weights, table_low, position, saved, grad_whole):
    w_in, w_pos, bias_pair, w_out = weights
    probs, context, query_u, query_v, key_rows, value_rows = saved
    seq_len, model_width = whole.shape
    local_width = w_out.shape[0]
    heads_here = local_width // HEAD
    rows = 128
    full = pl.BlockSpec(memory_space=pltpu.VMEM)
    d_projected, d_position, grad_bias = pl.pallas_call(
        functools.partial(attention_back_kernel, HEAD ** (-0.5)),
        grid=(seq_len // rows,),
        out_shape=[
            jax.ShapeDtypeStruct((seq_len, 3 * local_width), jnp.bfloat16),
            jax.ShapeDtypeStruct((2 * seq_len, local_width), jnp.bfloat16),
            jax.ShapeDtypeStruct((2, local_width), jnp.float32),
        ],
        in_specs=[
            pl.BlockSpec((rows, model_width), lambda block: (block, 0)),
            full,
            pl.BlockSpec((heads_here, rows, seq_len), lambda block: (0, block, 0)),
        ]
        + [full] * 5,
        out_specs=[full] * 3,
        scratch_shapes=[
            pltpu.VMEM((seq_len, local_width), jnp.float32),
            pltpu.VMEM((seq_len, local_width), jnp.float32),
            pltpu.VMEM((2 * seq_len, local_width), jnp.float32),
        ],
        compiler_params=pltpu.CompilerParams(vmem_limit_bytes=VMEM_LIMIT),
        name="attention_backward",
    )(grad_whole, w_out, probs, query_u, query_v, key_rows, value_rows, position)
    grad_in = contract_rows(whole, d_projected)
    d_normed = contract_cols(d_projected, w_in)
    grad_pos = contract_rows(table_low, d_position)
    grad_out = contract_rows(context, grad_whole)
    return (d_normed, grad_in, grad_pos, grad_bias, grad_out)


def conv_front(whole, w_in, kernel, mask_col):
    seq_len, model_width = whole.shape
    local_width = w_in.shape[1] // 2
    glu_in = matmul(whole, w_in)
    gate_value = glu_in[:, :local_width]
    logistic = jax.nn.sigmoid(glu_in[:, local_width:])
    glu_out = gate_value * logistic * mask_col
    tap_count = kernel.shape[0]
    half_taps = (tap_count - 1) // 2
    padded = jnp.pad(glu_out, ((half_taps, half_taps), (0, 0)))
    kernel_float = kernel.astype(jnp.float32)
    conved = kernel_float[0] * padded[0:seq_len]
    for tap_index in range(1, tap_count):
        conved = conved + kernel_float[tap_index] * padded[tap_index : tap_index + seq_len]
    return (gate_value, logistic, padded, conved)


def batch_stats(conved, mask_col, frame_count):
    local_sum = jnp.sum(conved * mask_col, axis=0)
    local_squares = jnp.sum(conved * conved * mask_col, axis=0)
    total_sum, total_squares = dp_total(jnp.stack([local_sum, local_squares]))
    average = total_sum / frame_count
    variance = total_squares / frame_count - average * average
    return (average, lax.rsqrt(variance + batch_eps))


def conv_tail(conved, stats, bn_gain, bn_bias):
    average, inv_std = stats
    normed_b = (conved - average) * inv_std * bn_gain.astype(jnp.float32) + bn_bias.astype(
        jnp.float32
    )
    return (normed_b, jax.nn.silu(normed_b).astype(jnp.bfloat16))


def conv_backward(whole, weights, mask_col, stats, frame_count, grad_whole):
    w_in, kernel, bn_gain, bn_bias, w_out = weights
    seq_len, model_width = whole.shape
    gate_value, logistic, padded, conved = conv_front(whole, w_in, kernel, mask_col)
    normed_b, active = conv_tail(conved, stats, bn_gain, bn_bias)
    average, inv_std = stats
    grad_out = contract_rows(active, grad_whole)
    d_normed = contract_cols(grad_whole, w_out) * silu_slope(normed_b)
    centred = (conved - average) * inv_std
    bias_total, gain_total = dp_total(
        jnp.stack([jnp.sum(d_normed, axis=0), jnp.sum(d_normed * centred, axis=0)])
    )
    d_conved = (
        bn_gain.astype(jnp.float32)
        * inv_std
        * (d_normed - mask_col * (bias_total + centred * gain_total) / frame_count)
    )
    tap_count = kernel.shape[0]
    half_taps = (tap_count - 1) // 2
    kernel_float = kernel.astype(jnp.float32)
    d_padded = jnp.pad(d_conved, ((half_taps, half_taps), (0, 0)))
    d_glu = kernel_float[0] * d_padded[tap_count - 1 : tap_count - 1 + seq_len]
    for tap_index in range(1, tap_count):
        d_glu = (
            d_glu
            + kernel_float[tap_index]
            * d_padded[tap_count - 1 - tap_index : tap_count - 1 - tap_index + seq_len]
        )
    grad_kernel = jnp.stack(
        [
            jnp.sum(d_conved * padded[tap_index : tap_index + seq_len], axis=0)
            for tap_index in range(tap_count)
        ]
    )
    d_glu = d_glu * mask_col
    d_pair = jnp.concatenate(
        [d_glu * logistic, d_glu * gate_value * logistic * (1.0 - logistic)], axis=1
    ).astype(jnp.bfloat16)
    grad_in = contract_rows(whole, d_pair)
    d_normed_in = contract_cols(d_pair, w_in)
    return (d_normed_in, grad_in, grad_kernel, grad_out, gain_total, bias_total)


def body(
    frames_in,
    lengths,
    out_grad,
    norm_gains,
    ffn1_up,
    ffn1_down,
    attn_in,
    pos_proj,
    pos_bias,
    attn_out,
    conv_in,
    depthwise,
    bn_scale,
    bn_shift,
    conv_out,
    ffn2_up,
    ffn2_down,
):
    unused, local_rows, model_width = frames_in.shape
    seq_len = local_rows * lax.axis_size("mp")
    dp_index = lax.axis_index("dp")
    own_length = lax.dynamic_slice_in_dim(lengths, dp_index, 1)[0]
    valid_keys = jnp.arange(seq_len) < own_length
    mask_col = valid_keys.astype(jnp.float32)[:, None]
    frame_count = jnp.sum(lengths).astype(jnp.float32)
    frames = frames_in.reshape(local_rows, model_width)
    _, whole_first, ffn_first = open_step(
        open_middle, [frames, norm_gains], [ffn1_up, ffn1_down], (0, 1), 0
    )
    small = jnp.concatenate([pos_bias, depthwise, bn_scale[None], bn_shift[None]], axis=0)
    table_low = position_table(seq_len, model_width).astype(jnp.bfloat16)
    if direct(model_width // lax.axis_size("dp")):
        packed = packed_rows(small)
    else:
        packed = small.T
    (after_first,), whole_attn, (attn_in_whole, pos_whole, attn_out_whole, packed) = between_step(
        functools.partial(forward_middle, 0.5, 1),
        ffn_forward(whole_first, ffn_first),
        [frames, norm_gains],
        1,
        fetch=[attn_in.reshape(attn_in.shape[0], -1), pos_proj, attn_out, packed],
        dims=(0, 0, 1, 0),
        ways=(False, True, True, True),
    )
    if direct(model_width // lax.axis_size("dp")):
        small = whole_rows(packed, small)
    else:
        small = packed.T
    taps = depthwise.shape[0]
    attn_held = (attn_in_whole, pos_whole, small[:2], attn_out_whole)
    conv_small = (
        small[2 : 2 + taps],
        small[2 + taps],
        small[3 + taps],
    )
    position = matmul(table_low, pos_whole).astype(jnp.bfloat16)
    attn_partial, *attn_saved = attention_forward(
        whole_attn, attn_held, position, own_length[None]
    )
    (after_attn,), whole_conv, (conv_in_whole, conv_out_whole, down_two) = between_step(
        functools.partial(forward_middle, 1.0, 2),
        attn_partial,
        [after_first, norm_gains],
        2,
        fetch=[conv_in.reshape(conv_in.shape[0], -1), conv_out, ffn2_down],
        dims=(0, 1, 1),
        ways=(False, False, True),
    )
    conv_held = (conv_in_whole, *conv_small, conv_out_whole)
    gate_value, logistic, padded, conved = conv_front(
        whole_conv, conv_held[0], conv_held[1], mask_col
    )
    stats = batch_stats(conved, mask_col, frame_count)
    normed_b, active = conv_tail(conved, stats, conv_held[2], conv_held[3])
    (after_conv,), whole_second, (up_two,) = between_step(
        functools.partial(forward_middle, 1.0, 3),
        matmul(active, conv_held[4]),
        [after_attn, norm_gains],
        3,
        fetch=[ffn2_up],
        dims=(0,),
        ways=(True,),
    )
    ffn_second = (up_two, down_two)
    (block_out, d_second, gain_five), whole_grads, _ = between_step(
        turn_middle,
        ffn_forward(whole_second, ffn_second),
        [after_conv, norm_gains, out_grad.reshape(local_rows, model_width)],
        4,
    )
    d_normed, grad_up, grad_down = ffn_backward(whole_second, ffn_second, whole_grads)
    (d_conv, gain_four), whole_grads, (total_up_two, total_down_two) = between_step(
        functools.partial(backward_middle, 1.0, 3),
        d_normed,
        [after_conv, norm_gains, d_second],
        5,
        grads=[grad_up, grad_down],
        dims=(0, 1),
        ways=(False, True),
    )
    d_normed, grad_conv_in, grad_kernel, grad_conv_out, gain_total, bias_total = conv_backward(
        whole_conv, conv_held, mask_col, stats, frame_count, whole_grads
    )
    (d_attn, gain_three), whole_grads, (total_conv_in, total_conv_out) = between_step(
        functools.partial(backward_middle, 1.0, 2),
        d_normed,
        [after_attn, norm_gains, d_conv],
        6,
        grads=[grad_conv_in, grad_conv_out],
        dims=(0, 1),
        ways=(False, True),
    )
    d_normed, grad_attn_in, grad_pos, grad_bias, grad_attn_out = attention_backward(
        whole_attn, attn_held, table_low, position, attn_saved, whole_grads
    )
    (d_first, gain_two), whole_grads, (total_attn_in, total_attn_out, total_pos) = between_step(
        functools.partial(backward_middle, 0.5, 1),
        d_normed,
        [after_first, norm_gains, d_attn],
        7,
        grads=[grad_attn_in, grad_attn_out, grad_pos],
        dims=(0, 1, 0),
        ways=(False, True, True),
    )
    d_normed, grad_up, grad_down = ffn_backward(whole_first, ffn_first, whole_grads)
    (in_grad,), small_grads, gains, (total_up_one, total_down_one) = close_step(
        close_middle,
        d_normed,
        jnp.concatenate([grad_bias, grad_kernel], axis=0),
        jnp.concatenate([gain_two, gain_three, gain_four, gain_five], axis=0),
        [frames, norm_gains, d_first],
        [grad_up, grad_down],
        (0, 1),
        (False, True),
        8,
    )
    gain_sum = jnp.concatenate([gains[4:], gains[:4]], axis=0)
    block = model_width // lax.axis_size("dp")
    piece_len = bn_scale.shape[0]
    own = dp_index * piece_len
    small_grads = lax.dynamic_slice_in_dim(small_grads, own, piece_len, axis=1)
    return (
        block_out.reshape(1, local_rows, model_width),
        in_grad.reshape(1, local_rows, model_width),
        gain_sum,
        total_up_one,
        total_down_one,
        total_attn_in.reshape(block, 3, -1),
        total_pos,
        small_grads[:2],
        total_attn_out,
        total_conv_in.reshape(block, 2, -1),
        small_grads[2:],
        lax.dynamic_slice_in_dim(gain_total, own, piece_len),
        lax.dynamic_slice_in_dim(bias_total, own, piece_len),
        total_conv_out,
        total_up_two,
        total_down_two,
    )


def solution(mesh):
    placed = (
        P("dp", "mp", None),
        P(),
        P("dp", "mp", None),
        P(),
        P("dp", "mp"),
        P("mp", "dp"),
        P("dp", None, "mp"),
        P("dp", "mp"),
        P(None, ("mp", "dp")),
        P("mp", "dp"),
        P("dp", None, "mp"),
        P(None, ("mp", "dp")),
        P(("mp", "dp")),
        P(("mp", "dp")),
        P("mp", "dp"),
        P("dp", "mp"),
        P("mp", "dp"),
    )
    return jax.shard_map(
        body,
        mesh=mesh,
        in_specs=placed,
        out_specs=(
            P("dp", "mp", None),
            P("dp", "mp", None),
            P(),
            P("dp", "mp"),
            P("mp", "dp"),
            P("dp", None, "mp"),
            P("dp", "mp"),
            P(None, ("mp", "dp")),
            P("mp", "dp"),
            P("dp", None, "mp"),
            P(None, ("mp", "dp")),
            P(("mp", "dp")),
            P(("mp", "dp")),
            P("mp", "dp"),
            P("dp", "mp"),
            P("mp", "dp"),
        ),
        check_vma=False,
    )
```

```python
import functools
import math

import jax
import jax.numpy as jnp
from jax import lax
from jax.experimental import pallas as pl
from jax.experimental.pallas import tpu as pltpu
from jax.sharding import PartitionSpec as P

HEAD = 128


norm_eps = 1e-05
batch_eps = 1e-05
masked_score = -1000000000.0


def matmul(left, right):
    return jnp.dot(left, right, preferred_element_type=jnp.float32)


def contract_rows(left, right):
    return lax.dot_general(
        left, right, (((0,), (0,)), ((), ())), preferred_element_type=jnp.float32
    )


def contract_cols(left, right):
    return lax.dot_general(
        left, right, (((1,), (1,)), ((), ())), preferred_element_type=jnp.float32
    )


def layer_norm(values, norm_gain):
    average = jnp.mean(values, axis=-1, keepdims=True)
    centred = values - average
    inv_std = lax.rsqrt(jnp.mean(centred * centred, axis=-1, keepdims=True) + norm_eps)
    return centred * inv_std * norm_gain


def silu_slope(values):
    logistic = jax.nn.sigmoid(values)
    return logistic * (1.0 + values * (1.0 - logistic))


def position_table(seq_len, model_width):
    fine = 32
    lane = jnp.arange(model_width)
    frequency = jnp.exp((lane // 2).astype(jnp.float32) * (-2.0 * math.log(10000.0) / model_width))
    coarse = (seq_len - 1 - fine * jnp.arange(2 * seq_len // fine)).astype(jnp.float32)
    wide = coarse[:, None] * frequency[None, :]
    small = -jnp.arange(fine).astype(jnp.float32)[:, None] * frequency[None, :]
    even = (lane % 2 == 0)[None, :]
    wide_sin, wide_cos = jnp.sin(wide), jnp.cos(wide)
    high = jnp.where(even, wide_sin, wide_cos)
    side = jnp.where(even, wide_cos, -wide_sin)
    table = high[:, None, :] * jnp.cos(small)[None] + side[:, None, :] * jnp.sin(small)[None]
    return table.reshape(2 * seq_len, model_width)


MESH = pl.DeviceIdType.MESH
VMEM_LIMIT = 24 * 1024 * 1024
CHUNKS = 4


def line_copy(src, dst, sems, index, axis, target):
    return pltpu.make_async_remote_copy(
        src_ref=src,
        dst_ref=dst,
        send_sem=sems.at[0, index],
        recv_sem=sems.at[1, index],
        device_id={axis: target},
        device_id_type=MESH,
    )


def bit_of(index, bit):
    return lax.rem(lax.div(index, bit), 2)


def partner(index, bit):
    return index + bit - 2 * bit * bit_of(index, bit)


def cube_bits(size, swap):
    bits = []
    bit = 2
    while bit < size:
        bits.append(bit)
        bit *= 2
    if swap:
        bits.reverse()
    return bits + [1]


def block_at(ref, dim, index, width):
    start = pl.multiple_of(index * width, width)
    return ref.at[pl.ds(start, width)] if dim == 0 else ref.at[:, pl.ds(start, width)]


def all_total_kernel(axis, in_ref, out_ref, slots, sems):
    size = lax.axis_size(axis)
    me = lax.axis_index(axis)
    barrier = pltpu.get_barrier_semaphore()
    targets = [lax.rem(me + step, size) for step in range(1, size)]
    for target in targets:
        pl.semaphore_signal(barrier, inc=1, device_id={axis: target}, device_id_type=MESH)
    pl.semaphore_wait(barrier, size - 1)
    copies = []
    for number, target in enumerate(targets):
        copy = line_copy(in_ref, slots.at[me], sems, number, axis, target)
        copy.start()
        copies.append(copy)
    slots[me] = in_ref[...]
    for copy in copies:
        copy.wait_recv()
    total = slots[0]
    for source in range(1, size):
        total = total + slots[source]
    out_ref[...] = total
    for copy in copies:
        copy.wait_send()


def all_total(values, axis, collective_id):
    size = lax.axis_size(axis)
    return pl.pallas_call(
        functools.partial(all_total_kernel, axis),
        out_shape=jax.ShapeDtypeStruct(values.shape, values.dtype),
        in_specs=[pl.BlockSpec(memory_space=pltpu.VMEM)],
        out_specs=pl.BlockSpec(memory_space=pltpu.VMEM),
        scratch_shapes=[
            pltpu.VMEM((size, *values.shape), values.dtype),
            pltpu.SemaphoreType.DMA((2, size - 1)),
        ],
        compiler_params=pltpu.CompilerParams(
            collective_id=collective_id, has_side_effects=True
        ),
        name="all_total",
    )(values)


def line_peers(axis):
    me, size = lax.axis_index(axis), lax.axis_size(axis)
    return jnp.minimum(me, 1) + jnp.minimum(size - 1 - me, 1)


def greet(line_axis, cube_axis, everyone):
    me, size = lax.axis_index(line_axis), lax.axis_size(line_axis)
    barrier = pltpu.get_barrier_semaphore()
    if everyone:
        for axis in (line_axis, cube_axis):
            here, count = lax.axis_index(axis), lax.axis_size(axis)
            for step in range(1, count):
                pl.semaphore_signal(
                    barrier, inc=1, device_id={axis: lax.rem(here + step, count)},
                    device_id_type=MESH,
                )
        pl.semaphore_wait(barrier, size - 1 + lax.axis_size(cube_axis) - 1)
        return

    @pl.when(me > 0)
    def _():
        pl.semaphore_signal(barrier, inc=1, device_id={line_axis: me - 1}, device_id_type=MESH)

    @pl.when(me < size - 1)
    def _():
        pl.semaphore_signal(barrier, inc=1, device_id={line_axis: me + 1}, device_id_type=MESH)

    bits = cube_bits(lax.axis_size(cube_axis), False) if cube_axis else []
    for bit in bits:
        pl.semaphore_signal(
            barrier, inc=1, device_id={cube_axis: partner(lax.axis_index(cube_axis), bit)},
            device_id_type=MESH,
        )
    pl.semaphore_wait(barrier, line_peers(line_axis) + len(bits))


class LineGather:
    def __init__(self, axis, out_ref, sems, chunks):
        self.axis, self.out, self.sems, self.chunks = axis, out_ref, sems, chunks
        self.size, self.me = lax.axis_size(axis), lax.axis_index(axis)
        self.rows = out_ref.shape[0] // self.size
        self.part = self.rows // chunks
        self.steps = self.size - 1

    def piece(self, index, chunk):
        start = pl.multiple_of(index * self.rows + chunk * self.part, self.part)
        return self.out.at[pl.ds(start, self.part)]

    def copy(self, way, step, index, chunk):
        place = self.piece(index, chunk)
        return line_copy(
            place, place, self.sems, (way * self.steps + step) * self.chunks + chunk, self.axis,
            self.me + 1 if way == 0 else self.me - 1,
        )

    def index(self, way, step):
        return self.me - step if way == 0 else self.me + step

    def held(self, way, step):
        return self.me >= step if way == 0 else self.me + step < self.size

    def onward(self, way):
        return self.me + 1 < self.size if way == 0 else self.me > 0

    def step(self, step, chunk):
        for way in range(2):
            if step > 0:
                @pl.when(self.held(way, step))
                def _():
                    self.copy(way, step - 1, self.index(way, step), chunk).wait_recv()

            if step < self.steps:
                @pl.when(jnp.logical_and(self.held(way, step), self.onward(way)))
                def _():
                    self.copy(way, step, self.index(way, step), chunk).start()

    def finish(self):
        for chunk in range(self.chunks):
            for step in range(self.steps):
                for way in range(2):
                    @pl.when(jnp.logical_and(self.held(way, step), self.onward(way)))
                    def _():
                        self.copy(way, step, self.index(way, step), chunk).wait_send()


class LineScatter:
    def __init__(self, axis, in_ref, total_ref, slots, staged, sems, chunks):
        self.axis, self.ins, self.total, self.chunks = axis, in_ref, total_ref, chunks
        self.slots, self.staged, self.sems = slots, staged, sems
        self.size, self.me = lax.axis_size(axis), lax.axis_index(axis)
        self.rows = total_ref.shape[0]
        self.part = self.rows // chunks
        self.first_way = lax.div(self.me, (self.size + 1) // 2)

    def mine(self, owner, chunk):
        start = pl.multiple_of(owner * self.rows + chunk * self.part, self.part)
        return self.ins.at[pl.ds(start, self.part)]

    def lines(self, chunk):
        return slice(chunk * self.part, (chunk + 1) * self.part)

    def copy(self, way, owner, chunk, src):
        return line_copy(
            src, self.slots.at[way, owner, self.lines(chunk)], self.sems,
            (way * self.size + owner) * self.chunks + chunk, self.axis,
            self.me + 1 - 2 * way,
        )

    def arrived(self, way, owner, chunk):
        return self.copy(way, owner, chunk, self.staged.at[way, owner, self.lines(chunk)])

    def place(self, way, step):
        owner = (1 - way) * (self.size - 1 - step) + way * step
        distance = (owner - self.me) * (1 - 2 * way)
        behind = (1 - way) * self.me + way * (self.size - 1 - self.me)
        return owner, distance, behind

    def lead(self, step, chunk):
        for way in range(2):
            owner, distance, behind = self.place(way, step)

            @pl.when(jnp.logical_and(distance > 0, behind == 0))
            def _():
                self.copy(way, owner, chunk, self.mine(owner, chunk)).start()

    def hop(self, way, step, chunk):
        owner, distance, behind = self.place(way, step)

        @pl.when(jnp.logical_and(distance > 0, behind > 0))
        def _():
            lines = self.lines(chunk)
            self.arrived(way, owner, chunk).wait_recv()
            self.staged[way, owner, lines] = (
                self.mine(owner, chunk)[...].astype(jnp.float32)
                + self.slots[way, owner, lines].astype(jnp.float32)
            ).astype(self.staged.dtype)
            self.arrived(way, owner, chunk).start()

    def run(self, halfway=None):
        marks = [(step, chunk) for step in range(self.size - 1) for chunk in range(self.chunks)]
        for mark in marks:
            self.lead(*mark)
        for number in range(len(marks) + self.chunks):
            if halfway and number == len(marks) // 2 + 1:
                halfway()
            if number < len(marks):
                self.hop(self.first_way, *marks[number])
            if number >= self.chunks:
                self.hop(1 - self.first_way, *marks[number - self.chunks])

    def result(self, chunk):
        lines = self.lines(chunk)
        self.total[lines] = self.mine(self.me, chunk)[...].astype(jnp.float32)
        for way in range(2):
            @pl.when(self.me > 0 if way == 0 else self.me < self.size - 1)
            def _():
                self.arrived(way, self.me, chunk).wait_recv()
                self.total[lines] += self.slots[way, self.me, lines].astype(jnp.float32)

        return self.total[lines]

    def finish(self):
        for chunk in range(self.chunks):
            for owner in range(self.size):
                for way in range(2):
                    @pl.when(self.me < owner if way == 0 else self.me > owner)
                    def _():
                        self.arrived(way, owner, chunk).wait_send()


class CubeGather:
    def __init__(self, axis, dims, ways, ins, outs, sems):
        self.axis, self.dims, self.ways = axis, dims, ways
        self.ins, self.outs, self.sems = ins, outs, sems
        self.size, self.me = lax.axis_size(axis), lax.axis_index(axis)
        self.stages = len(cube_bits(self.size, False))
        self.started = []
        self.waiting = [[] for _ in ins]

    def step(self, stage):
        per = self.size - 1
        for which in range(len(self.ins)):
            width = self.ins[which].shape[self.dims[which]]
            bits = cube_bits(self.size, self.ways[which])
            for copy in self.waiting[which]:
                copy.wait_recv()
            self.waiting[which] = []
            if stage == 0:
                block_at(self.outs[which], self.dims[which], self.me, width)[...] = (
                    self.ins[which][...]
                )
            if stage == self.stages:
                continue
            held = [self.me]
            for bit in bits[:stage]:
                held = held + [partner(index, bit) for index in held]
            for number, index in enumerate(held):
                place = block_at(self.outs[which], self.dims[which], index, width)
                copy = line_copy(
                    self.ins[which] if stage == 0 else place, place, self.sems,
                    which * per + 2**stage - 1 + number, self.axis, partner(self.me, bits[stage]),
                )
                copy.start()
                self.waiting[which].append(copy)
            self.started.extend(self.waiting[which])

    def finish(self):
        for copy in self.started:
            copy.wait_send()


class CubeScatter:
    def __init__(self, axis, dims, ways, ins, outs, slots, sems):
        self.axis, self.dims, self.ways = axis, dims, ways
        self.ins, self.outs, self.slots, self.sems = ins, outs, slots, sems
        self.size, self.me = lax.axis_size(axis), lax.axis_index(axis)
        self.stages = len(cube_bits(self.size, False))
        self.started = []

    def slot(self, which, stage, number):
        return self.slots[which].at[self.size - self.size // 2**stage + number]

    def sets(self, which, stage):
        bits = cube_bits(self.size, self.ways[which])[::-1]
        held = [self.me]
        for bit in bits[stage + 1 :]:
            held = held + [partner(index, bit) for index in held]
        return bits[stage], held

    def send(self, which, stage):
        width = self.outs[which].shape[self.dims[which]]
        bit, held = self.sets(which, stage)
        for number, index in enumerate(held):
            if stage == 0:
                src = block_at(self.ins[which], self.dims[which], partner(index, bit), width)
            else:
                src = self.slot(which, stage - 1, 2 * number + 1)
            copy = line_copy(
                src, self.slot(which, stage, number), self.sems,
                which * (self.size - 1) + self.size - self.size // 2**stage + number,
                self.axis, partner(self.me, bit),
            )
            copy.start()
            self.started.append((which, stage, copy))

    def receive(self, which, stage):
        width = self.outs[which].shape[self.dims[which]]
        _, held = self.sets(which, stage)
        for copy in [c for w, s, c in self.started if (w, s) == (which, stage)]:
            copy.wait_recv()
        for number, index in enumerate(held):
            got = self.slot(which, stage, number)
            if stage == 0:
                mine = block_at(self.ins[which], self.dims[which], index, width)
            else:
                mine = self.slot(which, stage - 1, 2 * number)
            total = got[...].astype(jnp.float32) + mine[...].astype(jnp.float32)
            if stage == self.stages - 1:
                self.outs[which][...] = total
            else:
                got[...] = total.astype(self.slots[which].dtype)

    def step(self, stage):
        for which in range(len(self.ins)):
            if stage > 0:
                self.receive(which, stage - 1)
            if stage < self.stages:
                self.send(which, stage)

    def finish(self):
        for _, _, copy in self.started:
            copy.wait_send()


class AllTotal:
    def __init__(self, axis, slots, sems):
        self.axis, self.slots, self.sems = axis, slots, sems
        self.size, self.me = lax.axis_size(axis), lax.axis_index(axis)
        self.copies = []

    def start(self):
        for step in range(1, self.size):
            copy = line_copy(
                self.slots.at[self.me], self.slots.at[self.me], self.sems, step - 1, self.axis,
                lax.rem(self.me + step, self.size),
            )
            copy.start()
            self.copies.append(copy)

    def result(self):
        for copy in self.copies:
            copy.wait_recv()
        total = self.slots[0]
        for source in range(1, self.size):
            total = total + self.slots[source]
        return total

    def finish(self):
        for copy in self.copies:
            copy.wait_send()


def open_kernel(middle, counts, chunks, dims, ways, *refs):
    local_count, mid_count = counts
    count = len(dims)
    refs = list(refs)
    take = lambda number: [refs.pop(0) for _ in range(number)]
    locals_, ins = take(local_count), take(count)
    mids, (whole,), outs = take(mid_count), take(1), take(count)
    gather_sems, cube_sems = refs
    fetch = CubeGather("dp", dims, ways, ins, outs, cube_sems)
    rows = LineGather("mp", whole, gather_sems, chunks)
    greet("mp", "dp", False)
    fetch.step(0)
    values, normed = middle(None, *[ref[...] for ref in locals_])
    for ref, value in zip(mids, values):
        ref[...] = value
    for chunk in range(chunks):
        part = rows.part
        rows.piece(rows.me, chunk)[...] = normed[chunk * part : (chunk + 1) * part]
        rows.step(0, chunk)
    for step in range(1, max(rows.steps, fetch.stages) + 1):
        if step <= fetch.stages:
            fetch.step(step)
        if step <= rows.steps:
            for chunk in range(chunks):
                rows.step(step, chunk)
    rows.finish()
    fetch.finish()


def between_kernel(middle, counts, chunks, fetches, dims, ways, *refs):
    local_count, mid_count = counts
    count = len(dims)
    refs = list(refs)
    take = lambda number: [refs.pop(0) for _ in range(number)]
    (partial,), locals_, ins = take(1), take(local_count), take(count)
    mids, (whole,), outs = take(mid_count), take(1), take(count)
    (total, slots, staged, scatter_sems, gather_sems), refs = refs[:5], refs[5:]
    sums = LineScatter("mp", partial, total, slots, staged, scatter_sems, chunks)
    rows = LineGather("mp", whole, gather_sems, chunks)
    beside, stages = None, 0
    if count:
        if fetches:
            beside = CubeGather("dp", dims, ways, ins, outs, refs[0])
        else:
            beside = CubeScatter("dp", dims, ways, ins, outs, refs[:count], refs[count])
        stages = beside.stages + 1
    greet("mp", "dp" if count else None, False)
    stage = 0
    if stages:
        beside.step(0)
        sums.run(lambda: beside.step(1))
        stage = 2
    else:
        sums.run()
    for chunk in range(chunks):
        lines = sums.lines(chunk)
        picked = [ref[lines] if ref.shape[0] == sums.rows else ref[...] for ref in locals_]
        values, normed = middle(sums.result(chunk), *picked)
        rows.piece(rows.me, chunk)[...] = normed
        rows.step(0, chunk)
        for ref, value in zip(mids, values):
            if ref.shape[0] == sums.rows:
                ref[lines] = value
            elif chunk == 0:
                ref[...] = value
            else:
                ref[...] += value
    for step in range(1, rows.steps + 1):
        if stage < stages:
            beside.step(stage)
            stage += 1
        for chunk in range(chunks):
            rows.step(step, chunk)
    for stage in range(stage, stages):
        beside.step(stage)
    if count:
        beside.finish()
    sums.finish()
    rows.finish()


def close_kernel(middle, counts, chunks, dims, ways, *refs):
    local_count, mid_count = counts
    count = len(dims)
    refs = list(refs)
    take = lambda number: [refs.pop(0) for _ in range(number)]
    (partial, small, gains), locals_, ins = take(3), take(local_count), take(count)
    mids, (small_out, gains_out), outs = take(mid_count), take(2), take(count)
    (total, slots, staged, scatter_sems), refs = refs[:4], refs[4:]
    (small_slots, small_sems, gain_slots, gain_sems, last_slots, last_sems), refs = refs[:6], refs[6:]
    sums = LineScatter("mp", partial, total, slots, staged, scatter_sems, chunks)
    grads = CubeScatter("dp", dims, ways, ins, outs, refs[:count], refs[count])
    little = AllTotal("dp", small_slots, small_sems)
    near, far = AllTotal("dp", gain_slots, gain_sems), AllTotal("mp", last_slots, last_sems)
    little.slots[little.me] = small[...]
    greet("mp", "dp", True)
    little.start()
    grads.step(0)
    sums.run(lambda: grads.step(1))
    total_rows = jnp.concatenate([sums.result(chunk) for chunk in range(chunks)], axis=0)
    values, gain = middle(total_rows, *[ref[...] for ref in locals_])
    near.slots[near.me] = jnp.concatenate([gains[...], gain], axis=0)
    near.start()
    for ref, value in zip(mids, values):
        ref[...] = value
    grads.step(2)
    far.slots[far.me] = near.result()
    far.start()
    for stage in range(3, grads.stages + 1):
        grads.step(stage)
    small_out[...] = little.result()
    gains_out[...] = far.result()
    for task in (grads, sums, little, near, far):
        task.finish()


def shapes_of(arrays):
    return [jax.ShapeDtypeStruct(value.shape, value.dtype) for value in arrays]


def call_step(kernel, inputs, out_shape, scratch, collective_id, name):
    vmem = pl.BlockSpec(memory_space=pltpu.VMEM)
    return pl.pallas_call(
        kernel,
        out_shape=out_shape,
        in_specs=[vmem] * len(inputs),
        out_specs=[vmem] * len(out_shape),
        scratch_shapes=scratch,
        compiler_params=pltpu.CompilerParams(
            collective_id=collective_id, has_side_effects=True, vmem_limit_bytes=VMEM_LIMIT
        ),
        name=name,
    )(*inputs)


def line_scratch(rows, width, chunks):
    size = lax.axis_size("mp")
    return [
        pltpu.VMEM((rows, width), jnp.float32),
        pltpu.VMEM((2, size, rows, width), jnp.bfloat16),
        pltpu.VMEM((2, size, rows, width), jnp.bfloat16),
        pltpu.SemaphoreType.DMA((2, 2 * size * chunks)),
    ]


def cube_scratch(arrays, dims):
    size = lax.axis_size("dp")
    shapes, slots = [], []
    for array, dim in zip(arrays, dims):
        shape = list(array.shape)
        shape[dim] //= size
        shapes.append(jax.ShapeDtypeStruct(tuple(shape), jnp.float32))
        slots.append(pltpu.VMEM((size - 1, *shape), array.dtype))
    if arrays:
        slots.append(pltpu.SemaphoreType.DMA((2, len(arrays) * (size - 1))))
    return shapes, slots


def plain_totals(grads, dims):
    return [
        lax.psum_scatter(grad, "dp", scatter_dimension=dim, tiled=True).astype(jnp.float32)
        for grad, dim in zip(grads, dims)
    ]


def direct(block):
    size = lax.axis_size("dp")
    return size & (size - 1) == 0 and block % 128 == 0


def fetched_shapes(arrays, dims):
    size, shapes = lax.axis_size("dp"), []
    for array, dim in zip(arrays, dims):
        shape = list(array.shape)
        shape[dim] *= size
        shapes.append(jax.ShapeDtypeStruct(tuple(shape), array.dtype))
    return shapes


def plain_fetch(arrays, dims):
    return [lax.all_gather(array, "dp", axis=dim, tiled=True) for array, dim in zip(arrays, dims)]


def packed_rows(small):
    return jnp.pad(small, ((0, 16 - small.shape[0]), (0, 128 - small.shape[1])))


def whole_rows(packed, small):
    size, (count, lanes) = lax.axis_size("dp"), small.shape
    packed = packed.reshape(size, 16, 128)[:, :count, :lanes]
    return packed.transpose(1, 0, 2).reshape(count, size * lanes)


def open_step(middle, locals_, arrays, dims, collective_id):
    if not direct(arrays[0].shape[dims[0]]):
        mids, normed = middle(None, *locals_)
        return mids, lax.all_gather(normed, "mp", axis=0, tiled=True), plain_fetch(arrays, dims)
    ways = [index % 2 == 1 for index in range(len(dims))]
    mid_shapes, normed_shape = jax.eval_shape(functools.partial(middle, None), *locals_)
    rows, width = normed_shape.shape
    whole_shape = jax.ShapeDtypeStruct((rows * lax.axis_size("mp"), width), normed_shape.dtype)
    count = len(mid_shapes)
    result = call_step(
        functools.partial(open_kernel, middle, (len(locals_), count), CHUNKS, dims, ways),
        [*locals_, *arrays],
        [*mid_shapes, whole_shape, *fetched_shapes(arrays, dims)],
        [
            pltpu.SemaphoreType.DMA((2, 2 * (lax.axis_size("mp") - 1) * CHUNKS)),
            pltpu.SemaphoreType.DMA((2, len(arrays) * (lax.axis_size("dp") - 1))),
        ],
        collective_id,
        "open_step",
    )
    return result[:count], result[count], result[count + 1 :]


def between_step(
    middle, partial_value, locals_, collective_id, grads=(), fetch=(), dims=(), ways=()
):
    partial_value = partial_value.astype(jnp.bfloat16)
    grads = [grad.astype(jnp.bfloat16) for grad in grads]
    size = lax.axis_size("mp")
    rows, width = partial_value.shape[0] // size, partial_value.shape[1]
    if not direct(width // lax.axis_size("dp")):
        total = lax.psum_scatter(partial_value, "mp", scatter_dimension=0, tiled=True)
        mids, normed = middle(total.astype(jnp.float32), *locals_)
        others = plain_fetch(fetch, dims) if fetch else plain_totals(grads, dims)
        return mids, lax.all_gather(normed, "mp", axis=0, tiled=True), others
    total = jax.ShapeDtypeStruct((rows, width), jnp.float32)
    mid_shapes, normed_shape = jax.eval_shape(middle, total, *locals_)
    if fetch:
        shapes = fetched_shapes(fetch, dims)
        scratch = [pltpu.SemaphoreType.DMA((2, len(fetch) * (lax.axis_size("dp") - 1)))]
    else:
        shapes, scratch = cube_scratch(grads, dims)
    count = len(mid_shapes)
    result = call_step(
        functools.partial(
            between_kernel, middle, (len(locals_), count), CHUNKS, bool(fetch), dims, ways
        ),
        [partial_value, *locals_, *grads, *fetch],
        [
            *mid_shapes,
            jax.ShapeDtypeStruct((rows * size, width), normed_shape.dtype),
            *shapes,
        ],
        line_scratch(rows, width, CHUNKS)
        + [pltpu.SemaphoreType.DMA((2, 2 * (size - 1) * CHUNKS))]
        + scratch,
        collective_id,
        "between_step",
    )
    return result[:count], result[count], result[count + 1 :]


def close_step(middle, partial_value, small, gains, locals_, grads, dims, ways, collective_id):
    partial_value = partial_value.astype(jnp.bfloat16)
    grads = [grad.astype(jnp.bfloat16) for grad in grads]
    size, dp_size = lax.axis_size("mp"), lax.axis_size("dp")
    rows, width = partial_value.shape[0] // size, partial_value.shape[1]
    if not direct(width // dp_size):
        total = lax.psum_scatter(partial_value, "mp", scatter_dimension=0, tiled=True)
        mids, gain = middle(total.astype(jnp.float32), *locals_)
        gains = lax.psum(jnp.concatenate([gains, gain], axis=0), ("dp", "mp"))
        return mids, lax.psum(small, "dp"), gains, plain_totals(grads, dims)
    total = jax.ShapeDtypeStruct((rows, width), jnp.float32)
    mid_shapes, gain_shape = jax.eval_shape(middle, total, *locals_)
    gains_shape = jax.ShapeDtypeStruct((gains.shape[0] + 1, width), jnp.float32)
    shapes, slots = cube_scratch(grads, dims)
    count = len(mid_shapes)
    result = call_step(
        functools.partial(close_kernel, middle, (len(locals_), count), CHUNKS, dims, ways),
        [partial_value, small, gains, *locals_, *grads],
        [*mid_shapes, *shapes_of([small]), gains_shape, *shapes],
        line_scratch(rows, width, CHUNKS)
        + [
            pltpu.VMEM((dp_size, *small.shape), jnp.float32),
            pltpu.SemaphoreType.DMA((2, dp_size - 1)),
            pltpu.VMEM((dp_size, *gains_shape.shape), jnp.float32),
            pltpu.SemaphoreType.DMA((2, dp_size - 1)),
            pltpu.VMEM((size, *gains_shape.shape), jnp.float32),
            pltpu.SemaphoreType.DMA((2, size - 1)),
        ]
        + slots,
        collective_id,
        "close_step",
    )
    return result[:count], result[count], result[count + 1], result[count + 2 :]


def forward_middle(scale, row, total, residual, norm_gains):
    residual = residual.astype(jnp.float32)
    if total is not None:
        residual = residual + scale * total
    return [residual], layer_norm(residual, norm_gains[row : row + 1]).astype(jnp.bfloat16)


def open_middle(total, frames, norm_gains):
    return [], layer_norm(frames.astype(jnp.float32), norm_gains[0:1]).astype(jnp.bfloat16)


def norm_back(values, norm_gain, upstream):
    centred = values - jnp.mean(values, axis=-1, keepdims=True)
    inv_std = lax.rsqrt(jnp.mean(centred * centred, axis=-1, keepdims=True) + norm_eps)
    normed = centred * inv_std
    scaled = upstream * norm_gain
    d_values = inv_std * (
        scaled
        - jnp.mean(scaled, axis=-1, keepdims=True)
        - normed * jnp.mean(scaled * normed, axis=-1, keepdims=True)
    )
    return d_values, jnp.sum(upstream * normed, axis=0, keepdims=True)


def turn_middle(total, residual, norm_gains, out_grad):
    after = residual + 0.5 * total
    gain = norm_gains[4:5]
    d_after, d_gain = norm_back(after, gain, out_grad.astype(jnp.float32))
    block_out = layer_norm(after, gain).astype(jnp.bfloat16)
    return [block_out, d_after, d_gain], (0.5 * d_after).astype(jnp.bfloat16)


def backward_middle(scale, row, total, values, norm_gains, upstream):
    d_branch, d_gain = norm_back(values.astype(jnp.float32), norm_gains[row : row + 1], total)
    d_values = upstream + d_branch
    return [d_values, d_gain], (scale * d_values).astype(jnp.bfloat16)


def close_middle(total, values, norm_gains, upstream):
    d_branch, d_gain = norm_back(values.astype(jnp.float32), norm_gains[0:1], total)
    return [upstream + d_branch], d_gain


def store_kernel(*refs):
    count = len(refs) // 2
    ins, outs, sems = refs[:count], refs[count : 2 * count], refs[2 * count]
    copies = [
        pltpu.make_async_copy(ins[number], outs[number], sems.at[number])
        for number in range(count)
    ]
    for copy in copies:
        copy.start()
    for copy in copies:
        copy.wait()


def store_all(arrays):
    return pl.pallas_call(
        store_kernel,
        out_shape=shapes_of(arrays),
        in_specs=[pl.BlockSpec(memory_space=pltpu.VMEM)] * len(arrays),
        out_specs=[pl.BlockSpec(memory_space=pl.ANY)] * len(arrays),
        scratch_shapes=[pltpu.SemaphoreType.DMA((len(arrays),))],
        compiler_params=pltpu.CompilerParams(vmem_limit_bytes=VMEM_LIMIT),
        name="store_all",
    )(*arrays)


def dp_total(values):
    if direct(128):
        return all_total(values, "dp", 9)
    return lax.psum(values, "dp")


def ffn_forward(whole, weights):
    w_up, w_down = weights
    hidden = matmul(whole, w_up)
    return matmul(jax.nn.silu(hidden).astype(jnp.bfloat16), w_down)


def ffn_backward(whole, weights, grad_whole):
    w_up, w_down = weights
    hidden = matmul(whole, w_up)
    active = jax.nn.silu(hidden).astype(jnp.bfloat16)
    grad_down = contract_rows(active, grad_whole)
    d_hidden = (contract_cols(grad_whole, w_down) * silu_slope(hidden)).astype(jnp.bfloat16)
    grad_up = contract_rows(whole, d_hidden)
    return (contract_cols(d_hidden, w_up), grad_up, grad_down)


def place_position(position_ref, block, rows, seq_len):
    start = pl.multiple_of(seq_len - rows - block * rows, rows)
    return position_ref.at[pl.ds(start, seq_len + rows)]


def attention_kernel(
    scaling, length_ref, whole_ref, in_ref, bias_ref, position_ref, out_w_ref,
    partial_ref, probs_ref, context_ref, query_u_ref, query_v_ref, key_ref, value_ref,
):
    block = pl.program_id(0)
    seq_len, local_width = key_ref.shape
    rows = partial_ref.shape[0]

    @pl.when(block == 0)
    def _():
        projected = matmul(whole_ref[...], in_ref[...])
        queries = projected[:, :local_width]
        query_u_ref[...] = ((queries + bias_ref[0:1]) * scaling).astype(jnp.bfloat16)
        query_v_ref[...] = ((queries + bias_ref[1:2]) * scaling).astype(jnp.bfloat16)
        key_ref[...] = projected[:, local_width : 2 * local_width].astype(jnp.bfloat16)
        value_ref[...] = projected[:, 2 * local_width :].astype(jnp.bfloat16)

    here = pl.ds(pl.multiple_of(block * rows, rows), rows)
    valid = lax.broadcasted_iota(jnp.int32, (rows, seq_len), 1) < length_ref[0]
    nearby = place_position(position_ref, block, rows, seq_len)
    pieces = []
    for head in range(local_width // HEAD):
        lanes = slice(head * HEAD, (head + 1) * HEAD)
        content = contract_cols(query_u_ref[here, lanes], key_ref[:, lanes])
        zeds = contract_cols(query_v_ref[here, lanes], nearby[:, lanes])
        shifted = pltpu.roll(zeds, seq_len + 1, 1, stride=1, stride_axis=0)[:, :seq_len]
        scores = jnp.where(valid, content + shifted, masked_score)
        exponent = jnp.exp(scores - jnp.max(scores, axis=-1, keepdims=True))
        probs = exponent / jnp.sum(exponent, axis=-1, keepdims=True)
        probs_ref[head] = probs
        pieces.append(matmul(probs.astype(jnp.bfloat16), value_ref[:, lanes]).astype(jnp.bfloat16))
    context = jnp.concatenate(pieces, axis=1)
    context_ref[...] = context
    partial_ref[...] = matmul(context, out_w_ref[...]).astype(jnp.bfloat16)


def attention_forward(whole, weights, position, own_length):
    w_in, w_pos, bias_pair, w_out = weights
    seq_len, model_width = whole.shape
    local_width = w_out.shape[0]
    heads_here = local_width // HEAD
    rows = 128
    full = pl.BlockSpec(memory_space=pltpu.VMEM)
    low = jnp.bfloat16
    return pl.pallas_call(
        functools.partial(attention_kernel, HEAD ** (-0.5)),
        grid=(seq_len // rows,),
        out_shape=[
            jax.ShapeDtypeStruct((seq_len, model_width), low),
            jax.ShapeDtypeStruct((heads_here, seq_len, seq_len), jnp.float32),
        ]
        + [jax.ShapeDtypeStruct((seq_len, local_width), low)] * 5,
        in_specs=[pl.BlockSpec(memory_space=pltpu.SMEM)] + [full] * 5,
        out_specs=[
            pl.BlockSpec((rows, model_width), lambda block: (block, 0)),
            pl.BlockSpec((heads_here, rows, seq_len), lambda block: (0, block, 0)),
            pl.BlockSpec((rows, local_width), lambda block: (block, 0)),
        ]
        + [full] * 4,
        compiler_params=pltpu.CompilerParams(vmem_limit_bytes=VMEM_LIMIT),
        name="attention_forward",
    )(own_length, whole, w_in, bias_pair.astype(jnp.float32), position, w_out)


def attention_back_kernel(
    scaling, grad_ref, out_w_ref, probs_ref, query_u_ref, query_v_ref, key_ref, value_ref,
    position_ref, d_projected_ref, d_position_ref, bias_ref, d_keys, d_values, d_places,
):
    block = pl.program_id(0)
    seq_len, local_width = key_ref.shape
    rows = grad_ref.shape[0]

    @pl.when(block == 0)
    def _():
        d_keys[...] = jnp.zeros_like(d_keys)
        d_values[...] = jnp.zeros_like(d_values)
        d_places[...] = jnp.zeros_like(d_places)
        bias_ref[...] = jnp.zeros_like(bias_ref)

    here = pl.ds(pl.multiple_of(block * rows, rows), rows)
    nearby = place_position(position_ref, block, rows, seq_len)
    d_nearby = place_position(d_places, block, rows, seq_len)
    upside = (
        lax.broadcasted_iota(jnp.int32, (rows, rows), 0)
        + lax.broadcasted_iota(jnp.int32, (rows, rows), 1)
        == rows - 1
    ).astype(jnp.bfloat16)
    d_context_all = contract_cols(grad_ref[...], out_w_ref[...]).astype(jnp.bfloat16)
    for head in range(local_width // HEAD):
        lanes = slice(head * HEAD, (head + 1) * HEAD)
        d_context = d_context_all[:, lanes]
        probs = probs_ref[head]
        d_probs = contract_cols(d_context, value_ref[:, lanes])
        inner = jnp.sum(probs * d_probs, axis=-1, keepdims=True)
        d_scores = (probs * (d_probs - inner)).astype(jnp.bfloat16)
        d_values[:, lanes] += contract_rows(probs.astype(jnp.bfloat16), d_context)
        d_keys[:, lanes] += contract_rows(d_scores, query_u_ref[here, lanes])
        grad_u = matmul(d_scores, key_ref[:, lanes]) * scaling
        turned = matmul(upside, d_scores)
        turned = jnp.concatenate([turned, jnp.zeros((rows, rows), jnp.float32)], axis=1)
        turned = pltpu.roll(turned, 0, 1, stride=1, stride_axis=0).astype(jnp.bfloat16)
        d_zeds = matmul(upside, turned).astype(jnp.bfloat16)
        grad_v = matmul(d_zeds, nearby[:, lanes]) * scaling
        d_nearby[:, lanes] += contract_rows(d_zeds, query_v_ref[here, lanes])
        d_projected_ref[here, lanes] = (grad_u + grad_v).astype(jnp.bfloat16)
        bias_ref[0:1, lanes] += jnp.sum(grad_u, axis=0, keepdims=True)
        bias_ref[1:2, lanes] += jnp.sum(grad_v, axis=0, keepdims=True)

    @pl.when(block == pl.num_programs(0) - 1)
    def _():
        d_projected_ref[:, local_width : 2 * local_width] = d_keys[...].astype(jnp.bfloat16)
        d_projected_ref[:, 2 * local_width :] = d_values[...].astype(jnp.bfloat16)
        d_position_ref[...] = d_places[...].astype(jnp.bfloat16)


def attention_backward(whole, weights, table_low, position, saved, grad_whole):
    w_in, w_pos, bias_pair, w_out = weights
    probs, context, query_u, query_v, key_rows, value_rows = saved
    seq_len, model_width = whole.shape
    local_width = w_out.shape[0]
    heads_here = local_width // HEAD
    rows = 128
    full = pl.BlockSpec(memory_space=pltpu.VMEM)
    d_projected, d_position, grad_bias = pl.pallas_call(
        functools.partial(attention_back_kernel, HEAD ** (-0.5)),
        grid=(seq_len // rows,),
        out_shape=[
            jax.ShapeDtypeStruct((seq_len, 3 * local_width), jnp.bfloat16),
            jax.ShapeDtypeStruct((2 * seq_len, local_width), jnp.bfloat16),
            jax.ShapeDtypeStruct((2, local_width), jnp.float32),
        ],
        in_specs=[
            pl.BlockSpec((rows, model_width), lambda block: (block, 0)),
            full,
            pl.BlockSpec((heads_here, rows, seq_len), lambda block: (0, block, 0)),
        ]
        + [full] * 5,
        out_specs=[full] * 3,
        scratch_shapes=[
            pltpu.VMEM((seq_len, local_width), jnp.float32),
            pltpu.VMEM((seq_len, local_width), jnp.float32),
            pltpu.VMEM((2 * seq_len, local_width), jnp.float32),
        ],
        compiler_params=pltpu.CompilerParams(vmem_limit_bytes=VMEM_LIMIT),
        name="attention_backward",
    )(grad_whole, w_out, probs, query_u, query_v, key_rows, value_rows, position)
    grad_in = contract_rows(whole, d_projected)
    d_normed = contract_cols(d_projected, w_in)
    grad_pos = contract_rows(table_low, d_position)
    grad_out = contract_rows(context, grad_whole)
    return (d_normed, grad_in, grad_pos, grad_bias, grad_out)


def conv_front(whole, w_in, kernel, mask_col):
    seq_len, model_width = whole.shape
    local_width = w_in.shape[1] // 2
    glu_in = matmul(whole, w_in)
    gate_value = glu_in[:, :local_width]
    logistic = jax.nn.sigmoid(glu_in[:, local_width:])
    glu_out = gate_value * logistic * mask_col
    tap_count = kernel.shape[0]
    half_taps = (tap_count - 1) // 2
    padded = jnp.pad(glu_out, ((half_taps, half_taps), (0, 0)))
    kernel_float = kernel.astype(jnp.float32)
    conved = kernel_float[0] * padded[0:seq_len]
    for tap_index in range(1, tap_count):
        conved = conved + kernel_float[tap_index] * padded[tap_index : tap_index + seq_len]
    return (gate_value, logistic, padded, conved)


def batch_stats(conved, mask_col, frame_count):
    local_sum = jnp.sum(conved * mask_col, axis=0)
    local_squares = jnp.sum(conved * conved * mask_col, axis=0)
    total_sum, total_squares = dp_total(jnp.stack([local_sum, local_squares]))
    average = total_sum / frame_count
    variance = total_squares / frame_count - average * average
    return (average, lax.rsqrt(variance + batch_eps))


def conv_tail(conved, stats, bn_gain, bn_bias):
    average, inv_std = stats
    normed_b = (conved - average) * inv_std * bn_gain.astype(jnp.float32) + bn_bias.astype(
        jnp.float32
    )
    return (normed_b, jax.nn.silu(normed_b).astype(jnp.bfloat16))


def conv_backward(whole, weights, mask_col, stats, frame_count, grad_whole):
    w_in, kernel, bn_gain, bn_bias, w_out = weights
    seq_len, model_width = whole.shape
    gate_value, logistic, padded, conved = conv_front(whole, w_in, kernel, mask_col)
    normed_b, active = conv_tail(conved, stats, bn_gain, bn_bias)
    average, inv_std = stats
    grad_out = contract_rows(active, grad_whole)
    d_normed = contract_cols(grad_whole, w_out) * silu_slope(normed_b)
    centred = (conved - average) * inv_std
    bias_total, gain_total = dp_total(
        jnp.stack([jnp.sum(d_normed, axis=0), jnp.sum(d_normed * centred, axis=0)])
    )
    d_conved = (
        bn_gain.astype(jnp.float32)
        * inv_std
        * (d_normed - mask_col * (bias_total + centred * gain_total) / frame_count)
    )
    tap_count = kernel.shape[0]
    half_taps = (tap_count - 1) // 2
    kernel_float = kernel.astype(jnp.float32)
    d_padded = jnp.pad(d_conved, ((half_taps, half_taps), (0, 0)))
    d_glu = kernel_float[0] * d_padded[tap_count - 1 : tap_count - 1 + seq_len]
    for tap_index in range(1, tap_count):
        d_glu = (
            d_glu
            + kernel_float[tap_index]
            * d_padded[tap_count - 1 - tap_index : tap_count - 1 - tap_index + seq_len]
        )
    grad_kernel = jnp.stack(
        [
            jnp.sum(d_conved * padded[tap_index : tap_index + seq_len], axis=0)
            for tap_index in range(tap_count)
        ]
    )
    d_glu = d_glu * mask_col
    d_pair = jnp.concatenate(
        [d_glu * logistic, d_glu * gate_value * logistic * (1.0 - logistic)], axis=1
    ).astype(jnp.bfloat16)
    grad_in = contract_rows(whole, d_pair)
    d_normed_in = contract_cols(d_pair, w_in)
    return (d_normed_in, grad_in, grad_kernel, grad_out, gain_total, bias_total)


def body(
    frames_in,
    lengths,
    out_grad,
    norm_gains,
    ffn1_up,
    ffn1_down,
    attn_in,
    pos_proj,
    pos_bias,
    attn_out,
    conv_in,
    depthwise,
    bn_scale,
    bn_shift,
    conv_out,
    ffn2_up,
    ffn2_down,
):
    unused, local_rows, model_width = frames_in.shape
    seq_len = local_rows * lax.axis_size("mp")
    dp_index = lax.axis_index("dp")
    own_length = lax.dynamic_slice_in_dim(lengths, dp_index, 1)[0]
    valid_keys = jnp.arange(seq_len) < own_length
    mask_col = valid_keys.astype(jnp.float32)[:, None]
    frame_count = jnp.sum(lengths).astype(jnp.float32)
    frames = frames_in.reshape(local_rows, model_width)
    _, whole_first, ffn_first = open_step(
        open_middle, [frames, norm_gains], [ffn1_up, ffn1_down], (0, 1), 0
    )
    small = jnp.concatenate([pos_bias, depthwise, bn_scale[None], bn_shift[None]], axis=0)
    table_low = position_table(seq_len, model_width).astype(jnp.bfloat16)
    if direct(model_width // lax.axis_size("dp")):
        packed = packed_rows(small)
    else:
        packed = small.T
    (after_first,), whole_attn, (attn_in_whole, pos_whole, attn_out_whole, packed) = between_step(
        functools.partial(forward_middle, 0.5, 1),
        ffn_forward(whole_first, ffn_first),
        [frames, norm_gains],
        1,
        fetch=[attn_in.reshape(attn_in.shape[0], -1), pos_proj, attn_out, packed],
        dims=(0, 0, 1, 0),
        ways=(False, True, True, True),
    )
    if direct(model_width // lax.axis_size("dp")):
        small = whole_rows(packed, small)
    else:
        small = packed.T
    taps = depthwise.shape[0]
    attn_held = (attn_in_whole, pos_whole, small[:2], attn_out_whole)
    conv_small = (
        small[2 : 2 + taps],
        small[2 + taps],
        small[3 + taps],
    )
    position = matmul(table_low, pos_whole).astype(jnp.bfloat16)
    attn_partial, *attn_saved = attention_forward(
        whole_attn, attn_held, position, own_length[None]
    )
    (after_attn,), whole_conv, (conv_in_whole, conv_out_whole, down_two) = between_step(
        functools.partial(forward_middle, 1.0, 2),
        attn_partial,
        [after_first, norm_gains],
        2,
        fetch=[conv_in.reshape(conv_in.shape[0], -1), conv_out, ffn2_down],
        dims=(0, 1, 1),
        ways=(False, False, True),
    )
    conv_held = (conv_in_whole, *conv_small, conv_out_whole)
    gate_value, logistic, padded, conved = conv_front(
        whole_conv, conv_held[0], conv_held[1], mask_col
    )
    stats = batch_stats(conved, mask_col, frame_count)
    normed_b, active = conv_tail(conved, stats, conv_held[2], conv_held[3])
    (after_conv,), whole_second, (up_two,) = between_step(
        functools.partial(forward_middle, 1.0, 3),
        matmul(active, conv_held[4]),
        [after_attn, norm_gains],
        3,
        fetch=[ffn2_up],
        dims=(0,),
        ways=(True,),
    )
    ffn_second = (up_two, down_two)
    (block_out, d_second, gain_five), whole_grads, _ = between_step(
        turn_middle,
        ffn_forward(whole_second, ffn_second),
        [after_conv, norm_gains, out_grad.reshape(local_rows, model_width)],
        4,
    )
    d_normed, grad_up, grad_down = ffn_backward(whole_second, ffn_second, whole_grads)
    (d_conv, gain_four), whole_grads, (total_up_two, total_down_two) = between_step(
        functools.partial(backward_middle, 1.0, 3),
        d_normed,
        [after_conv, norm_gains, d_second],
        5,
        grads=[grad_up, grad_down],
        dims=(0, 1),
        ways=(False, True),
    )
    d_normed, grad_conv_in, grad_kernel, grad_conv_out, gain_total, bias_total = conv_backward(
        whole_conv, conv_held, mask_col, stats, frame_count, whole_grads
    )
    (d_attn, gain_three), whole_grads, (total_conv_in, total_conv_out) = between_step(
        functools.partial(backward_middle, 1.0, 2),
        d_normed,
        [after_attn, norm_gains, d_conv],
        6,
        grads=[grad_conv_in, grad_conv_out],
        dims=(0, 1),
        ways=(False, True),
    )
    d_normed, grad_attn_in, grad_pos, grad_bias, grad_attn_out = attention_backward(
        whole_attn, attn_held, table_low, position, attn_saved, whole_grads
    )
    (d_first, gain_two), whole_grads, (total_attn_in, total_attn_out, total_pos) = between_step(
        functools.partial(backward_middle, 0.5, 1),
        d_normed,
        [after_first, norm_gains, d_attn],
        7,
        grads=[grad_attn_in, grad_attn_out, grad_pos],
        dims=(0, 1, 0),
        ways=(False, True, True),
    )
    d_normed, grad_up, grad_down = ffn_backward(whole_first, ffn_first, whole_grads)
    (in_grad,), small_grads, gains, (total_up_one, total_down_one) = close_step(
        close_middle,
        d_normed,
        jnp.concatenate([grad_bias, grad_kernel], axis=0),
        jnp.concatenate([gain_two, gain_three, gain_four, gain_five], axis=0),
        [frames, norm_gains, d_first],
        [grad_up, grad_down],
        (0, 1),
        (False, True),
        8,
    )
    gain_sum = jnp.concatenate([gains[4:], gains[:4]], axis=0)
    if direct(model_width // lax.axis_size("dp")):
        (
            block_out,
            in_grad,
            total_up_one,
            total_down_one,
            total_pos,
            total_attn_out,
            total_conv_out,
            total_up_two,
            total_down_two,
        ) = store_all(
            [
                block_out,
                in_grad,
                total_up_one,
                total_down_one,
                total_pos,
                total_attn_out,
                total_conv_out,
                total_up_two,
                total_down_two,
            ]
        )
    block = model_width // lax.axis_size("dp")
    piece_len = bn_scale.shape[0]
    own = dp_index * piece_len
    small_grads = lax.dynamic_slice_in_dim(small_grads, own, piece_len, axis=1)
    return (
        block_out.reshape(1, local_rows, model_width),
        in_grad.reshape(1, local_rows, model_width),
        gain_sum,
        total_up_one,
        total_down_one,
        total_attn_in.reshape(block, 3, -1),
        total_pos,
        small_grads[:2],
        total_attn_out,
        total_conv_in.reshape(block, 2, -1),
        small_grads[2:],
        lax.dynamic_slice_in_dim(gain_total, own, piece_len),
        lax.dynamic_slice_in_dim(bias_total, own, piece_len),
        total_conv_out,
        total_up_two,
        total_down_two,
    )


def solution(mesh):
    placed = (
        P("dp", "mp", None),
        P(),
        P("dp", "mp", None),
        P(),
        P("dp", "mp"),
        P("mp", "dp"),
        P("dp", None, "mp"),
        P("dp", "mp"),
        P(None, ("mp", "dp")),
        P("mp", "dp"),
        P("dp", None, "mp"),
        P(None, ("mp", "dp")),
        P(("mp", "dp")),
        P(("mp", "dp")),
        P("mp", "dp"),
        P("dp", "mp"),
        P("mp", "dp"),
    )
    return jax.shard_map(
        body,
        mesh=mesh,
        in_specs=placed,
        out_specs=(
            P("dp", "mp", None),
            P("dp", "mp", None),
            P(),
            P("dp", "mp"),
            P("mp", "dp"),
            P("dp", None, "mp"),
            P("dp", "mp"),
            P(None, ("mp", "dp")),
            P("mp", "dp"),
            P("dp", None, "mp"),
            P(None, ("mp", "dp")),
            P(("mp", "dp")),
            P(("mp", "dp")),
            P("mp", "dp"),
            P("dp", "mp"),
            P("mp", "dp"),
        ),
        check_vma=False,
    )
```

```python
import functools
import math

import jax
import jax.numpy as jnp
from jax import lax
from jax.experimental import pallas as pl
from jax.experimental.pallas import tpu as pltpu
from jax.sharding import PartitionSpec as P

HEAD = 128


norm_eps = 1e-05
batch_eps = 1e-05
masked_score = -1000000000.0


def matmul(left, right):
    return jnp.dot(left, right, preferred_element_type=jnp.float32)


def contract_rows(left, right):
    return lax.dot_general(
        left, right, (((0,), (0,)), ((), ())), preferred_element_type=jnp.float32
    )


def contract_cols(left, right):
    return lax.dot_general(
        left, right, (((1,), (1,)), ((), ())), preferred_element_type=jnp.float32
    )


def layer_norm(values, norm_gain):
    average = jnp.mean(values, axis=-1, keepdims=True)
    centred = values - average
    inv_std = lax.rsqrt(jnp.mean(centred * centred, axis=-1, keepdims=True) + norm_eps)
    return centred * inv_std * norm_gain


def silu_slope(values):
    logistic = jax.nn.sigmoid(values)
    return logistic * (1.0 + values * (1.0 - logistic))


def position_table(seq_len, model_width):
    fine = 32
    lane = jnp.arange(model_width)
    frequency = jnp.exp((lane // 2).astype(jnp.float32) * (-2.0 * math.log(10000.0) / model_width))
    coarse = (seq_len - 1 - fine * jnp.arange(2 * seq_len // fine)).astype(jnp.float32)
    wide = coarse[:, None] * frequency[None, :]
    small = -jnp.arange(fine).astype(jnp.float32)[:, None] * frequency[None, :]
    even = (lane % 2 == 0)[None, :]
    wide_sin, wide_cos = jnp.sin(wide), jnp.cos(wide)
    high = jnp.where(even, wide_sin, wide_cos)
    side = jnp.where(even, wide_cos, -wide_sin)
    table = high[:, None, :] * jnp.cos(small)[None] + side[:, None, :] * jnp.sin(small)[None]
    return table.reshape(2 * seq_len, model_width)


MESH = pl.DeviceIdType.MESH
VMEM_LIMIT = 24 * 1024 * 1024
CHUNKS = 4


def line_copy(src, dst, sems, index, axis, target):
    return pltpu.make_async_remote_copy(
        src_ref=src,
        dst_ref=dst,
        send_sem=sems.at[0, index],
        recv_sem=sems.at[1, index],
        device_id={axis: target},
        device_id_type=MESH,
    )


def bit_of(index, bit):
    return lax.rem(lax.div(index, bit), 2)


def partner(index, bit):
    return index + bit - 2 * bit * bit_of(index, bit)


def cube_bits(size, swap):
    bits = []
    bit = 2
    while bit < size:
        bits.append(bit)
        bit *= 2
    if swap:
        bits.reverse()
    return bits + [1]


def block_at(ref, dim, index, width):
    start = pl.multiple_of(index * width, width)
    return ref.at[pl.ds(start, width)] if dim == 0 else ref.at[:, pl.ds(start, width)]


def all_total_kernel(axis, in_ref, out_ref, slots, sems):
    size = lax.axis_size(axis)
    me = lax.axis_index(axis)
    barrier = pltpu.get_barrier_semaphore()
    targets = [lax.rem(me + step, size) for step in range(1, size)]
    for target in targets:
        pl.semaphore_signal(barrier, inc=1, device_id={axis: target}, device_id_type=MESH)
    pl.semaphore_wait(barrier, size - 1)
    copies = []
    for number, target in enumerate(targets):
        copy = line_copy(in_ref, slots.at[me], sems, number, axis, target)
        copy.start()
        copies.append(copy)
    slots[me] = in_ref[...]
    for copy in copies:
        copy.wait_recv()
    total = slots[0]
    for source in range(1, size):
        total = total + slots[source]
    out_ref[...] = total
    for copy in copies:
        copy.wait_send()


def all_total(values, axis, collective_id):
    size = lax.axis_size(axis)
    return pl.pallas_call(
        functools.partial(all_total_kernel, axis),
        out_shape=jax.ShapeDtypeStruct(values.shape, values.dtype),
        in_specs=[pl.BlockSpec(memory_space=pltpu.VMEM)],
        out_specs=pl.BlockSpec(memory_space=pltpu.VMEM),
        scratch_shapes=[
            pltpu.VMEM((size, *values.shape), values.dtype),
            pltpu.SemaphoreType.DMA((2, size - 1)),
        ],
        compiler_params=pltpu.CompilerParams(
            collective_id=collective_id, has_side_effects=True
        ),
        name="all_total",
    )(values)


def line_peers(axis):
    me, size = lax.axis_index(axis), lax.axis_size(axis)
    return jnp.minimum(me, 1) + jnp.minimum(size - 1 - me, 1)


def greet(line_axis, cube_axis, everyone):
    me, size = lax.axis_index(line_axis), lax.axis_size(line_axis)
    barrier = pltpu.get_barrier_semaphore()
    if everyone:
        for axis in (line_axis, cube_axis):
            here, count = lax.axis_index(axis), lax.axis_size(axis)
            for step in range(1, count):
                pl.semaphore_signal(
                    barrier, inc=1, device_id={axis: lax.rem(here + step, count)},
                    device_id_type=MESH,
                )
        pl.semaphore_wait(barrier, size - 1 + lax.axis_size(cube_axis) - 1)
        return

    @pl.when(me > 0)
    def _():
        pl.semaphore_signal(barrier, inc=1, device_id={line_axis: me - 1}, device_id_type=MESH)

    @pl.when(me < size - 1)
    def _():
        pl.semaphore_signal(barrier, inc=1, device_id={line_axis: me + 1}, device_id_type=MESH)

    bits = cube_bits(lax.axis_size(cube_axis), False) if cube_axis else []
    for bit in bits:
        pl.semaphore_signal(
            barrier, inc=1, device_id={cube_axis: partner(lax.axis_index(cube_axis), bit)},
            device_id_type=MESH,
        )
    pl.semaphore_wait(barrier, line_peers(line_axis) + len(bits))


class LineGather:
    def __init__(self, axis, out_ref, sems, chunks):
        self.axis, self.out, self.sems, self.chunks = axis, out_ref, sems, chunks
        self.size, self.me = lax.axis_size(axis), lax.axis_index(axis)
        self.rows = out_ref.shape[0] // self.size
        self.part = self.rows // chunks
        self.steps = self.size - 1

    def piece(self, index, chunk):
        start = pl.multiple_of(index * self.rows + chunk * self.part, self.part)
        return self.out.at[pl.ds(start, self.part)]

    def copy(self, way, step, index, chunk):
        place = self.piece(index, chunk)
        return line_copy(
            place, place, self.sems, (way * self.steps + step) * self.chunks + chunk, self.axis,
            self.me + 1 if way == 0 else self.me - 1,
        )

    def index(self, way, step):
        return self.me - step if way == 0 else self.me + step

    def held(self, way, step):
        return self.me >= step if way == 0 else self.me + step < self.size

    def onward(self, way):
        return self.me + 1 < self.size if way == 0 else self.me > 0

    def step(self, step, chunk):
        for way in range(2):
            if step > 0:
                @pl.when(self.held(way, step))
                def _():
                    self.copy(way, step - 1, self.index(way, step), chunk).wait_recv()

            if step < self.steps:
                @pl.when(jnp.logical_and(self.held(way, step), self.onward(way)))
                def _():
                    self.copy(way, step, self.index(way, step), chunk).start()

    def finish(self):
        for chunk in range(self.chunks):
            for step in range(self.steps):
                for way in range(2):
                    @pl.when(jnp.logical_and(self.held(way, step), self.onward(way)))
                    def _():
                        self.copy(way, step, self.index(way, step), chunk).wait_send()


class LineScatter:
    def __init__(self, axis, in_ref, total_ref, slots, staged, sems, chunks):
        self.axis, self.ins, self.total, self.chunks = axis, in_ref, total_ref, chunks
        self.slots, self.staged, self.sems = slots, staged, sems
        self.size, self.me = lax.axis_size(axis), lax.axis_index(axis)
        self.rows = total_ref.shape[0]
        self.part = self.rows // chunks
        self.first_way = lax.div(self.me, (self.size + 1) // 2)

    def mine(self, owner, chunk):
        start = pl.multiple_of(owner * self.rows + chunk * self.part, self.part)
        return self.ins.at[pl.ds(start, self.part)]

    def lines(self, chunk):
        return slice(chunk * self.part, (chunk + 1) * self.part)

    def copy(self, way, owner, chunk, src):
        return line_copy(
            src, self.slots.at[way, owner, self.lines(chunk)], self.sems,
            (way * self.size + owner) * self.chunks + chunk, self.axis,
            self.me + 1 - 2 * way,
        )

    def arrived(self, way, owner, chunk):
        return self.copy(way, owner, chunk, self.staged.at[way, owner, self.lines(chunk)])

    def place(self, way, step):
        owner = (1 - way) * (self.size - 1 - step) + way * step
        distance = (owner - self.me) * (1 - 2 * way)
        behind = (1 - way) * self.me + way * (self.size - 1 - self.me)
        return owner, distance, behind

    def lead(self, step, chunk):
        for way in range(2):
            owner, distance, behind = self.place(way, step)

            @pl.when(jnp.logical_and(distance > 0, behind == 0))
            def _():
                self.copy(way, owner, chunk, self.mine(owner, chunk)).start()

    def hop(self, way, step, chunk):
        owner, distance, behind = self.place(way, step)

        @pl.when(jnp.logical_and(distance > 0, behind > 0))
        def _():
            lines = self.lines(chunk)
            self.arrived(way, owner, chunk).wait_recv()
            self.staged[way, owner, lines] = (
                self.mine(owner, chunk)[...].astype(jnp.float32)
                + self.slots[way, owner, lines].astype(jnp.float32)
            ).astype(self.staged.dtype)
            self.arrived(way, owner, chunk).start()

    def run(self, first=None, halfway=None):
        marks = [(step, chunk) for step in range(self.size - 1) for chunk in range(self.chunks)]
        for mark in marks:
            self.lead(*mark)
        if first:
            first()
        for number in range(len(marks) + self.chunks):
            if halfway and number == max(len(marks) // 2 - 1, 1):
                halfway()
            if number < len(marks):
                self.hop(self.first_way, *marks[number])
            if number >= self.chunks:
                self.hop(1 - self.first_way, *marks[number - self.chunks])

    def result(self, chunk):
        lines = self.lines(chunk)
        self.total[lines] = self.mine(self.me, chunk)[...].astype(jnp.float32)
        for way in range(2):
            @pl.when(self.me > 0 if way == 0 else self.me < self.size - 1)
            def _():
                self.arrived(way, self.me, chunk).wait_recv()
                self.total[lines] += self.slots[way, self.me, lines].astype(jnp.float32)

        return self.total[lines]

    def finish(self):
        for chunk in range(self.chunks):
            for owner in range(self.size):
                for way in range(2):
                    @pl.when(self.me < owner if way == 0 else self.me > owner)
                    def _():
                        self.arrived(way, owner, chunk).wait_send()


class CubeGather:
    def __init__(self, axis, dims, ways, ins, outs, sems):
        self.axis, self.dims, self.ways = axis, dims, ways
        self.ins, self.outs, self.sems = ins, outs, sems
        self.size, self.me = lax.axis_size(axis), lax.axis_index(axis)
        self.stages = len(cube_bits(self.size, False))
        self.started = []
        self.waiting = [[] for _ in ins]

    def step(self, stage):
        per = self.size - 1
        for which in range(len(self.ins)):
            width = self.ins[which].shape[self.dims[which]]
            bits = cube_bits(self.size, self.ways[which])
            for copy in self.waiting[which]:
                copy.wait_recv()
            self.waiting[which] = []
            if stage == 0:
                block_at(self.outs[which], self.dims[which], self.me, width)[...] = (
                    self.ins[which][...]
                )
            if stage == self.stages:
                continue
            held = [self.me]
            for bit in bits[:stage]:
                held = held + [partner(index, bit) for index in held]
            for number, index in enumerate(held):
                place = block_at(self.outs[which], self.dims[which], index, width)
                copy = line_copy(
                    self.ins[which] if stage == 0 else place, place, self.sems,
                    which * per + 2**stage - 1 + number, self.axis, partner(self.me, bits[stage]),
                )
                copy.start()
                self.waiting[which].append(copy)
            self.started.extend(self.waiting[which])

    def finish(self):
        for copy in self.started:
            copy.wait_send()


class CubeScatter:
    def __init__(self, axis, dims, ways, ins, outs, slots, sems):
        self.axis, self.dims, self.ways = axis, dims, ways
        self.ins, self.outs, self.slots, self.sems = ins, outs, slots, sems
        self.size, self.me = lax.axis_size(axis), lax.axis_index(axis)
        self.stages = len(cube_bits(self.size, False))
        self.started = []

    def slot(self, which, stage, number):
        return self.slots[which].at[self.size - self.size // 2**stage + number]

    def sets(self, which, stage):
        bits = cube_bits(self.size, self.ways[which])[::-1]
        held = [self.me]
        for bit in bits[stage + 1 :]:
            held = held + [partner(index, bit) for index in held]
        return bits[stage], held

    def send(self, which, stage):
        width = self.outs[which].shape[self.dims[which]]
        bit, held = self.sets(which, stage)
        for number, index in enumerate(held):
            if stage == 0:
                src = block_at(self.ins[which], self.dims[which], partner(index, bit), width)
            else:
                src = self.slot(which, stage - 1, 2 * number + 1)
            copy = line_copy(
                src, self.slot(which, stage, number), self.sems,
                which * (self.size - 1) + self.size - self.size // 2**stage + number,
                self.axis, partner(self.me, bit),
            )
            copy.start()
            self.started.append((which, stage, copy))

    def receive(self, which, stage):
        width = self.outs[which].shape[self.dims[which]]
        _, held = self.sets(which, stage)
        for copy in [c for w, s, c in self.started if (w, s) == (which, stage)]:
            copy.wait_recv()
        for number, index in enumerate(held):
            got = self.slot(which, stage, number)
            if stage == 0:
                mine = block_at(self.ins[which], self.dims[which], index, width)
            else:
                mine = self.slot(which, stage - 1, 2 * number)
            total = got[...].astype(jnp.float32) + mine[...].astype(jnp.float32)
            if stage == self.stages - 1:
                self.outs[which][...] = total
            else:
                got[...] = total.astype(self.slots[which].dtype)

    def step(self, stage):
        for which in range(len(self.ins)):
            if stage > 0:
                self.receive(which, stage - 1)
            if stage < self.stages:
                self.send(which, stage)

    def finish(self):
        for _, _, copy in self.started:
            copy.wait_send()


class AllTotal:
    def __init__(self, axis, slots, sems):
        self.axis, self.slots, self.sems = axis, slots, sems
        self.size, self.me = lax.axis_size(axis), lax.axis_index(axis)
        self.copies = []

    def start(self):
        for step in range(1, self.size):
            copy = line_copy(
                self.slots.at[self.me], self.slots.at[self.me], self.sems, step - 1, self.axis,
                lax.rem(self.me + step, self.size),
            )
            copy.start()
            self.copies.append(copy)

    def result(self):
        for copy in self.copies:
            copy.wait_recv()
        total = self.slots[0]
        for source in range(1, self.size):
            total = total + self.slots[source]
        return total

    def finish(self):
        for copy in self.copies:
            copy.wait_send()


def open_kernel(middle, counts, chunks, dims, ways, *refs):
    local_count, mid_count = counts
    count = len(dims)
    refs = list(refs)
    take = lambda number: [refs.pop(0) for _ in range(number)]
    locals_, ins = take(local_count), take(count)
    mids, (whole,), outs = take(mid_count), take(1), take(count)
    gather_sems, cube_sems = refs
    fetch = CubeGather("dp", dims, ways, ins, outs, cube_sems)
    rows = LineGather("mp", whole, gather_sems, chunks)
    greet("mp", "dp", False)
    fetch.step(0)
    values, normed = middle(None, *[ref[...] for ref in locals_])
    for ref, value in zip(mids, values):
        ref[...] = value
    for chunk in range(chunks):
        part = rows.part
        rows.piece(rows.me, chunk)[...] = normed[chunk * part : (chunk + 1) * part]
        rows.step(0, chunk)
    for step in range(1, max(rows.steps, fetch.stages) + 1):
        if step <= fetch.stages:
            fetch.step(step)
        if step <= rows.steps:
            for chunk in range(chunks):
                rows.step(step, chunk)
    rows.finish()
    fetch.finish()


def between_kernel(middle, counts, chunks, fetches, dims, ways, *refs):
    local_count, mid_count = counts
    count = len(dims)
    refs = list(refs)
    take = lambda number: [refs.pop(0) for _ in range(number)]
    (partial,), locals_, ins = take(1), take(local_count), take(count)
    mids, (whole,), outs = take(mid_count), take(1), take(count)
    (total, slots, staged, scatter_sems, gather_sems), refs = refs[:5], refs[5:]
    sums = LineScatter("mp", partial, total, slots, staged, scatter_sems, chunks)
    rows = LineGather("mp", whole, gather_sems, chunks)
    beside, stages = None, 0
    if count:
        if fetches:
            beside = CubeGather("dp", dims, ways, ins, outs, refs[0])
        else:
            beside = CubeScatter("dp", dims, ways, ins, outs, refs[:count], refs[count])
        stages = beside.stages + 1
    greet("mp", "dp" if count else None, False)
    stage = 0
    if stages:
        sums.run(lambda: beside.step(0), lambda: beside.step(1))
        stage = 2
    else:
        sums.run()
    for chunk in range(chunks):
        lines = sums.lines(chunk)
        picked = [ref[lines] if ref.shape[0] == sums.rows else ref[...] for ref in locals_]
        values, normed = middle(sums.result(chunk), *picked)
        rows.piece(rows.me, chunk)[...] = normed
        rows.step(0, chunk)
        for ref, value in zip(mids, values):
            if ref.shape[0] == sums.rows:
                ref[lines] = value
            elif chunk == 0:
                ref[...] = value
            else:
                ref[...] += value
    for step in range(1, rows.steps + 1):
        if 1 < step and stage < stages:
            beside.step(stage)
            stage += 1
        for chunk in range(chunks):
            rows.step(step, chunk)
    for stage in range(stage, stages):
        beside.step(stage)
    if count:
        beside.finish()
    sums.finish()
    rows.finish()


def close_kernel(middle, counts, chunks, dims, ways, *refs):
    local_count, mid_count = counts
    count = len(dims)
    refs = list(refs)
    take = lambda number: [refs.pop(0) for _ in range(number)]
    (partial, small, gains), locals_, ins = take(3), take(local_count), take(count)
    mids, (small_out, gains_out), outs = take(mid_count), take(2), take(count)
    (total, slots, staged, scatter_sems), refs = refs[:4], refs[4:]
    (small_slots, small_sems, gain_slots, gain_sems, last_slots, last_sems), refs = refs[:6], refs[6:]
    sums = LineScatter("mp", partial, total, slots, staged, scatter_sems, chunks)
    grads = CubeScatter("dp", dims, ways, ins, outs, refs[:count], refs[count])
    little = AllTotal("dp", small_slots, small_sems)
    near, far = AllTotal("dp", gain_slots, gain_sems), AllTotal("mp", last_slots, last_sems)
    little.slots[little.me] = small[...]
    greet("mp", "dp", True)

    def first():
        grads.step(0)
        little.start()

    sums.run(first, lambda: grads.step(1))
    total_rows = jnp.concatenate([sums.result(chunk) for chunk in range(chunks)], axis=0)
    values, gain = middle(total_rows, *[ref[...] for ref in locals_])
    near.slots[near.me] = jnp.concatenate([gains[...], gain], axis=0)
    near.start()
    for ref, value in zip(mids, values):
        ref[...] = value
    grads.step(2)
    far.slots[far.me] = near.result()
    far.start()
    for stage in range(3, grads.stages + 1):
        grads.step(stage)
    small_out[...] = little.result()
    gains_out[...] = far.result()
    for task in (grads, sums, little, near, far):
        task.finish()


def shapes_of(arrays):
    return [jax.ShapeDtypeStruct(value.shape, value.dtype) for value in arrays]


def call_step(kernel, inputs, out_shape, scratch, collective_id, name):
    vmem = pl.BlockSpec(memory_space=pltpu.VMEM)
    return pl.pallas_call(
        kernel,
        out_shape=out_shape,
        in_specs=[vmem] * len(inputs),
        out_specs=[vmem] * len(out_shape),
        scratch_shapes=scratch,
        compiler_params=pltpu.CompilerParams(
            collective_id=collective_id, has_side_effects=True, vmem_limit_bytes=VMEM_LIMIT
        ),
        name=name,
    )(*inputs)


def line_scratch(rows, width, chunks):
    size = lax.axis_size("mp")
    return [
        pltpu.VMEM((rows, width), jnp.float32),
        pltpu.VMEM((2, size, rows, width), jnp.bfloat16),
        pltpu.VMEM((2, size, rows, width), jnp.bfloat16),
        pltpu.SemaphoreType.DMA((2, 2 * size * chunks)),
    ]


def cube_scratch(arrays, dims):
    size = lax.axis_size("dp")
    shapes, slots = [], []
    for array, dim in zip(arrays, dims):
        shape = list(array.shape)
        shape[dim] //= size
        shapes.append(jax.ShapeDtypeStruct(tuple(shape), jnp.float32))
        slots.append(pltpu.VMEM((size - 1, *shape), array.dtype))
    if arrays:
        slots.append(pltpu.SemaphoreType.DMA((2, len(arrays) * (size - 1))))
    return shapes, slots


def plain_totals(grads, dims):
    return [
        lax.psum_scatter(grad, "dp", scatter_dimension=dim, tiled=True).astype(jnp.float32)
        for grad, dim in zip(grads, dims)
    ]


def direct(block):
    size = lax.axis_size("dp")
    return size & (size - 1) == 0 and block % 128 == 0


def fetched_shapes(arrays, dims):
    size, shapes = lax.axis_size("dp"), []
    for array, dim in zip(arrays, dims):
        shape = list(array.shape)
        shape[dim] *= size
        shapes.append(jax.ShapeDtypeStruct(tuple(shape), array.dtype))
    return shapes


def plain_fetch(arrays, dims):
    return [lax.all_gather(array, "dp", axis=dim, tiled=True) for array, dim in zip(arrays, dims)]


def packed_rows(small):
    return jnp.pad(small, ((0, 16 - small.shape[0]), (0, 128 - small.shape[1])))


def whole_rows(packed, small):
    size, (count, lanes) = lax.axis_size("dp"), small.shape
    packed = packed.reshape(size, 16, 128)[:, :count, :lanes]
    return packed.transpose(1, 0, 2).reshape(count, size * lanes)


def open_step(middle, locals_, arrays, dims, collective_id):
    if not direct(arrays[0].shape[dims[0]]):
        mids, normed = middle(None, *locals_)
        return mids, lax.all_gather(normed, "mp", axis=0, tiled=True), plain_fetch(arrays, dims)
    ways = [index % 2 == 1 for index in range(len(dims))]
    mid_shapes, normed_shape = jax.eval_shape(functools.partial(middle, None), *locals_)
    rows, width = normed_shape.shape
    whole_shape = jax.ShapeDtypeStruct((rows * lax.axis_size("mp"), width), normed_shape.dtype)
    count = len(mid_shapes)
    result = call_step(
        functools.partial(open_kernel, middle, (len(locals_), count), CHUNKS, dims, ways),
        [*locals_, *arrays],
        [*mid_shapes, whole_shape, *fetched_shapes(arrays, dims)],
        [
            pltpu.SemaphoreType.DMA((2, 2 * (lax.axis_size("mp") - 1) * CHUNKS)),
            pltpu.SemaphoreType.DMA((2, len(arrays) * (lax.axis_size("dp") - 1))),
        ],
        collective_id,
        "open_step",
    )
    return result[:count], result[count], result[count + 1 :]


def between_step(
    middle, partial_value, locals_, collective_id, grads=(), fetch=(), dims=(), ways=()
):
    partial_value = partial_value.astype(jnp.bfloat16)
    grads = [grad.astype(jnp.bfloat16) for grad in grads]
    size = lax.axis_size("mp")
    rows, width = partial_value.shape[0] // size, partial_value.shape[1]
    if not direct(width // lax.axis_size("dp")):
        total = lax.psum_scatter(partial_value, "mp", scatter_dimension=0, tiled=True)
        mids, normed = middle(total.astype(jnp.float32), *locals_)
        others = plain_fetch(fetch, dims) if fetch else plain_totals(grads, dims)
        return mids, lax.all_gather(normed, "mp", axis=0, tiled=True), others
    total = jax.ShapeDtypeStruct((rows, width), jnp.float32)
    mid_shapes, normed_shape = jax.eval_shape(middle, total, *locals_)
    if fetch:
        shapes = fetched_shapes(fetch, dims)
        scratch = [pltpu.SemaphoreType.DMA((2, len(fetch) * (lax.axis_size("dp") - 1)))]
    else:
        shapes, scratch = cube_scratch(grads, dims)
    count = len(mid_shapes)
    result = call_step(
        functools.partial(
            between_kernel, middle, (len(locals_), count), CHUNKS, bool(fetch), dims, ways
        ),
        [partial_value, *locals_, *grads, *fetch],
        [
            *mid_shapes,
            jax.ShapeDtypeStruct((rows * size, width), normed_shape.dtype),
            *shapes,
        ],
        line_scratch(rows, width, CHUNKS)
        + [pltpu.SemaphoreType.DMA((2, 2 * (size - 1) * CHUNKS))]
        + scratch,
        collective_id,
        "between_step",
    )
    return result[:count], result[count], result[count + 1 :]


def close_step(middle, partial_value, small, gains, locals_, grads, dims, ways, collective_id):
    partial_value = partial_value.astype(jnp.bfloat16)
    grads = [grad.astype(jnp.bfloat16) for grad in grads]
    size, dp_size = lax.axis_size("mp"), lax.axis_size("dp")
    rows, width = partial_value.shape[0] // size, partial_value.shape[1]
    if not direct(width // dp_size):
        total = lax.psum_scatter(partial_value, "mp", scatter_dimension=0, tiled=True)
        mids, gain = middle(total.astype(jnp.float32), *locals_)
        gains = lax.psum(jnp.concatenate([gains, gain], axis=0), ("dp", "mp"))
        return mids, lax.psum(small, "dp"), gains, plain_totals(grads, dims)
    total = jax.ShapeDtypeStruct((rows, width), jnp.float32)
    mid_shapes, gain_shape = jax.eval_shape(middle, total, *locals_)
    gains_shape = jax.ShapeDtypeStruct((gains.shape[0] + 1, width), jnp.float32)
    shapes, slots = cube_scratch(grads, dims)
    count = len(mid_shapes)
    result = call_step(
        functools.partial(close_kernel, middle, (len(locals_), count), CHUNKS, dims, ways),
        [partial_value, small, gains, *locals_, *grads],
        [*mid_shapes, *shapes_of([small]), gains_shape, *shapes],
        line_scratch(rows, width, CHUNKS)
        + [
            pltpu.VMEM((dp_size, *small.shape), jnp.float32),
            pltpu.SemaphoreType.DMA((2, dp_size - 1)),
            pltpu.VMEM((dp_size, *gains_shape.shape), jnp.float32),
            pltpu.SemaphoreType.DMA((2, dp_size - 1)),
            pltpu.VMEM((size, *gains_shape.shape), jnp.float32),
            pltpu.SemaphoreType.DMA((2, size - 1)),
        ]
        + slots,
        collective_id,
        "close_step",
    )
    return result[:count], result[count], result[count + 1], result[count + 2 :]


def forward_middle(scale, row, total, residual, norm_gains):
    residual = residual.astype(jnp.float32)
    if total is not None:
        residual = residual + scale * total
    return [residual], layer_norm(residual, norm_gains[row : row + 1]).astype(jnp.bfloat16)


def open_middle(total, frames, norm_gains):
    return [], layer_norm(frames.astype(jnp.float32), norm_gains[0:1]).astype(jnp.bfloat16)


def norm_back(values, norm_gain, upstream):
    centred = values - jnp.mean(values, axis=-1, keepdims=True)
    inv_std = lax.rsqrt(jnp.mean(centred * centred, axis=-1, keepdims=True) + norm_eps)
    normed = centred * inv_std
    scaled = upstream * norm_gain
    d_values = inv_std * (
        scaled
        - jnp.mean(scaled, axis=-1, keepdims=True)
        - normed * jnp.mean(scaled * normed, axis=-1, keepdims=True)
    )
    return d_values, jnp.sum(upstream * normed, axis=0, keepdims=True)


def turn_middle(total, residual, norm_gains, out_grad):
    after = residual + 0.5 * total
    gain = norm_gains[4:5]
    d_after, d_gain = norm_back(after, gain, out_grad.astype(jnp.float32))
    block_out = layer_norm(after, gain).astype(jnp.bfloat16)
    return [block_out, d_after, d_gain], (0.5 * d_after).astype(jnp.bfloat16)


def backward_middle(scale, row, total, values, norm_gains, upstream):
    d_branch, d_gain = norm_back(values.astype(jnp.float32), norm_gains[row : row + 1], total)
    d_values = upstream + d_branch
    return [d_values, d_gain], (scale * d_values).astype(jnp.bfloat16)


def close_middle(total, values, norm_gains, upstream):
    d_branch, d_gain = norm_back(values.astype(jnp.float32), norm_gains[0:1], total)
    return [upstream + d_branch], d_gain


def store_kernel(*refs):
    count = len(refs) // 2
    ins, outs, sems = refs[:count], refs[count : 2 * count], refs[2 * count]
    copies = [
        pltpu.make_async_copy(ins[number], outs[number], sems.at[number])
        for number in range(count)
    ]
    for copy in copies:
        copy.start()
    for copy in copies:
        copy.wait()


def store_all(arrays):
    return pl.pallas_call(
        store_kernel,
        out_shape=shapes_of(arrays),
        in_specs=[pl.BlockSpec(memory_space=pltpu.VMEM)] * len(arrays),
        out_specs=[pl.BlockSpec(memory_space=pl.ANY)] * len(arrays),
        scratch_shapes=[pltpu.SemaphoreType.DMA((len(arrays),))],
        compiler_params=pltpu.CompilerParams(vmem_limit_bytes=VMEM_LIMIT),
        name="store_all",
    )(*arrays)


def dp_total(values):
    if direct(128):
        return all_total(values, "dp", 9)
    return lax.psum(values, "dp")


def ffn_forward(whole, weights):
    w_up, w_down = weights
    hidden = matmul(whole, w_up)
    return matmul(jax.nn.silu(hidden).astype(jnp.bfloat16), w_down)


def ffn_backward(whole, weights, grad_whole):
    w_up, w_down = weights
    hidden = matmul(whole, w_up)
    active = jax.nn.silu(hidden).astype(jnp.bfloat16)
    grad_down = contract_rows(active, grad_whole)
    d_hidden = (contract_cols(grad_whole, w_down) * silu_slope(hidden)).astype(jnp.bfloat16)
    grad_up = contract_rows(whole, d_hidden)
    return (contract_cols(d_hidden, w_up), grad_up, grad_down)


def place_position(position_ref, block, rows, seq_len):
    start = pl.multiple_of(seq_len - rows - block * rows, rows)
    return position_ref.at[pl.ds(start, seq_len + rows)]


def attention_kernel(
    scaling, length_ref, whole_ref, in_ref, bias_ref, position_ref, out_w_ref,
    partial_ref, probs_ref, context_ref, query_u_ref, query_v_ref, key_ref, value_ref,
):
    block = pl.program_id(0)
    seq_len, local_width = key_ref.shape
    rows = partial_ref.shape[0]

    @pl.when(block == 0)
    def _():
        projected = matmul(whole_ref[...], in_ref[...])
        queries = projected[:, :local_width]
        query_u_ref[...] = ((queries + bias_ref[0:1]) * scaling).astype(jnp.bfloat16)
        query_v_ref[...] = ((queries + bias_ref[1:2]) * scaling).astype(jnp.bfloat16)
        key_ref[...] = projected[:, local_width : 2 * local_width].astype(jnp.bfloat16)
        value_ref[...] = projected[:, 2 * local_width :].astype(jnp.bfloat16)

    here = pl.ds(pl.multiple_of(block * rows, rows), rows)
    valid = lax.broadcasted_iota(jnp.int32, (rows, seq_len), 1) < length_ref[0]
    nearby = place_position(position_ref, block, rows, seq_len)
    pieces = []
    for head in range(local_width // HEAD):
        lanes = slice(head * HEAD, (head + 1) * HEAD)
        content = contract_cols(query_u_ref[here, lanes], key_ref[:, lanes])
        zeds = contract_cols(query_v_ref[here, lanes], nearby[:, lanes])
        shifted = pltpu.roll(zeds, seq_len + 1, 1, stride=1, stride_axis=0)[:, :seq_len]
        scores = jnp.where(valid, content + shifted, masked_score)
        exponent = jnp.exp(scores - jnp.max(scores, axis=-1, keepdims=True))
        probs = exponent / jnp.sum(exponent, axis=-1, keepdims=True)
        probs_ref[head] = probs
        pieces.append(matmul(probs.astype(jnp.bfloat16), value_ref[:, lanes]).astype(jnp.bfloat16))
    context = jnp.concatenate(pieces, axis=1)
    context_ref[...] = context
    partial_ref[...] = matmul(context, out_w_ref[...]).astype(jnp.bfloat16)


def attention_forward(whole, weights, position, own_length):
    w_in, w_pos, bias_pair, w_out = weights
    seq_len, model_width = whole.shape
    local_width = w_out.shape[0]
    heads_here = local_width // HEAD
    rows = 128
    full = pl.BlockSpec(memory_space=pltpu.VMEM)
    low = jnp.bfloat16
    return pl.pallas_call(
        functools.partial(attention_kernel, HEAD ** (-0.5)),
        grid=(seq_len // rows,),
        out_shape=[
            jax.ShapeDtypeStruct((seq_len, model_width), low),
            jax.ShapeDtypeStruct((heads_here, seq_len, seq_len), jnp.float32),
        ]
        + [jax.ShapeDtypeStruct((seq_len, local_width), low)] * 5,
        in_specs=[pl.BlockSpec(memory_space=pltpu.SMEM)] + [full] * 5,
        out_specs=[
            pl.BlockSpec((rows, model_width), lambda block: (block, 0)),
            pl.BlockSpec((heads_here, rows, seq_len), lambda block: (0, block, 0)),
            pl.BlockSpec((rows, local_width), lambda block: (block, 0)),
        ]
        + [full] * 4,
        compiler_params=pltpu.CompilerParams(vmem_limit_bytes=VMEM_LIMIT),
        name="attention_forward",
    )(own_length, whole, w_in, bias_pair.astype(jnp.float32), position, w_out)


def attention_back_kernel(
    scaling, grad_ref, out_w_ref, probs_ref, query_u_ref, query_v_ref, key_ref, value_ref,
    position_ref, d_projected_ref, d_position_ref, bias_ref, d_keys, d_values, d_places,
):
    block = pl.program_id(0)
    seq_len, local_width = key_ref.shape
    rows = grad_ref.shape[0]

    @pl.when(block == 0)
    def _():
        d_keys[...] = jnp.zeros_like(d_keys)
        d_values[...] = jnp.zeros_like(d_values)
        d_places[...] = jnp.zeros_like(d_places)
        bias_ref[...] = jnp.zeros_like(bias_ref)

    here = pl.ds(pl.multiple_of(block * rows, rows), rows)
    nearby = place_position(position_ref, block, rows, seq_len)
    d_nearby = place_position(d_places, block, rows, seq_len)
    upside = (
        lax.broadcasted_iota(jnp.int32, (rows, rows), 0)
        + lax.broadcasted_iota(jnp.int32, (rows, rows), 1)
        == rows - 1
    ).astype(jnp.bfloat16)
    d_context_all = contract_cols(grad_ref[...], out_w_ref[...]).astype(jnp.bfloat16)
    for head in range(local_width // HEAD):
        lanes = slice(head * HEAD, (head + 1) * HEAD)
        d_context = d_context_all[:, lanes]
        probs = probs_ref[head]
        d_probs = contract_cols(d_context, value_ref[:, lanes])
        inner = jnp.sum(probs * d_probs, axis=-1, keepdims=True)
        d_scores = (probs * (d_probs - inner)).astype(jnp.bfloat16)
        d_values[:, lanes] += contract_rows(probs.astype(jnp.bfloat16), d_context)
        d_keys[:, lanes] += contract_rows(d_scores, query_u_ref[here, lanes])
        grad_u = matmul(d_scores, key_ref[:, lanes]) * scaling
        turned = matmul(upside, d_scores)
        turned = jnp.concatenate([turned, jnp.zeros((rows, rows), jnp.float32)], axis=1)
        turned = pltpu.roll(turned, 0, 1, stride=1, stride_axis=0).astype(jnp.bfloat16)
        d_zeds = matmul(upside, turned).astype(jnp.bfloat16)
        grad_v = matmul(d_zeds, nearby[:, lanes]) * scaling
        d_nearby[:, lanes] += contract_rows(d_zeds, query_v_ref[here, lanes])
        d_projected_ref[here, lanes] = (grad_u + grad_v).astype(jnp.bfloat16)
        bias_ref[0:1, lanes] += jnp.sum(grad_u, axis=0, keepdims=True)
        bias_ref[1:2, lanes] += jnp.sum(grad_v, axis=0, keepdims=True)

    @pl.when(block == pl.num_programs(0) - 1)
    def _():
        d_projected_ref[:, local_width : 2 * local_width] = d_keys[...].astype(jnp.bfloat16)
        d_projected_ref[:, 2 * local_width :] = d_values[...].astype(jnp.bfloat16)
        d_position_ref[...] = d_places[...].astype(jnp.bfloat16)


def attention_backward(whole, weights, table_low, position, saved, grad_whole):
    w_in, w_pos, bias_pair, w_out = weights
    probs, context, query_u, query_v, key_rows, value_rows = saved
    seq_len, model_width = whole.shape
    local_width = w_out.shape[0]
    heads_here = local_width // HEAD
    rows = 128
    full = pl.BlockSpec(memory_space=pltpu.VMEM)
    d_projected, d_position, grad_bias = pl.pallas_call(
        functools.partial(attention_back_kernel, HEAD ** (-0.5)),
        grid=(seq_len // rows,),
        out_shape=[
            jax.ShapeDtypeStruct((seq_len, 3 * local_width), jnp.bfloat16),
            jax.ShapeDtypeStruct((2 * seq_len, local_width), jnp.bfloat16),
            jax.ShapeDtypeStruct((2, local_width), jnp.float32),
        ],
        in_specs=[
            pl.BlockSpec((rows, model_width), lambda block: (block, 0)),
            full,
            pl.BlockSpec((heads_here, rows, seq_len), lambda block: (0, block, 0)),
        ]
        + [full] * 5,
        out_specs=[full] * 3,
        scratch_shapes=[
            pltpu.VMEM((seq_len, local_width), jnp.float32),
            pltpu.VMEM((seq_len, local_width), jnp.float32),
            pltpu.VMEM((2 * seq_len, local_width), jnp.float32),
        ],
        compiler_params=pltpu.CompilerParams(vmem_limit_bytes=VMEM_LIMIT),
        name="attention_backward",
    )(grad_whole, w_out, probs, query_u, query_v, key_rows, value_rows, position)
    grad_in = contract_rows(whole, d_projected)
    d_normed = contract_cols(d_projected, w_in)
    grad_pos = contract_rows(table_low, d_position)
    grad_out = contract_rows(context, grad_whole)
    return (d_normed, grad_in, grad_pos, grad_bias, grad_out)


def conv_front(whole, w_in, kernel, mask_col):
    seq_len, model_width = whole.shape
    local_width = w_in.shape[1] // 2
    glu_in = matmul(whole, w_in)
    gate_value = glu_in[:, :local_width]
    logistic = jax.nn.sigmoid(glu_in[:, local_width:])
    glu_out = gate_value * logistic * mask_col
    tap_count = kernel.shape[0]
    half_taps = (tap_count - 1) // 2
    padded = jnp.pad(glu_out, ((half_taps, half_taps), (0, 0)))
    kernel_float = kernel.astype(jnp.float32)
    conved = kernel_float[0] * padded[0:seq_len]
    for tap_index in range(1, tap_count):
        conved = conved + kernel_float[tap_index] * padded[tap_index : tap_index + seq_len]
    return (gate_value, logistic, padded, conved)


def batch_stats(conved, mask_col, frame_count):
    local_sum = jnp.sum(conved * mask_col, axis=0)
    local_squares = jnp.sum(conved * conved * mask_col, axis=0)
    total_sum, total_squares = dp_total(jnp.stack([local_sum, local_squares]))
    average = total_sum / frame_count
    variance = total_squares / frame_count - average * average
    return (average, lax.rsqrt(variance + batch_eps))


def conv_tail(conved, stats, bn_gain, bn_bias):
    average, inv_std = stats
    normed_b = (conved - average) * inv_std * bn_gain.astype(jnp.float32) + bn_bias.astype(
        jnp.float32
    )
    return (normed_b, jax.nn.silu(normed_b).astype(jnp.bfloat16))


def conv_backward(whole, weights, mask_col, stats, frame_count, grad_whole):
    w_in, kernel, bn_gain, bn_bias, w_out = weights
    seq_len, model_width = whole.shape
    gate_value, logistic, padded, conved = conv_front(whole, w_in, kernel, mask_col)
    normed_b, active = conv_tail(conved, stats, bn_gain, bn_bias)
    average, inv_std = stats
    grad_out = contract_rows(active, grad_whole)
    d_normed = contract_cols(grad_whole, w_out) * silu_slope(normed_b)
    centred = (conved - average) * inv_std
    bias_total, gain_total = dp_total(
        jnp.stack([jnp.sum(d_normed, axis=0), jnp.sum(d_normed * centred, axis=0)])
    )
    d_conved = (
        bn_gain.astype(jnp.float32)
        * inv_std
        * (d_normed - mask_col * (bias_total + centred * gain_total) / frame_count)
    )
    tap_count = kernel.shape[0]
    half_taps = (tap_count - 1) // 2
    kernel_float = kernel.astype(jnp.float32)
    d_padded = jnp.pad(d_conved, ((half_taps, half_taps), (0, 0)))
    d_glu = kernel_float[0] * d_padded[tap_count - 1 : tap_count - 1 + seq_len]
    for tap_index in range(1, tap_count):
        d_glu = (
            d_glu
            + kernel_float[tap_index]
            * d_padded[tap_count - 1 - tap_index : tap_count - 1 - tap_index + seq_len]
        )
    grad_kernel = jnp.stack(
        [
            jnp.sum(d_conved * padded[tap_index : tap_index + seq_len], axis=0)
            for tap_index in range(tap_count)
        ]
    )
    d_glu = d_glu * mask_col
    d_pair = jnp.concatenate(
        [d_glu * logistic, d_glu * gate_value * logistic * (1.0 - logistic)], axis=1
    ).astype(jnp.bfloat16)
    grad_in = contract_rows(whole, d_pair)
    d_normed_in = contract_cols(d_pair, w_in)
    return (d_normed_in, grad_in, grad_kernel, grad_out, gain_total, bias_total)


def body(
    frames_in,
    lengths,
    out_grad,
    norm_gains,
    ffn1_up,
    ffn1_down,
    attn_in,
    pos_proj,
    pos_bias,
    attn_out,
    conv_in,
    depthwise,
    bn_scale,
    bn_shift,
    conv_out,
    ffn2_up,
    ffn2_down,
):
    unused, local_rows, model_width = frames_in.shape
    seq_len = local_rows * lax.axis_size("mp")
    dp_index = lax.axis_index("dp")
    picked = jnp.where(jnp.arange(lengths.shape[0]) == dp_index, lengths, 0)
    own_length = jnp.sum(picked)
    valid_keys = jnp.arange(seq_len) < own_length
    mask_col = valid_keys.astype(jnp.float32)[:, None]
    frame_count = jnp.sum(lengths).astype(jnp.float32)
    frames = frames_in.reshape(local_rows, model_width)
    _, whole_first, ffn_first = open_step(
        open_middle, [frames, norm_gains], [ffn1_up, ffn1_down], (0, 1), 0
    )
    small = jnp.concatenate([pos_bias, depthwise, bn_scale[None], bn_shift[None]], axis=0)
    table_low = position_table(seq_len, model_width).astype(jnp.bfloat16)
    if direct(model_width // lax.axis_size("dp")):
        packed = packed_rows(small)
    else:
        packed = small.T
    (after_first,), whole_attn, (attn_in_whole, pos_whole, attn_out_whole, packed) = between_step(
        functools.partial(forward_middle, 0.5, 1),
        ffn_forward(whole_first, ffn_first),
        [frames, norm_gains],
        1,
        fetch=[attn_in.reshape(attn_in.shape[0], -1), pos_proj, attn_out, packed],
        dims=(0, 0, 1, 0),
        ways=(False, True, True, True),
    )
    if direct(model_width // lax.axis_size("dp")):
        small = whole_rows(packed, small)
    else:
        small = packed.T
    taps = depthwise.shape[0]
    attn_held = (attn_in_whole, pos_whole, small[:2], attn_out_whole)
    conv_small = (
        small[2 : 2 + taps],
        small[2 + taps],
        small[3 + taps],
    )
    position = matmul(table_low, pos_whole).astype(jnp.bfloat16)
    attn_partial, *attn_saved = attention_forward(
        whole_attn, attn_held, position, own_length[None]
    )
    (after_attn,), whole_conv, (conv_in_whole, conv_out_whole, down_two) = between_step(
        functools.partial(forward_middle, 1.0, 2),
        attn_partial,
        [after_first, norm_gains],
        2,
        fetch=[conv_in.reshape(conv_in.shape[0], -1), conv_out, ffn2_down],
        dims=(0, 1, 1),
        ways=(False, False, True),
    )
    conv_held = (conv_in_whole, *conv_small, conv_out_whole)
    gate_value, logistic, padded, conved = conv_front(
        whole_conv, conv_held[0], conv_held[1], mask_col
    )
    stats = batch_stats(conved, mask_col, frame_count)
    normed_b, active = conv_tail(conved, stats, conv_held[2], conv_held[3])
    (after_conv,), whole_second, (up_two,) = between_step(
        functools.partial(forward_middle, 1.0, 3),
        matmul(active, conv_held[4]),
        [after_attn, norm_gains],
        3,
        fetch=[ffn2_up],
        dims=(0,),
        ways=(True,),
    )
    ffn_second = (up_two, down_two)
    (block_out, d_second, gain_five), whole_grads, _ = between_step(
        turn_middle,
        ffn_forward(whole_second, ffn_second),
        [after_conv, norm_gains, out_grad.reshape(local_rows, model_width)],
        4,
    )
    d_normed, grad_up, grad_down = ffn_backward(whole_second, ffn_second, whole_grads)
    (d_conv, gain_four), whole_grads, (total_up_two, total_down_two) = between_step(
        functools.partial(backward_middle, 1.0, 3),
        d_normed,
        [after_conv, norm_gains, d_second],
        5,
        grads=[grad_up, grad_down],
        dims=(0, 1),
        ways=(False, True),
    )
    d_normed, grad_conv_in, grad_kernel, grad_conv_out, gain_total, bias_total = conv_backward(
        whole_conv, conv_held, mask_col, stats, frame_count, whole_grads
    )
    (d_attn, gain_three), whole_grads, (total_conv_in, total_conv_out) = between_step(
        functools.partial(backward_middle, 1.0, 2),
        d_normed,
        [after_attn, norm_gains, d_conv],
        6,
        grads=[grad_conv_in, grad_conv_out],
        dims=(0, 1),
        ways=(False, True),
    )
    d_normed, grad_attn_in, grad_pos, grad_bias, grad_attn_out = attention_backward(
        whole_attn, attn_held, table_low, position, attn_saved, whole_grads
    )
    (d_first, gain_two), whole_grads, (total_attn_in, total_attn_out, total_pos) = between_step(
        functools.partial(backward_middle, 0.5, 1),
        d_normed,
        [after_first, norm_gains, d_attn],
        7,
        grads=[grad_attn_in, grad_attn_out, grad_pos],
        dims=(0, 1, 0),
        ways=(False, True, True),
    )
    d_normed, grad_up, grad_down = ffn_backward(whole_first, ffn_first, whole_grads)
    (in_grad,), small_grads, gains, (total_up_one, total_down_one) = close_step(
        close_middle,
        d_normed,
        jnp.concatenate([grad_bias, grad_kernel], axis=0),
        jnp.concatenate([gain_two, gain_three, gain_four, gain_five], axis=0),
        [frames, norm_gains, d_first],
        [grad_up, grad_down],
        (0, 1),
        (False, True),
        8,
    )
    gain_sum = jnp.concatenate([gains[4:], gains[:4]], axis=0)
    if direct(model_width // lax.axis_size("dp")):
        (
            block_out,
            in_grad,
            total_up_one,
            total_down_one,
            total_pos,
            total_attn_out,
            total_conv_out,
            total_up_two,
            total_down_two,
        ) = store_all(
            [
                block_out,
                in_grad,
                total_up_one,
                total_down_one,
                total_pos,
                total_attn_out,
                total_conv_out,
                total_up_two,
                total_down_two,
            ]
        )
    block = model_width // lax.axis_size("dp")
    piece_len = bn_scale.shape[0]
    own = dp_index * piece_len
    small_grads = lax.dynamic_slice_in_dim(small_grads, own, piece_len, axis=1)
    return (
        block_out.reshape(1, local_rows, model_width),
        in_grad.reshape(1, local_rows, model_width),
        gain_sum,
        total_up_one,
        total_down_one,
        total_attn_in.reshape(block, 3, -1),
        total_pos,
        small_grads[:2],
        total_attn_out,
        total_conv_in.reshape(block, 2, -1),
        small_grads[2:],
        lax.dynamic_slice_in_dim(gain_total, own, piece_len),
        lax.dynamic_slice_in_dim(bias_total, own, piece_len),
        total_conv_out,
        total_up_two,
        total_down_two,
    )


def solution(mesh):
    placed = (
        P("dp", "mp", None),
        P(),
        P("dp", "mp", None),
        P(),
        P("dp", "mp"),
        P("mp", "dp"),
        P("dp", None, "mp"),
        P("dp", "mp"),
        P(None, ("mp", "dp")),
        P("mp", "dp"),
        P("dp", None, "mp"),
        P(None, ("mp", "dp")),
        P(("mp", "dp")),
        P(("mp", "dp")),
        P("mp", "dp"),
        P("dp", "mp"),
        P("mp", "dp"),
    )
    return jax.shard_map(
        body,
        mesh=mesh,
        in_specs=placed,
        out_specs=(
            P("dp", "mp", None),
            P("dp", "mp", None),
            P(),
            P("dp", "mp"),
            P("mp", "dp"),
            P("dp", None, "mp"),
            P("dp", "mp"),
            P(None, ("mp", "dp")),
            P("mp", "dp"),
            P("dp", None, "mp"),
            P(None, ("mp", "dp")),
            P(("mp", "dp")),
            P(("mp", "dp")),
            P("mp", "dp"),
            P("dp", "mp"),
            P("mp", "dp"),
        ),
        check_vma=False,
    )
```
